128 devices in a mesh: band: 4 (over z_lo, core), pos: 32 (over z_hi, y, x).
Axes of the slice: x: 4, y: 4, z: 4 (z_hi: 2, z_lo: 2; z = z_hi * 2 + z_lo), core: 2. Of those that a mesh axis runs over, the one named last changes fastest.
Arguments:
- input_map: bfloat16 [1, 32, 4, 64, 4096], P(None, 'pos', 'band'), may hold values from -6 to 6
- cotangent: bfloat16 [1, 32, 4, 64, 4096], P(None, 'pos', 'band'), may hold values from -6 to 6
- band_width: int32 [32], P('pos'), may hold values from 2 to 3
- dilation: int32 [2], replicated, may hold values from 1 to 16, as said below
- conv_weight: bfloat16 [2, 64, 576], replicated, may hold values from -0.25 to 0.25
- conv_bias: float32 [2, 64], replicated, may hold values from -3 to 3
Outputs:
- output_map: bfloat16 [1, 32, 4, 64, 4096], P(None, 'pos', 'band')
- input_grad: float32 [1, 32, 4, 64, 4096], P(None, 'pos', 'band')
- weight_grad: float32 [2, 64, 576], replicated
- bias_grad: float32 [2, 64], replicated
The draws below stay inside these ranges and needn't reach their ends.
Inputs may be any that keep to these rules, and one draw needn't show every extreme that they name: Some layer has dilation exactly 16.
All inputs are finite; a program needn't handle non-finite values.
Results may differ from the reference program's by a relative error of at most 0.0075.
Values may be sent and summed in bfloat16 or wider, within the bound.
A program may use at most 128 MiB of HBM per device.

```python
import math
import jax
import jax.numpy as jnp
import numpy as np
from jax import lax

CHANNELS = 64
BLOCK = 64
DMAX = 16
OFFSETS = 4
LAYERS = 2
BATCH = 1
NB = 32


def draw_dilation(key, part):
    choose_key = jax.random.fold_in(key, 11)
    value_key = jax.random.fold_in(key, 12)
    picked = jax.random.randint(choose_key, (), 0, LAYERS)
    values = jax.random.randint(value_key, (LAYERS,), 1, DMAX + 1)
    return jnp.where(jnp.arange(LAYERS) == picked, DMAX, values).astype(jnp.int32)


def touch_ends(entries, own_key, smallest, largest):
    extent = entries.shape
    index_at = [jax.random.randint(jax.random.fold_in(own_key, axis), (), 0, extent[axis]) for axis in range(len(extent))]
    entries = entries.at[tuple(index_at)].set(smallest)
    longest = extent.index(max(extent))
    index_at[longest] = (index_at[longest] + 1) % extent[longest]
    return entries.at[tuple(index_at)].set(largest)


def block_scale(rng, dims, split, least, largest):
    level = 1.0
    for axis_at, blocks in split:
        draws = jax.random.uniform(jax.random.fold_in(jax.random.fold_in(rng, 6), axis_at), (blocks,), jnp.float32, least / len(split), largest / len(split))
        level = level * jnp.repeat(jnp.exp(draws), dims[axis_at] // blocks).reshape((-1,) + (1,) * (len(dims) - 1 - axis_at))
    return level


def normal_values(stream_key, extent, scale, reach, split=(), kind=jnp.bfloat16):
    result = scale * jax.random.normal(stream_key, extent, jnp.float32)
    if split:
        result = result * block_scale(stream_key, extent, split, -0.22, 0.18)
    return jnp.clip(result, -reach, reach).astype(kind)


def setup_inputs(seed: int = 0) -> dict:
    splits = jax.random.split(jax.random.key(seed), 7)
    input_map = normal_values(splits[0], (BATCH, NB, OFFSETS, CHANNELS, BLOCK * BLOCK), 1.0, 6.0, ((1, 32), (2, 4)))
    cotangent = normal_values(splits[1], (BATCH, NB, OFFSETS, CHANNELS, BLOCK * BLOCK), 1.0, 6.0, ((1, 32), (2, 4)))
    band_width = touch_ends(jax.random.randint(splits[2], (NB,), 2, OFFSETS), jax.random.fold_in(splits[2], 1), 2, OFFSETS - 1).astype(jnp.int32)
    dilation = draw_dilation(jax.random.fold_in(splits[6], 71), 0)
    conv_weight = normal_values(splits[4], (LAYERS, CHANNELS, 9 * CHANNELS), (9 * CHANNELS) ** -0.5, 0.25)
    conv_bias = normal_values(splits[5], (LAYERS, CHANNELS), 0.5, 3.0, (), jnp.float32)
    return {"input_map": input_map, "cotangent": cotangent, "band_width": band_width, "dilation": dilation, "conv_weight": conv_weight, "conv_bias": conv_bias}


tap_order = np.array([0, 3, 6, 1, 4, 7, 2, 5, 8])

def own_parts(stored):
    leading = stored.shape[:-2]
    flat_shape = leading + (DMAX * DMAX,)
    top_rows = stored[..., :DMAX, :]
    bottom_rows = stored[..., -DMAX:, :]
    left_cols = jnp.swapaxes(stored[..., :DMAX], -1, -2)
    right_cols = jnp.swapaxes(stored[..., -DMAX:], -1, -2)
    low_corner = stored[..., -DMAX:, :DMAX].reshape(flat_shape)
    high_corner = stored[..., :DMAX, -DMAX:].reshape(flat_shape)
    lower_right = stored[..., -DMAX:, -DMAX:].reshape(flat_shape)
    upper_left = stored[..., :DMAX, :DMAX].reshape(flat_shape)
    return (top_rows, bottom_rows, left_cols, right_cols, low_corner, high_corner, lower_right, upper_left)

def assemble(stored, pieces, block_offset):
    from_above, from_right, from_left, from_below, corner_above, far_above, far_below, corner_below = pieces
    square = corner_above.shape[:-1] + (DMAX, DMAX)
    far_up = far_above.reshape(square)
    own_low = jnp.swapaxes(stored[..., -DMAX:, :DMAX], -1, -2)
    down_left = jnp.where(block_offset == 0, jnp.swapaxes(far_up, -1, -2), jnp.where(block_offset == 1, own_low, far_below.reshape(square)))
    lower_rim = jnp.where(block_offset == 0, from_right, from_below)
    left_rim = jnp.where(block_offset == 0, from_above, from_left)
    upper = jnp.concatenate([corner_above.reshape(square), from_above, far_up], axis=-1)
    middle = jnp.concatenate([jnp.swapaxes(left_rim, -1, -2), stored, jnp.swapaxes(from_right, -1, -2)], axis=-1)
    lower = jnp.concatenate([down_left, lower_rim, corner_below.reshape(square)], axis=-1)
    return jnp.concatenate([upper, middle, lower], axis=-2)

def patches(framed, spread):
    channels = framed.shape[0]
    edge_bins = framed.shape[1] - 2 * DMAX
    anchor = spread * 0
    windows = []
    for row_tap in range(3):
        for col_tap in range(3):
            start_row = DMAX + (row_tap - 1) * spread
            start_col = DMAX + (col_tap - 1) * spread
            windows.append(lax.dynamic_slice(framed, (anchor, start_row, start_col), (channels, edge_bins, edge_bins)))
    return jnp.stack(windows, 0).reshape(9 * channels, edge_bins * edge_bins)

def paired(weight):
    channels = weight.shape[0]
    turned = weight.reshape(channels, 9, channels)[:, tap_order, :].reshape(channels, 9 * channels)
    return jnp.concatenate([weight, turned], axis=0)

def fold_pair(pair_grad):
    channels = pair_grad.shape[0] // 2
    turned = pair_grad[channels:].reshape(channels, 9, channels)[:, tap_order, :].reshape(channels, 9 * channels)
    return pair_grad[:channels] + turned

def forward_block(framed, stored, weight_pair, bias_pair, kept_block, spread):
    channels, edge_bins = (stored.shape[0], stored.shape[1])
    columns = patches(framed, spread)
    mixed_sum = jnp.dot(weight_pair, columns, preferred_element_type=jnp.float32) + bias_pair[:, None]
    active = 0.5 * (jax.nn.gelu(mixed_sum[:channels]) + jax.nn.gelu(mixed_sum[channels:]))
    return (kept_block * (stored.astype(jnp.float32) + active.reshape(channels, edge_bins, edge_bins))).astype(jnp.bfloat16)

def backward_block(framed, gradient, weight_pair, bias_pair, kept_block, spread):
    channels, edge_bins = (gradient.shape[0], gradient.shape[1])
    columns = patches(framed, spread)
    mixed_sum = jnp.dot(weight_pair, columns, preferred_element_type=jnp.float32) + bias_pair[:, None]
    masked = kept_block * gradient
    half_grad = 0.5 * masked.reshape(channels, edge_bins * edge_bins)
    slope_grad = jax.vjp(jax.nn.gelu, mixed_sum)[1](jnp.concatenate([half_grad, half_grad], axis=0))[0]
    slope_low = slope_grad.astype(jnp.bfloat16)
    pair_grad = lax.dot_general(slope_low, columns, (((1,), (1,)), ((), ())), preferred_element_type=jnp.float32)
    bias_term = lax.optimization_barrier(jnp.sum(slope_grad, axis=1))
    column_grad = lax.dot_general(weight_pair, slope_low, (((0,), (0,)), ((), ())), preferred_element_type=jnp.float32)
    pullback = jax.vjp(lambda whole: patches(whole, spread), framed.astype(jnp.float32))[1]
    tile_grad = pullback(column_grad)[0]
    return (masked, tile_grad, pair_grad, bias_term)

def displace(values_in, along, shift_by):
    total = values_in.shape[along]
    zero_fill = jnp.zeros_like(values_in)
    padded = jnp.concatenate([zero_fill, values_in, zero_fill], axis=along)
    return lax.slice_in_dim(padded, total - shift_by, 2 * total - shift_by, axis=along)

def neighbour_pieces(stored):
    top_rows, bottom_rows, left_cols, right_cols, low_corner, high_corner, lower_right, upper_left = own_parts(stored)
    from_above = displace(displace(bottom_rows, 2, -1), 1, 1)
    from_right = displace(left_cols, 2, -1)
    from_left = displace(right_cols, 2, 1)
    from_below = displace(displace(top_rows, 2, 1), 1, -1)
    corner_above = displace(lower_right, 1, 1)
    far_above = displace(displace(low_corner, 2, -2), 1, 1)
    far_below = displace(displace(high_corner, 2, 2), 1, -1)
    corner_below = displace(upper_left, 1, -1)
    return (from_above, from_right, from_left, from_below, corner_above, far_above, far_below, corner_below)

def reference(input_map, cotangent, band_width, dilation, conv_weight, conv_bias):
    flat_layout = input_map.shape
    full_shape = flat_layout[:4] + (BLOCK, BLOCK)
    input_map = input_map.reshape(full_shape)
    cotangent = cotangent.reshape(full_shape)
    samples, rows_all, offsets_all, channels, edge_bins = input_map.shape[:5]
    offset_ids = jnp.arange(offsets_all, dtype=jnp.int32)
    row_ids = jnp.arange(rows_all, dtype=jnp.int32)
    inside = (offset_ids[None, :] <= band_width[:, None]) & (row_ids[:, None] + offset_ids[None, :] < rows_all)
    kept = jnp.where(inside, 1.0, 0.0).astype(jnp.float32)
    kept_wide = kept[None, :, :, None, None, None]
    offset_grid = offset_ids[None, None, :, None, None, None]
    total_blocks = samples * rows_all * offsets_all
    flat_kept = jnp.broadcast_to(kept[None], (samples, rows_all, offsets_all)).reshape(total_blocks)
    inner = input_map.shape[3:]
    current = (input_map.astype(jnp.float32) * kept_wide).astype(jnp.bfloat16)
    stored_layers = []
    for layer_index in range(LAYERS):
        weight_pair = paired(conv_weight[layer_index])
        bias_pair = jnp.concatenate([conv_bias[layer_index], conv_bias[layer_index]])
        spread = dilation[layer_index]
        framed = assemble(current, neighbour_pieces(current), offset_grid)
        stored_layers.append(current)
        flat_framed = framed.reshape((total_blocks,) + framed.shape[3:])
        flat_stored = current.reshape((total_blocks,) + inner)
        current = lax.map(lambda element: forward_block(element[0], element[1], weight_pair, bias_pair, element[2], spread), (flat_framed, flat_stored, flat_kept)).reshape(input_map.shape)
    output_map = current
    gradient = cotangent.astype(jnp.float32)
    weight_terms = [None] * LAYERS
    bias_terms = [None] * LAYERS
    for layer_index in reversed(range(LAYERS)):
        weight_pair = paired(conv_weight[layer_index])
        bias_pair = jnp.concatenate([conv_bias[layer_index], conv_bias[layer_index]])
        spread = dilation[layer_index]
        stored = stored_layers[layer_index]
        framed = assemble(stored, neighbour_pieces(stored), offset_grid)
        flat_framed = framed.reshape((total_blocks,) + framed.shape[3:])
        flat_grad = gradient.reshape((total_blocks,) + inner)
        masked, tile_grad, pair_grad, bias_term = lax.map(lambda element: backward_block(element[0], element[1], weight_pair, bias_pair, element[2], spread), (flat_framed, flat_grad, flat_kept))
        weight_terms[layer_index] = fold_pair(lax.optimization_barrier(jnp.sum(pair_grad, axis=0)))
        bias_both = lax.optimization_barrier(jnp.sum(bias_term, axis=0))
        bias_terms[layer_index] = bias_both[:channels] + bias_both[channels:]
        tile_grad = tile_grad.reshape(framed.shape)
        wide_stored = stored.astype(jnp.float32)
        wide_pieces = tuple((piece.astype(jnp.float32) for piece in neighbour_pieces(stored)))
        pullback = jax.vjp(lambda whole, pieces: assemble(whole, pieces, offset_grid), wide_stored, wide_pieces)[1]
        block_grad, piece_grads = pullback(tile_grad)
        rounded = lax.optimization_barrier(tuple((piece.astype(jnp.bfloat16) for piece in piece_grads)))
        rounded = tuple((piece.astype(jnp.float32) for piece in rounded))
        spread_back = jax.vjp(neighbour_pieces, wide_stored)[1]
        neighbour_grad = spread_back(rounded)[0]
        gradient = masked.reshape(input_map.shape) + block_grad + neighbour_grad
    input_grad = gradient * kept_wide
    scale = 1.0 / (BLOCK * math.sqrt(BATCH * NB * OFFSETS))
    weight_grad = jnp.stack(weight_terms) * scale
    bias_grad = jnp.stack(bias_terms) * scale
    return (output_map.reshape(flat_layout), input_grad.reshape(flat_layout), weight_grad, bias_grad)
```

```python
import functools
import math

import jax
import jax.numpy as jnp
from jax import lax
from jax.experimental import pallas as pl
from jax.experimental.pallas import tpu as pltpu
from jax.sharding import PartitionSpec as P

BLOCK = 64
DMAX = 16
LAYERS = 2
CH = 64
LANES = 128
HALF = 32
WIDE = BLOCK + 2 * DMAX
F32 = jnp.float32
BF16 = jnp.bfloat16
MESH = pl.DeviceIdType.MESH

STEPS = ((1, -1), (0, -1), (0, 1), (-1, 1), (1, 0), (1, -2), (-1, 2), (-1, 0))
ABOVE, RIGHT, LEFT, BELOW, CORNER_ABOVE, FAR_ABOVE, FAR_BELOW, CORNER_BELOW = range(8)
EDGE_LOW = slice(0, DMAX)
CENTRE = slice(DMAX, DMAX + BLOCK)
EDGE_HIGH = slice(DMAX + BLOCK, WIDE)
SQRT_2_PI = math.sqrt(2.0 / math.pi)
CUBIC = 0.044715


def is_low(shape):
    return lax.broadcasted_iota(jnp.int32, shape, len(shape) - 1) < CH


def swap(value):
    return pltpu.roll(value, CH, value.ndim - 1)


def pick(low_value, high_value):
    return jnp.where(is_low(low_value.shape), low_value, high_value)


def merge(first, second):
    return jnp.concatenate([pick(first, swap(second)), pick(swap(first), second)], axis=0)


def both_gelu(value):
    square = value * value
    inner = SQRT_2_PI * (value + CUBIC * (square * value))
    bend = jnp.tanh(inner)
    cdf = 0.5 * (1.0 + bend)
    slope = cdf + 0.5 * value * (1.0 - bend * bend) * (SQRT_2_PI * (1.0 + 3.0 * CUBIC * square))
    return value * cdf, slope


def net_kernel(
    rows_all,
    offsets_all,
    width_ref,
    dilation_ref,
    input_ref,
    cot_ref,
    weight_ref,
    bias_ref,
    out_ref,
    grad_ref,
    term_ref,
    frame,
    cols,
    slopes,
    slope_low,
    padded,
    grad,
    pair_grad,
    w_fwd,
    w_bwd,
    turn,
    send_a,
    send_b,
    send_l,
    send_r,
    recv_a,
    recv_b,
    recv_l,
    recv_r,
    recv_c,
    send_sem,
    recv_sem,
):
    row = lax.axis_index("pos")
    off = lax.axis_index("band")

    def exists(di, do):
        return (row + di >= 0) & (row + di < rows_all) & (off + do >= 0) & (off + do < offsets_all)

    kept = jnp.where(
        (off <= width_ref[0]) & (row + off < rows_all), jnp.float32(1.0), jnp.float32(0.0)
    )

    views = {
        ABOVE: (send_a, recv_a, CENTRE, CENTRE),
        CORNER_ABOVE: (send_a, recv_c, slice(64, 80), EDGE_LOW),
        FAR_ABOVE: (send_a, recv_c, slice(16, 32), EDGE_HIGH),
        BELOW: (send_b, recv_b, CENTRE, CENTRE),
        FAR_BELOW: (send_b, recv_c, slice(64, 80), EDGE_LOW),
        CORNER_BELOW: (send_b, recv_c, slice(16, 32), EDGE_HIGH),
        LEFT: (send_l, recv_l, slice(0, 16), slice(0, 16)),
        RIGHT: (send_r, recv_r, slice(0, 16), slice(0, 16)),
    }

    for piece in range(8):
        di, do = STEPS[piece]
        target = views[piece][1]
        for sign, indices in ((1, (0, 1)), (-1, (2, 3))):

            @pl.when(jnp.logical_not(exists(-sign * di, -sign * do)))
            def _():
                for index in indices:
                    there = target.at[(index, piece - 4) if piece >= 4 else (index,)]
                    there[...] = jnp.zeros(there.shape, BF16)

    barrier = pltpu.get_barrier_semaphore()
    count = jnp.int32(0)
    for di, do in STEPS:
        count = count + exists(di, do).astype(jnp.int32)

        @pl.when(exists(di, do))
        def _():
            pl.semaphore_signal(
                barrier,
                inc=1,
                device_id={"pos": row + di, "band": off + do},
                device_id_type=MESH,
            )

    def piece_copy(index, piece):
        di, do = STEPS[piece]
        source, target, fwd_part, bwd_part = views[piece]
        there = (index, piece - 4) if piece >= 4 else (index,)
        forward = index < LAYERS
        part = fwd_part if forward else bwd_part
        sign = 1 if forward else -1
        return pltpu.make_async_remote_copy(
            src_ref=source.at[index, :, part, :],
            dst_ref=target.at[there],
            send_sem=send_sem.at[index, piece],
            recv_sem=recv_sem.at[index, piece],
            device_id={"pos": row + sign * di, "band": off + sign * do},
            device_id_type=MESH,
        )

    def send(index, pieces):
        sign = 1 if index < LAYERS else -1
        for piece in pieces:
            di, do = STEPS[piece]

            @pl.when(exists(sign * di, sign * do))
            def _():
                piece_copy(index, piece).start()

    def wait(index, pieces):
        sign = 1 if index < LAYERS else -1
        for piece in pieces:
            di, do = STEPS[piece]

            @pl.when(exists(-sign * di, -sign * do))
            def _():
                piece_copy(index, piece).wait_recv()

    def finish(index):
        sign = 1 if index < LAYERS else -1
        for piece in range(8):
            di, do = STEPS[piece]

            @pl.when(exists(sign * di, sign * do))
            def _():
                piece_copy(index, piece).wait_send()

    def to_tiles(source, k):
        first = source[:, pl.ds(pl.multiple_of(k * LANES, LANES), LANES)].astype(F32)
        second = source[:, pl.ds(pl.multiple_of((k + 16) * LANES, LANES), LANES)].astype(F32)
        return jnp.concatenate([first, second], axis=0).T

    def from_tiles(target, k, first, second):
        turned = jnp.concatenate([first, second], axis=0).T.astype(target.dtype)
        target[:, pl.ds(pl.multiple_of(k * LANES, LANES), LANES)] = turned[:CH]
        target[:, pl.ds(pl.multiple_of((k + 16) * LANES, LANES), LANES)] = turned[CH:]

    def rows_to_cols(load, store):
        @pl.loop(0, 8)
        def _(k):
            turn[pl.ds(pl.multiple_of(k * 64, 64), 64), :] = load(k)

        for t in range(HALF):
            store(t, merge(turn[pl.ds(t, 8, stride=64), :], turn[pl.ds(HALF + t, 8, stride=64), :]))

    def cols_to_rows(load, store):
        @pl.loop(0, HALF)
        def _(t):
            turn[pl.ds(pl.multiple_of(t * 16, 16), 16), :] = load(t)

        for k in range(8):
            store(
                k,
                merge(turn[pl.ds(k, HALF, stride=16), :], turn[pl.ds(8 + k, HALF, stride=16), :]),
            )

    def turn_corner(load, store):
        for k in range(8):
            turn[pl.ds(k * 16, 16), :] = load(k)
        for k in range(8):
            store(k, merge(turn[pl.ds(k, 8, stride=16), :], turn[pl.ds(8 + k, 8, stride=16), :]))

    def pack_forward(index):
        @pl.loop(0, 8)
        def _(k):
            send_a[index, k, CENTRE, :] = pick(
                swap(frame[32 + k, CENTRE, :]), frame[40 + k, CENTRE, :]
            ).astype(BF16)
            send_b[index, k, CENTRE, :] = pick(
                frame[16 + k, CENTRE, :], swap(frame[24 + k, CENTRE, :])
            ).astype(BF16)

        @pl.loop(0, HALF)
        def _(t):
            send_l[index, t] = frame[16 + t, slice(64, 80), :].astype(BF16)
            send_r[index, t] = frame[16 + t, slice(16, 32), :].astype(BF16)

    def unpack_forward(index):
        def put_down_left(k, value):
            recv_c[index, FAR_BELOW - 4, k] = value.astype(BF16)

        @pl.when(off == 0)
        def _():
            def put_left(t, value):
                recv_l[index, t] = value.astype(BF16)

            def put_below(k, value):
                recv_b[index, k] = value.astype(BF16)

            rows_to_cols(lambda k: recv_a[index, k].astype(F32), put_left)
            cols_to_rows(lambda t: recv_r[index, t].astype(F32), put_below)
            turn_corner(
                lambda k: recv_c[index, FAR_ABOVE - 4, k].astype(F32), put_down_left
            )

        @pl.when(off == 1)
        def _():
            turn_corner(
                lambda k: send_a[index, k, slice(16, 32), :].astype(F32), put_down_left
            )

        @pl.loop(0, HALF)
        def _(t):
            frame[16 + t, EDGE_LOW, :] = recv_l[index, t].astype(F32)
            frame[16 + t, EDGE_HIGH, :] = recv_r[index, t].astype(F32)

        @pl.loop(0, 8)
        def _(k):
            above, below = (
                jnp.concatenate(
                    [recv_c[index, low - 4, k], strip[index, k], recv_c[index, high - 4, k]], axis=0
                ).astype(F32)
                for low, strip, high in (
                    (CORNER_ABOVE, recv_a, FAR_ABOVE),
                    (FAR_BELOW, recv_b, CORNER_BELOW),
                )
            )
            frame[k] = pick(above, swap(frame[32 + k]))
            frame[8 + k] = swap(pick(frame[40 + k], above))
            frame[48 + k] = swap(pick(below, frame[16 + k]))
            frame[56 + k] = pick(swap(frame[24 + k]), below)

    def prepare_weights(layer):
        weight = weight_ref[layer].astype(F32)
        pieces = [weight[:, j * LANES : (j + 1) * LANES] for j in range(4)]
        pieces.append(
            jnp.concatenate([weight[:, 512:576], jnp.zeros((CH, CH), F32)], axis=1)
        )
        turned = [jnp.concatenate([piece, piece], axis=0).T for piece in pieces]
        for a in range(3):
            for b in range(3):
                for pair, tap in enumerate((3 * a + b, 3 * b + a)):
                    plain = turned[tap // 2][(tap % 2) * CH : (tap % 2) * CH + CH]
                    low = is_low(plain.shape)
                    at = (3 * a + b) * LANES
                    lane = pair * LANES
                    w_fwd[layer, at : at + CH, lane : lane + LANES] = jnp.where(
                        low, plain, 0.0
                    ).astype(BF16)
                    w_fwd[layer, at + CH : at + LANES, lane : lane + LANES] = jnp.where(
                        low, 0.0, plain
                    ).astype(BF16)
                    own = pieces[tap // 2]
                    other = swap(own)
                    if tap % 2:
                        own, other = other, own
                    at = a * 2 * LANES + pair * LANES
                    lane = b * LANES
                    w_bwd[layer, at : at + CH, lane : lane + LANES] = jnp.where(
                        low, own, 0.0
                    ).astype(BF16)
                    w_bwd[layer, at + CH : at + LANES, lane : lane + LANES] = jnp.where(
                        low, 0.0, other
                    ).astype(BF16)

    def shift_columns(layer):
        spread = dilation_ref[layer]

        @pl.loop(0, 64)
        def _(t):
            for b in range(3):
                cols[layer, t, :, b * LANES : (b + 1) * LANES] = frame[
                    t, pl.ds(DMAX + (b - 1) * spread, BLOCK), :
                ].astype(BF16)

    def taps(layer, t, tiles):
        spread = dilation_ref[layer]
        return [
            cols[layer, pl.ds(DMAX + t + (a - 1) * spread, tiles)].reshape(tiles * BLOCK, 3 * LANES)
            for a in range(3)
        ]

    FWD = 4

    def forward(layer):
        bias = bias_ref[layer : layer + 1, :]
        bias = jnp.concatenate([bias, bias, bias, bias], axis=1)

        @pl.loop(0, HALF // FWD)
        def _(step):
            t = step * FWD
            mixed = (
                jnp.dot(
                    jnp.concatenate(taps(layer, t, FWD), axis=1),
                    w_fwd[layer],
                    preferred_element_type=F32,
                )
                + bias
            )
            value, slope = both_gelu(mixed)
            slopes[layer, pl.ds(t, FWD)] = slope.reshape(FWD, BLOCK, 2 * LANES)
            active = 0.5 * (value[:, :LANES] + value[:, LANES:])
            stored = frame[pl.ds(16 + t, FWD), CENTRE, :].reshape(FWD * BLOCK, LANES)
            result = (kept * (stored + active)).astype(BF16).astype(F32)
            frame[pl.ds(16 + t, FWD), CENTRE, :] = result.reshape(FWD, BLOCK, LANES)

    @pl.loop(0, 16)
    def _(k):
        tiles = (to_tiles(input_ref, k) * kept).astype(BF16).astype(F32)
        frame[16 + 2 * k, CENTRE, :] = tiles[:BLOCK]
        frame[17 + 2 * k, CENTRE, :] = tiles[BLOCK:]

    pack_forward(0)
    pl.semaphore_wait(barrier, count)
    send(0, range(8))
    for layer in range(LAYERS):
        prepare_weights(layer)

    @pl.loop(0, 16)
    def _(k):
        tiles = to_tiles(cot_ref, k)
        grad[2 * k] = tiles[:BLOCK]
        grad[2 * k + 1] = tiles[BLOCK:]

    for layer in range(LAYERS):
        wait(layer, range(8))
        unpack_forward(layer)
        shift_columns(layer)
        forward(layer)
        if layer < LAYERS - 1:
            pack_forward(layer + 1)
            send(layer + 1, range(8))

    @pl.loop(0, 16)
    def _(k):
        from_tiles(out_ref, k, frame[16 + 2 * k, CENTRE, :], frame[17 + 2 * k, CENTRE, :])

    @pl.loop(0, 16)
    def _(t):
        slope_low[t] = jnp.zeros((BLOCK, 2 * LANES), BF16)
        slope_low[48 + t] = jnp.zeros((BLOCK, 2 * LANES), BF16)

    @pl.loop(0, 8)
    def _(t):
        for b in range(3):
            padded[b, t, 0:32, :] = jnp.zeros((32, LANES), F32)
            padded[b, t, 96:128, :] = jnp.zeros((32, LANES), F32)

    def slope_step(layer):
        def step(t, total):
            masked = kept * grad[t]
            grad[t] = masked
            half = 0.5 * masked
            slope = slopes[layer, t] * jnp.concatenate([half, half], axis=1)
            slope_low[16 + t] = slope.astype(BF16)
            return total + jnp.sum(slope.reshape(8, 8, 2 * LANES), axis=0)

        return lax.fori_loop(0, HALF, step, jnp.zeros((8, 2 * LANES), F32))

    BWD = 8

    def tile_grad(layer):
        spread = dilation_ref[layer]

        def part(step, which):
            first = step * BWD
            held = [
                slope_low[pl.ds(first - (a - 1) * spread, BWD)].reshape(BWD * BLOCK, 2 * LANES)
                for a in which
            ]
            left = held[0] if len(held) == 1 else jnp.concatenate(held, axis=1)
            rows = w_bwd[layer, which[0] * 2 * LANES : (which[-1] + 1) * 2 * LANES, :]
            result = jnp.dot(left, rows, preferred_element_type=F32)
            for b in range(3):
                padded[b, :, 32:96, :] = result[:, b * LANES : (b + 1) * LANES].reshape(
                    BWD, BLOCK, LANES
                )
            for at in range(BWD):
                total = None
                for b in range(3):
                    term = padded[b, at, pl.ds(DMAX - (b - 1) * spread, WIDE), :]
                    total = term if total is None else total + term
                frame[first + at] = total

        @pl.loop(0, 2)
        def _(step):
            part(step, (0,))

        @pl.loop(2, 6)
        def _(step):
            part(step, (0, 1, 2))

        @pl.loop(6, 8)
        def _(step):
            part(step, (2,))

    def pack_backward(index):
        @pl.loop(0, 8)
        def _(k):
            above = pick(frame[k], swap(frame[8 + k]))
            below = pick(swap(frame[48 + k]), frame[56 + k])
            low = is_low(above.shape)
            frame[16 + k] = frame[16 + k] + jnp.where(low, 0.0, swap(frame[48 + k]))
            frame[24 + k] = frame[24 + k] + jnp.where(low, 0.0, swap(frame[56 + k]))
            frame[32 + k] = frame[32 + k] + jnp.where(low, swap(frame[k]), 0.0)
            frame[40 + k] = frame[40 + k] + jnp.where(low, swap(frame[8 + k]), 0.0)
            frame[k] = above
            frame[48 + k] = below

        @pl.when(off == 0)
        def _():
            def add_above(k, value):
                frame[k, CENTRE, :] = frame[k, CENTRE, :] + value

            def add_right(t, value):
                frame[16 + t, EDGE_HIGH, :] = frame[16 + t, EDGE_HIGH, :] + value

            def add_far(k, value):
                frame[k, EDGE_HIGH, :] = frame[k, EDGE_HIGH, :] + value

            cols_to_rows(lambda t: frame[16 + t, EDGE_LOW, :], add_above)
            rows_to_cols(lambda k: frame[48 + k, CENTRE, :], add_right)
            turn_corner(lambda k: frame[48 + k, EDGE_LOW, :], add_far)

        @pl.when(off == 1)
        def _():
            def add_own(k, value):
                low = is_low(value.shape)
                at = slice(16, 32)
                frame[32 + k, at, :] = frame[32 + k, at, :] + jnp.where(low, 0.0, swap(value))
                frame[40 + k, at, :] = frame[40 + k, at, :] + jnp.where(low, 0.0, value)

            turn_corner(lambda k: frame[48 + k, EDGE_LOW, :], add_own)

        @pl.loop(0, 8)
        def _(k):
            send_a[index, k] = frame[k].astype(BF16)
            send_b[index, k] = frame[48 + k].astype(BF16)

        @pl.loop(0, HALF)
        def _(t):
            send_l[index, t] = frame[16 + t, EDGE_LOW, :].astype(BF16)
            send_r[index, t] = frame[16 + t, EDGE_HIGH, :].astype(BF16)

    def unpack_backward(index):
        @pl.loop(0, HALF)
        def _(t):
            total = grad[t] + frame[16 + t, CENTRE, :]
            right = recv_r[index, t].astype(F32)
            left = recv_l[index, t].astype(F32)
            edge = jnp.concatenate([right, jnp.zeros((32, LANES), F32), left], axis=0)
            grad[t] = total + edge

        @pl.loop(0, 8)
        def _(k):
            def strip(ref, low, high):
                corners = [
                    recv_c[index, high - 4, k].astype(F32),
                    jnp.zeros((32, LANES), F32),
                    recv_c[index, low - 4, k].astype(F32),
                ]
                return ref[index, k].astype(F32) + jnp.concatenate(corners, axis=0)

            top = strip(recv_b, FAR_BELOW, CORNER_BELOW)
            bottom = strip(recv_a, CORNER_ABOVE, FAR_ABOVE)
            low = is_low(top.shape)
            grad[k] = grad[k] + jnp.where(low, top, 0.0)
            grad[8 + k] = grad[8 + k] + jnp.where(low, swap(top), 0.0)
            grad[16 + k] = grad[16 + k] + jnp.where(low, 0.0, swap(bottom))
            grad[24 + k] = grad[24 + k] + jnp.where(low, 0.0, bottom)

    PG = 8

    def weight_terms(layer, bias_rows):
        pair_grad[...] = jnp.zeros_like(pair_grad)

        @pl.loop(0, HALF // PG)
        def _(step):
            t = step * PG
            left = slope_low[pl.ds(16 + t, PG)].reshape(PG * BLOCK, 2 * LANES)
            for a, part in enumerate(taps(layer, t, PG)):
                lane = a * 3 * LANES
                pair_grad[:, lane : lane + 3 * LANES] += lax.dot_general(
                    left, part, (((0,), (0,)), ((), ())), preferred_element_type=F32
                )

        def tap_part(tap, half):
            turned = 3 * (tap % 3) + tap // 3
            first = pair_grad[half * CH : half * CH + CH, tap * LANES : (tap + 1) * LANES]
            at = LANES + half * CH
            second = pair_grad[at : at + CH, turned * LANES : (turned + 1) * LANES]
            return first + second

        for j in range(5):
            low_part = tap_part(2 * j, 0) + swap(tap_part(2 * j, 1))
            if j < 4:
                high_part = tap_part(2 * j + 1, 1) + swap(tap_part(2 * j + 1, 0))
            else:
                total = jnp.sum(bias_rows, axis=0, keepdims=True)
                total = total[:, :LANES] + total[:, LANES:]
                total = total + swap(total)
                high_part = jnp.broadcast_to(total, (LANES, LANES)).T[:CH]
            term_ref[layer * CH : (layer + 1) * CH, j * LANES : (j + 1) * LANES] = pick(
                low_part, high_part
            )

    for layer in reversed(range(LAYERS)):
        index = 2 * LAYERS - 1 - layer
        bias_rows = slope_step(layer)
        tile_grad(layer)
        pack_backward(index)
        send(index, range(8))
        weight_terms(layer, bias_rows)
        wait(index, range(8))
        unpack_backward(index)

    @pl.loop(0, 16)
    def _(k):
        from_tiles(grad_ref, k, kept * grad[2 * k], kept * grad[2 * k + 1])

    for index in range(2 * LAYERS):
        finish(index)


def sum_kernel(
    group, outer, offsets_all, scale, term_ref, weight_ref, bias_ref, slots, shards, whole, send_sem, recv_sem
):
    pos = lax.axis_index("pos")
    band = lax.axis_index("band")
    inner = lax.rem(pos, group)
    high = lax.div(pos, group)
    rows = term_ref.shape[0] // group
    many = outer * offsets_all
    mine = high * offsets_all + band

    def in_plane(step):
        other = lax.rem(inner + step, group)
        return other, {"pos": high * group + other, "band": band}

    def across(step):
        other = lax.rem(mine + step, many)
        return other, {
            "pos": lax.div(other, offsets_all) * group + inner,
            "band": lax.rem(other, offsets_all),
        }

    barrier = pltpu.get_barrier_semaphore()
    for step in range(1, group):
        pl.semaphore_signal(barrier, inc=1, device_id=in_plane(step)[1], device_id_type=MESH)
    for step in range(1, many):
        pl.semaphore_signal(barrier, inc=1, device_id=across(step)[1], device_id_type=MESH)
    pl.semaphore_wait(barrier, group + many - 2)

    def span(at):
        return pl.ds(pl.multiple_of(at * rows, rows), rows)

    copies = []
    for step in range(1, group):
        other, device = in_plane(step)
        copies.append(
            pltpu.make_async_remote_copy(
                src_ref=term_ref.at[span(other)],
                dst_ref=slots.at[step],
                send_sem=send_sem.at[0, step],
                recv_sem=recv_sem.at[0, step],
                device_id=device,
                device_id_type=MESH,
            )
        )
        copies[-1].start()
    total = term_ref[span(inner)]
    for step in range(1, group):
        copies[step - 1].wait_recv()
        total = total + slots[step]
    shards[mine] = total
    seconds = []
    for step in range(1, many):
        other, device = across(step)
        seconds.append(
            pltpu.make_async_remote_copy(
                src_ref=shards.at[mine],
                dst_ref=shards.at[mine],
                send_sem=send_sem.at[1, step],
                recv_sem=recv_sem.at[1, step],
                device_id=device,
                device_id_type=MESH,
            )
        )
        seconds[-1].start()
    for copy in seconds:
        copy.wait_recv()
    total = shards[0]
    for at in range(1, many):
        total = total + shards[at]
    whole[inner] = total * scale
    thirds = []
    for step in range(1, group):
        other, device = in_plane(step)
        thirds.append(
            pltpu.make_async_remote_copy(
                src_ref=whole.at[inner],
                dst_ref=whole.at[inner],
                send_sem=send_sem.at[2, step],
                recv_sem=recv_sem.at[2, step],
                device_id=device,
                device_id_type=MESH,
            )
        )
        thirds[-1].start()
    for copy in thirds:
        copy.wait_recv()
    result = whole[...].reshape(group * rows, 5 * LANES)
    for layer in range(LAYERS):
        weight_ref[layer] = result[layer * CH : (layer + 1) * CH, :576]
    column = result[:, 4 * LANES :].T[CH : CH + 1]
    bias_ref[0:1, :] = column[:, :CH]
    bias_ref[1:2, :] = swap(column)[:, :CH]
    for copy in copies + seconds + thirds:
        copy.wait_send()


def per_device(input_map, cotangent, band_width, dilation, conv_weight, conv_bias):
    rows_all = lax.axis_size("pos")
    offsets_all = lax.axis_size("band")
    bins = BLOCK * BLOCK
    vmem = pl.BlockSpec(memory_space=pltpu.VMEM)
    smem = pl.BlockSpec(memory_space=pltpu.SMEM)
    output, input_grad, terms = pl.pallas_call(
        functools.partial(net_kernel, rows_all, offsets_all),
        out_shape=(
            jax.ShapeDtypeStruct((CH, bins), BF16),
            jax.ShapeDtypeStruct((CH, bins), F32),
            jax.ShapeDtypeStruct((LAYERS * CH, 5 * LANES), F32),
        ),
        in_specs=[smem, smem, vmem, vmem, vmem, vmem],
        out_specs=(vmem, vmem, vmem),
        scratch_shapes=[
            pltpu.VMEM((64, WIDE, LANES), F32),
            pltpu.VMEM((LAYERS, 64, BLOCK, 3 * LANES), BF16),
            pltpu.VMEM((LAYERS, HALF, BLOCK, 2 * LANES), F32),
            pltpu.VMEM((64, BLOCK, 2 * LANES), BF16),
            pltpu.VMEM((3, 8, 128, LANES), F32),
            pltpu.VMEM((HALF, BLOCK, LANES), F32),
            pltpu.VMEM((2 * LANES, 9 * LANES), F32),
            pltpu.VMEM((LAYERS, 9 * LANES, 2 * LANES), BF16),
            pltpu.VMEM((LAYERS, 6 * LANES, 3 * LANES), BF16),
            pltpu.VMEM((512, LANES), F32),
            pltpu.VMEM((4, 8, WIDE, LANES), BF16),
            pltpu.VMEM((4, 8, WIDE, LANES), BF16),
            pltpu.VMEM((4, HALF, DMAX, LANES), BF16),
            pltpu.VMEM((4, HALF, DMAX, LANES), BF16),
            pltpu.VMEM((4, 8, BLOCK, LANES), BF16),
            pltpu.VMEM((4, 8, BLOCK, LANES), BF16),
            pltpu.VMEM((4, HALF, DMAX, LANES), BF16),
            pltpu.VMEM((4, HALF, DMAX, LANES), BF16),
            pltpu.VMEM((4, 4, 8, DMAX, LANES), BF16),
            pltpu.SemaphoreType.DMA((4, 8)),
            pltpu.SemaphoreType.DMA((4, 8)),
        ],
        compiler_params=pltpu.CompilerParams(collective_id=0, has_side_effects=True),
        name="net",
    )(
        band_width,
        dilation,
        input_map.reshape(CH, bins),
        cotangent.reshape(CH, bins),
        conv_weight,
        conv_bias,
    )
    group = 16 if rows_all % 16 == 0 else rows_all
    outer = rows_all // group
    rows = LAYERS * CH // group
    scale = 1.0 / (BLOCK * math.sqrt(input_map.shape[0] * rows_all * offsets_all))
    weight_grad, bias_grad = pl.pallas_call(
        functools.partial(sum_kernel, group, outer, offsets_all, scale),
        out_shape=(
            jax.ShapeDtypeStruct((LAYERS, CH, 576), F32),
            jax.ShapeDtypeStruct((LAYERS, CH), F32),
        ),
        in_specs=[vmem],
        out_specs=(vmem, vmem),
        scratch_shapes=[
            pltpu.VMEM((group, rows, 5 * LANES), F32),
            pltpu.VMEM((outer * offsets_all, rows, 5 * LANES), F32),
            pltpu.VMEM((group, rows, 5 * LANES), F32),
            pltpu.SemaphoreType.DMA((3, 16)),
            pltpu.SemaphoreType.DMA((3, 16)),
        ],
        compiler_params=pltpu.CompilerParams(collective_id=1, has_side_effects=True),
        name="sum",
    )(terms)
    return (
        output.reshape(input_map.shape),
        input_grad.reshape(input_map.shape),
        weight_grad,
        bias_grad,
    )


def solution(mesh):
    split = P(None, "pos", "band", None, None)
    return jax.shard_map(
        per_device,
        mesh=mesh,
        in_specs=(split, split, P("pos"), P(), P(), P()),
        out_specs=(split, split, P(), P()),
        check_vma=False,
    )
```

```python
import functools
import math

import jax
import jax.numpy as jnp
from jax import lax
from jax.experimental import pallas as pl
from jax.experimental.pallas import tpu as pltpu
from jax.sharding import PartitionSpec as P

BLOCK = 64
DMAX = 16
LAYERS = 2
BWD = 8
SLOTS = 2
CH = 64
LANES = 128
HALF = 32
WIDE = BLOCK + 2 * DMAX
F32 = jnp.float32
BF16 = jnp.bfloat16
MESH = pl.DeviceIdType.MESH

STEPS = ((1, -1), (0, -1), (0, 1), (-1, 1), (1, 0), (1, -2), (-1, 2), (-1, 0))
ABOVE, RIGHT, LEFT, BELOW, CORNER_ABOVE, FAR_ABOVE, FAR_BELOW, CORNER_BELOW = range(8)
EDGE_LOW = slice(0, DMAX)
CENTRE = slice(DMAX, DMAX + BLOCK)
EDGE_HIGH = slice(DMAX + BLOCK, WIDE)
SQRT_2_PI = math.sqrt(2.0 / math.pi)
CUBIC = 0.044715


def is_low(shape):
    return lax.broadcasted_iota(jnp.int32, shape, len(shape) - 1) < CH


def swap(value):
    return pltpu.roll(value, CH, value.ndim - 1)


def pick(low_value, high_value):
    return jnp.where(is_low(low_value.shape), low_value, high_value)


def merge(first, second):
    return jnp.concatenate([pick(first, swap(second)), pick(swap(first), second)], axis=0)


def both_gelu(value):
    square = value * value
    inner = SQRT_2_PI * (value + CUBIC * (square * value))
    bend = jnp.tanh(inner)
    cdf = 0.5 * (1.0 + bend)
    slope = cdf + 0.5 * value * (1.0 - bend * bend) * (SQRT_2_PI * (1.0 + 3.0 * CUBIC * square))
    return value * cdf, slope


def net_kernel(
    rows_all,
    offsets_all,
    scale,
    width_ref,
    dilation_ref,
    input_ref,
    cot_ref,
    weight_ref,
    bias_ref,
    out_ref,
    grad_ref,
    sums_ref,
    frame,
    term_ref,
    slots,
    shards,
    whole,
    cols,
    slopes,
    slope_low,
    padded,
    grad,
    above,
    below,
    pair_grad,
    w_fwd,
    w_bwd,
    turn,
    send_a,
    send_b,
    send_l,
    send_r,
    send_c,
    recv_a,
    recv_b,
    recv_l,
    recv_r,
    recv_c,
    send_sem,
    recv_sem,
    sum_send,
    sum_recv,
):
    row = lax.axis_index("pos")
    off = lax.axis_index("band")

    def exists(di, do):
        return (row + di >= 0) & (row + di < rows_all) & (off + do >= 0) & (off + do < offsets_all)

    group = whole.shape[0]
    many = shards.shape[0]
    rows = term_ref.shape[1]
    inner = lax.rem(row, group)
    high = lax.div(row, group)
    mine = high * offsets_all + off

    def in_plane(step):
        other = lax.rem(inner + step, group)
        return other, {"pos": high * group + other, "band": off}

    def across(step):
        other = lax.rem(mine + step, many)
        return other, {
            "pos": lax.div(other, offsets_all) * group + inner,
            "band": lax.rem(other, offsets_all),
        }

    kept = jnp.where(
        (off <= width_ref[0]) & (row + off < rows_all), jnp.float32(1.0), jnp.float32(0.0)
    )

    first, final = slice(0, DMAX), slice(BLOCK - DMAX, BLOCK)
    strips = {
        ABOVE: (send_a, recv_a),
        RIGHT: (send_r, recv_r),
        LEFT: (send_l, recv_l),
        BELOW: (send_b, recv_b),
    }
    corners = {
        CORNER_ABOVE: (send_a, final),
        FAR_ABOVE: (send_a, first),
        FAR_BELOW: (send_b, final),
        CORNER_BELOW: (send_b, first),
    }

    def arrival(index, piece):
        if piece in corners:
            return recv_c.at[index, piece - 4]
        return strips[piece][1].at[index]

    def departure(index, piece):
        if piece in strips:
            return strips[piece][0].at[index]
        if index < LAYERS:
            source, part = corners[piece]
            return source.at[index, :, part, :]
        return send_c.at[index - LAYERS, piece - 4]

    for piece in range(8):
        di, do = STEPS[piece]
        for sign, indices in ((1, (0, 1)), (-1, (2, 3))):

            @pl.when(jnp.logical_not(exists(-sign * di, -sign * do)))
            def _():
                for index in indices:
                    there = arrival(index, piece)
                    there[...] = jnp.zeros(there.shape, BF16)

    barrier = pltpu.get_barrier_semaphore()
    count = jnp.int32(0)
    for di, do in STEPS:
        count = count + exists(di, do).astype(jnp.int32)

        @pl.when(exists(di, do))
        def _():
            pl.semaphore_signal(
                barrier,
                inc=1,
                device_id={"pos": row + di, "band": off + do},
                device_id_type=MESH,
            )

    for step in range(1, group):
        pl.semaphore_signal(barrier, inc=1, device_id=in_plane(step)[1], device_id_type=MESH)
    for step in range(1, many):
        pl.semaphore_signal(barrier, inc=1, device_id=across(step)[1], device_id_type=MESH)
    count = count + (group + many - 2)

    def piece_copy(index, piece):
        di, do = STEPS[piece]
        sign = 1 if index < LAYERS else -1
        return pltpu.make_async_remote_copy(
            src_ref=departure(index, piece),
            dst_ref=arrival(index, piece),
            send_sem=send_sem.at[index, piece],
            recv_sem=recv_sem.at[index, piece],
            device_id={"pos": row + sign * di, "band": off + sign * do},
            device_id_type=MESH,
        )

    def send(index, pieces):
        sign = 1 if index < LAYERS else -1
        for piece in pieces:
            di, do = STEPS[piece]

            @pl.when(exists(sign * di, sign * do))
            def _():
                piece_copy(index, piece).start()

    def wait(index, pieces):
        sign = 1 if index < LAYERS else -1
        for piece in pieces:
            di, do = STEPS[piece]

            @pl.when(exists(-sign * di, -sign * do))
            def _():
                piece_copy(index, piece).wait_recv()

    def finish(index):
        sign = 1 if index < LAYERS else -1
        for piece in range(8):
            di, do = STEPS[piece]

            @pl.when(exists(sign * di, sign * do))
            def _():
                piece_copy(index, piece).wait_send()

    def to_tiles(source, k):
        first = source[:, pl.ds(pl.multiple_of(k * LANES, LANES), LANES)].astype(F32)
        second = source[:, pl.ds(pl.multiple_of((k + 16) * LANES, LANES), LANES)].astype(F32)
        return jnp.concatenate([first, second], axis=0).T

    def rows_to_cols(load, store):
        @pl.loop(0, 8, unroll=8)
        def _(k):
            turn[pl.ds(pl.multiple_of(k * 64, 64), 64), :] = load(k)

        for t in range(HALF):
            store(t, merge(turn[pl.ds(t, 8, stride=64), :], turn[pl.ds(HALF + t, 8, stride=64), :]))

    def cols_to_rows(load, store):
        @pl.loop(0, HALF, unroll=8)
        def _(t):
            turn[pl.ds(pl.multiple_of(t * 16, 16), 16), :] = load(t)

        for k in range(8):
            store(
                k,
                merge(turn[pl.ds(k, HALF, stride=16), :], turn[pl.ds(8 + k, HALF, stride=16), :]),
            )

    def turn_corner(load, store):
        for k in range(8):
            turn[pl.ds(k * 16, 16), :] = load(k)
        for k in range(8):
            store(k, merge(turn[pl.ds(k, 8, stride=16), :], turn[pl.ds(8 + k, 8, stride=16), :]))

    def pack_forward(index):
        @pl.loop(0, 8, unroll=8)
        def _(k):
            send_a[index, k] = pick(
                swap(frame[32 + k, CENTRE, :]), frame[40 + k, CENTRE, :]
            ).astype(BF16)
            send_b[index, k] = pick(
                frame[16 + k, CENTRE, :], swap(frame[24 + k, CENTRE, :])
            ).astype(BF16)

        @pl.loop(0, HALF, unroll=8)
        def _(t):
            send_l[index, t] = frame[16 + t, slice(64, 80), :].astype(BF16)
            send_r[index, t] = frame[16 + t, slice(16, 32), :].astype(BF16)

    def unpack_forward(index):
        def put_down_left(k, value):
            recv_c[index, FAR_BELOW - 4, k] = value.astype(BF16)

        @pl.when(off == 0)
        def _():
            def put_left(t, value):
                recv_l[index, t] = value.astype(BF16)

            def put_below(k, value):
                recv_b[index, k] = value.astype(BF16)

            rows_to_cols(lambda k: recv_a[index, k].astype(F32), put_left)
            cols_to_rows(lambda t: recv_r[index, t].astype(F32), put_below)
            turn_corner(
                lambda k: recv_c[index, FAR_ABOVE - 4, k].astype(F32), put_down_left
            )

        @pl.when(off == 1)
        def _():
            turn_corner(
                lambda k: send_a[index, k, first, :].astype(F32), put_down_left
            )

        @pl.loop(0, HALF, unroll=8)
        def _(t):
            frame[16 + t, EDGE_LOW, :] = recv_l[index, t].astype(F32)
            frame[16 + t, EDGE_HIGH, :] = recv_r[index, t].astype(F32)

        @pl.loop(0, 8, unroll=8)
        def _(k):
            above, below = (
                jnp.concatenate(
                    [recv_c[index, low - 4, k], strip[index, k], recv_c[index, high - 4, k]], axis=0
                ).astype(F32)
                for low, strip, high in (
                    (CORNER_ABOVE, recv_a, FAR_ABOVE),
                    (FAR_BELOW, recv_b, CORNER_BELOW),
                )
            )
            frame[k] = pick(above, swap(frame[32 + k]))
            frame[8 + k] = swap(pick(frame[40 + k], above))
            frame[48 + k] = swap(pick(below, frame[16 + k]))
            frame[56 + k] = pick(swap(frame[24 + k]), below)

    def prepare_weights(layer):
        weight = weight_ref[layer].astype(F32)
        pieces = [weight[:, j * LANES : (j + 1) * LANES] for j in range(4)]
        pieces.append(
            jnp.concatenate([weight[:, 512:576], jnp.zeros((CH, CH), F32)], axis=1)
        )
        turned = [jnp.concatenate([piece, piece], axis=0).T for piece in pieces]
        for a in range(3):
            for b in range(3):
                for pair, tap in enumerate((3 * a + b, 3 * b + a)):
                    plain = turned[tap // 2][(tap % 2) * CH : (tap % 2) * CH + CH]
                    low = is_low(plain.shape)
                    at = (3 * a + b) * LANES
                    lane = pair * LANES
                    w_fwd[layer, at : at + CH, lane : lane + LANES] = jnp.where(
                        low, plain, 0.0
                    ).astype(BF16)
                    w_fwd[layer, at + CH : at + LANES, lane : lane + LANES] = jnp.where(
                        low, 0.0, plain
                    ).astype(BF16)
                    own = pieces[tap // 2]
                    other = swap(own)
                    if tap % 2:
                        own, other = other, own
                    at = a * 2 * LANES + pair * LANES
                    lane = b * LANES
                    w_bwd[layer, at : at + CH, lane : lane + LANES] = jnp.where(
                        low, own, 0.0
                    ).astype(BF16)
                    w_bwd[layer, at + CH : at + LANES, lane : lane + LANES] = jnp.where(
                        low, 0.0, other
                    ).astype(BF16)

    def shift_columns(layer):
        spread = dilation_ref[layer]

        @pl.loop(0, 64, unroll=4)
        def _(t):
            for b in range(3):
                cols[layer, t, :, b * LANES : (b + 1) * LANES] = frame[
                    t, pl.ds(DMAX + (b - 1) * spread, BLOCK), :
                ].astype(BF16)

    def taps(layer, t, tiles):
        spread = dilation_ref[layer]
        return [
            cols[layer, pl.ds(DMAX + t + (a - 1) * spread, tiles)].reshape(tiles * BLOCK, 3 * LANES)
            for a in range(3)
        ]

    FWD = 8

    def forward(layer):
        bias = bias_ref[layer : layer + 1, :]
        bias = jnp.concatenate([bias, bias, bias, bias], axis=1)

        @pl.loop(0, HALF // FWD, unroll=4)
        def _(step):
            t = step * FWD
            mixed = (
                jnp.dot(
                    jnp.concatenate(taps(layer, t, FWD), axis=1),
                    w_fwd[layer],
                    preferred_element_type=F32,
                )
                + bias
            )
            value, slope = both_gelu(mixed)
            slopes[layer, pl.ds(t, FWD)] = slope.reshape(FWD, BLOCK, 2 * LANES)
            active = 0.5 * (value[:, :LANES] + value[:, LANES:])
            stored = frame[pl.ds(16 + t, FWD), CENTRE, :].reshape(FWD * BLOCK, LANES)
            result = (kept * (stored + active)).astype(BF16).astype(F32)
            result = result.reshape(FWD, BLOCK, LANES)
            if layer == LAYERS - 1:
                out_ref[pl.ds(t, FWD)] = result.astype(BF16)
            else:
                frame[pl.ds(16 + t, FWD), CENTRE, :] = result

    @pl.loop(0, 16, unroll=4)
    def _(k):
        tiles = (to_tiles(input_ref, k) * kept).astype(BF16).astype(F32)
        frame[16 + 2 * k, CENTRE, :] = tiles[:BLOCK]
        frame[17 + 2 * k, CENTRE, :] = tiles[BLOCK:]

    pack_forward(0)
    pl.semaphore_wait(barrier, count)
    send(0, range(8))
    for layer in range(LAYERS):
        prepare_weights(layer)

    @pl.loop(0, 16, unroll=4)
    def _(k):
        tiles = to_tiles(cot_ref, k)
        grad[2 * k] = tiles[:BLOCK]
        grad[2 * k + 1] = tiles[BLOCK:]

    for layer in range(LAYERS):
        wait(layer, range(8))
        unpack_forward(layer)
        shift_columns(layer)
        forward(layer)
        if layer < LAYERS - 1:
            pack_forward(layer + 1)
            send(layer + 1, range(8))

    @pl.loop(0, 16, unroll=4)
    def _(t):
        slope_low[t] = jnp.zeros((BLOCK, 2 * LANES), BF16)
        slope_low[48 + t] = jnp.zeros((BLOCK, 2 * LANES), BF16)

    @pl.loop(0, BWD, unroll=4)
    def _(t):
        for b in range(3):
            for slot in range(SLOTS):
                padded[slot, b, t, 0:32, :] = jnp.zeros((32, LANES), F32)
                padded[slot, b, t, 96:128, :] = jnp.zeros((32, LANES), F32)

    def slope_step(layer):
        def step(t, total):
            masked = kept * grad[t]
            grad[t] = masked
            half = 0.5 * masked
            slope = slopes[layer, t] * jnp.concatenate([half, half], axis=1)
            slope_low[16 + t] = slope.astype(BF16)
            return total + jnp.sum(slope.reshape(8, 8, 2 * LANES), axis=0)

        return lax.fori_loop(0, HALF, step, jnp.zeros((8, 2 * LANES), F32), unroll=4)

    def tile_grad(layer, steps):
        spread = dilation_ref[layer]

        def part(step, which, slot):
            first = step * BWD
            held = [
                slope_low[pl.ds(first - (a - 1) * spread, BWD)].reshape(BWD * BLOCK, 2 * LANES)
                for a in which
            ]
            left = held[0] if len(held) == 1 else jnp.concatenate(held, axis=1)
            rows = w_bwd[layer, which[0] * 2 * LANES : (which[-1] + 1) * 2 * LANES, :]
            result = jnp.dot(left, rows, preferred_element_type=F32)
            for b in range(3):
                padded[slot, b, :, 32:96, :] = result[:, b * LANES : (b + 1) * LANES].reshape(
                    BWD, BLOCK, LANES
                )
            for at in range(BWD):
                total = None
                for b in range(3):
                    term = padded[slot, b, at, pl.ds(DMAX - (b - 1) * spread, WIDE), :]
                    total = term if total is None else total + term
                frame[first + at] = total

        for count, step in enumerate(steps):
            at = step * BWD
            which = (0,) if at < 16 else (2,) if at >= 48 else (0, 1, 2)
            part(step, which, count % SLOTS)

    def pack_outer(index):
        @pl.loop(0, 8, unroll=8)
        def _(k):
            above[k] = pick(frame[k], swap(frame[8 + k]))
            below[k] = pick(swap(frame[48 + k]), frame[56 + k])

        @pl.when(off == 0)
        def _():
            def add_far(k, value):
                above[k, EDGE_HIGH, :] = above[k, EDGE_HIGH, :] + value

            turn_corner(lambda k: below[k, EDGE_LOW, :], add_far)

        @pl.loop(0, 8, unroll=8)
        def _(k):
            send_b[index, k] = below[k, CENTRE, :].astype(BF16)
            for piece, strip, part in (
                (CORNER_ABOVE, above, EDGE_LOW),
                (FAR_ABOVE, above, EDGE_HIGH),
                (FAR_BELOW, below, EDGE_LOW),
                (CORNER_BELOW, below, EDGE_HIGH),
            ):
                send_c[index - LAYERS, piece - 4, k] = strip[k, part, :].astype(BF16)

        @pl.when(off > 0)
        def _():
            send_above(index)

        send(index, (BELOW, CORNER_ABOVE, FAR_ABOVE, FAR_BELOW, CORNER_BELOW))

    def send_above(index):
        @pl.loop(0, 8, unroll=8)
        def _(k):
            send_a[index, k] = above[k, CENTRE, :].astype(BF16)

        send(index, (ABOVE,))

    def pack_centre(index):
        @pl.when(off == 0)
        def _():
            @pl.loop(0, 8, unroll=8)
            def _(k):
                share(k, EDGE_LOW)

            def add_above(k, value):
                above[k, CENTRE, :] = above[k, CENTRE, :] + value

            cols_to_rows(lambda t: frame[16 + t, EDGE_LOW, :], add_above)
            send_above(index)

            @pl.loop(0, 8, unroll=8)
            def _(k):
                share(k, slice(DMAX, WIDE))

            def add_right(t, value):
                frame[16 + t, EDGE_HIGH, :] = frame[16 + t, EDGE_HIGH, :] + value

            rows_to_cols(lambda k: below[k, CENTRE, :], add_right)

        @pl.when(off > 0)
        def _():
            @pl.loop(0, 8, unroll=8)
            def _(k):
                share(k, slice(0, WIDE))

        @pl.when(off == 1)
        def _():
            def add_own(k, value):
                low = is_low(value.shape)
                at = slice(16, 32)
                frame[32 + k, at, :] = frame[32 + k, at, :] + jnp.where(low, 0.0, swap(value))
                frame[40 + k, at, :] = frame[40 + k, at, :] + jnp.where(low, 0.0, value)

            turn_corner(lambda k: below[k, EDGE_LOW, :], add_own)

        @pl.loop(0, HALF, unroll=8)
        def _(t):
            send_l[index, t] = frame[16 + t, EDGE_LOW, :].astype(BF16)
            send_r[index, t] = frame[16 + t, EDGE_HIGH, :].astype(BF16)

        send(index, (LEFT, RIGHT))

    def share(k, part):
        def add(to, value, keep_low):
            low = is_low(value.shape)
            moved = swap(value)
            moved = jnp.where(low, moved, 0.0) if keep_low else jnp.where(low, 0.0, moved)
            frame[to, part, :] = frame[to, part, :] + moved

        add(16 + k, frame[48 + k, part, :], False)
        add(24 + k, frame[56 + k, part, :], False)
        add(32 + k, frame[k, part, :], True)
        add(40 + k, frame[8 + k, part, :], True)

    def unpack_backward(index):
        @pl.loop(0, HALF, unroll=8)
        def _(t):
            total = grad[t] + frame[16 + t, CENTRE, :]
            right = recv_r[index, t].astype(F32)
            left = recv_l[index, t].astype(F32)
            edge = jnp.concatenate([right, jnp.zeros((32, LANES), F32), left], axis=0)
            grad[t] = total + edge

        @pl.loop(0, 8, unroll=8)
        def _(k):
            def strip(ref, low, high):
                corners = [
                    recv_c[index, high - 4, k].astype(F32),
                    jnp.zeros((32, LANES), F32),
                    recv_c[index, low - 4, k].astype(F32),
                ]
                return ref[index, k].astype(F32) + jnp.concatenate(corners, axis=0)

            top = strip(recv_b, FAR_BELOW, CORNER_BELOW)
            bottom = strip(recv_a, CORNER_ABOVE, FAR_ABOVE)
            low = is_low(top.shape)
            grad[k] = grad[k] + jnp.where(low, top, 0.0)
            grad[8 + k] = grad[8 + k] + jnp.where(low, swap(top), 0.0)
            grad[16 + k] = grad[16 + k] + jnp.where(low, 0.0, swap(bottom))
            grad[24 + k] = grad[24 + k] + jnp.where(low, 0.0, bottom)

    PG = 16

    def weight_terms(layer, bias_rows):
        pair_grad[...] = jnp.zeros_like(pair_grad)

        @pl.loop(0, HALF // PG)
        def _(step):
            t = step * PG
            left = slope_low[pl.ds(16 + t, PG)].reshape(PG * BLOCK, 2 * LANES)
            for a, part in enumerate(taps(layer, t, PG)):
                lane = a * 3 * LANES
                pair_grad[:, lane : lane + 3 * LANES] += lax.dot_general(
                    left, part, (((0,), (0,)), ((), ())), preferred_element_type=F32
                )

        def tap_part(tap, half):
            turned = 3 * (tap % 3) + tap // 3
            first = pair_grad[half * CH : half * CH + CH, tap * LANES : (tap + 1) * LANES]
            at = LANES + half * CH
            second = pair_grad[at : at + CH, turned * LANES : (turned + 1) * LANES]
            return first + second

        for j in range(5):
            low_part = tap_part(2 * j, 0) + swap(tap_part(2 * j, 1))
            if j < 4:
                high_part = tap_part(2 * j + 1, 1) + swap(tap_part(2 * j + 1, 0))
            else:
                total = jnp.sum(bias_rows, axis=0, keepdims=True)
                total = total[:, :LANES] + total[:, LANES:]
                total = total + swap(total)
                high_part = jnp.broadcast_to(total, (LANES, LANES)).T[:CH]
            part = pick(low_part, high_part).astype(BF16)
            for at in range(CH // rows):
                term_ref[layer * (CH // rows) + at, :, j * LANES : (j + 1) * LANES] = part[
                    at * rows : (at + 1) * rows
                ]

    def sum_copy(stage, step):
        if stage == 1:
            other, device = across(step)
            source, target = shards.at[mine], shards.at[mine]
        else:
            other, device = in_plane(step)
            if stage == 0:
                source, target = term_ref.at[other], slots.at[step]
            else:
                source, target = whole.at[inner], whole.at[inner]
        return pltpu.make_async_remote_copy(
            src_ref=source,
            dst_ref=target,
            send_sem=sum_send.at[stage, step],
            recv_sem=sum_recv.at[stage, step],
            device_id=device,
            device_id_type=MESH,
        )

    def peers(stage):
        return range(1, many if stage == 1 else group)

    def sum_start(stage):
        if stage == 1:
            total = term_ref[inner].astype(F32)
            for step in peers(0):
                sum_copy(0, step).wait_recv()
                total = total + slots[step].astype(F32)
            shards[mine] = total
        elif stage == 2:
            for step in peers(1):
                sum_copy(1, step).wait_recv()
            total = shards[0]
            for at in range(1, many):
                total = total + shards[at]
            whole[inner] = (total * scale).astype(BF16)
        for step in peers(stage):
            sum_copy(stage, step).start()

    def sum_end():
        for step in peers(2):
            sum_copy(2, step).wait_recv()
        sums_ref[...] = whole[...].astype(F32)
        for stage in range(3):
            for step in peers(stage):
                sum_copy(stage, step).wait_send()

    for layer in reversed(range(LAYERS)):
        index = 2 * LAYERS - 1 - layer
        bias_rows = slope_step(layer)
        if layer == 0:
            weight_terms(layer, bias_rows)
            sum_start(0)
        edge = 64 // BWD // 4
        tile_grad(layer, (*range(edge), *range(3 * edge, 4 * edge)))
        pack_outer(index)
        tile_grad(layer, range(edge, 3 * edge))
        pack_centre(index)
        if layer == 0:
            sum_start(1)
            sum_start(2)
        else:
            weight_terms(layer, bias_rows)
        wait(index, range(8))
        unpack_backward(index)

    @pl.loop(0, HALF, unroll=4)
    def _(t):
        grad_ref[t] = kept * grad[t]

    sum_end()
    for index in range(2 * LAYERS):
        finish(index)


def finish_kernel(
    tiles_ref, grad_ref, sums_ref, out_ref, grad_out_ref, weight_ref, bias_ref, tiles, grad, out, turned, sems
):
    parts = 4
    each = HALF // parts
    lanes = each * BLOCK
    half = HALF * BLOCK
    loads = []
    for part in range(parts):
        span = pl.ds(part * each, each)
        loads.append(
            (
                pltpu.make_async_copy(tiles_ref.at[span], tiles.at[span], sems.at[0, part]),
                pltpu.make_async_copy(grad_ref.at[span], grad.at[span], sems.at[1, part]),
            )
        )
        for copy in loads[-1]:
            copy.start()
    total = jnp.concatenate([sums_ref[at] for at in range(sums_ref.shape[0])], axis=0)
    for layer in range(LAYERS):
        weight_ref[layer] = total[layer * CH : (layer + 1) * CH, :576]
    column = total[:, 4 * LANES :].T[CH : CH + 1]
    bias_ref[0:1, :] = column[:, :CH]
    bias_ref[1:2, :] = swap(column)[:, :CH]
    stores = []
    for part in range(parts):
        for at, (source, held, target) in enumerate(((tiles, out, out_ref), (grad, turned, grad_out_ref))):
            loads[part][at].wait()
            for k in range(part * each // 2, (part + 1) * each // 2):
                both = source[2 * k : 2 * k + 2].reshape(LANES, LANES).astype(F32).T
                both = both.astype(held.dtype)
                held[:, k * LANES : (k + 1) * LANES] = both[:CH]
                held[:, half + k * LANES : half + (k + 1) * LANES] = both[CH:]
            for side in range(2):
                span = pl.ds(side * half + part * lanes, lanes)
                copy = pltpu.make_async_copy(
                    held.at[:, span], target.at[:, span], sems.at[2 + 2 * at + side, part]
                )
                copy.start()
                stores.append(copy)
    for copy in stores:
        copy.wait()


def per_device(input_map, cotangent, band_width, dilation, conv_weight, conv_bias):
    rows_all = lax.axis_size("pos")
    offsets_all = lax.axis_size("band")
    bins = BLOCK * BLOCK
    vmem = pl.BlockSpec(memory_space=pltpu.VMEM)
    smem = pl.BlockSpec(memory_space=pltpu.SMEM)
    group = 16 if rows_all % 16 == 0 else rows_all
    many = rows_all // group * offsets_all
    shard = (LAYERS * CH // group, 5 * LANES)
    scale = 1.0 / (BLOCK * math.sqrt(input_map.shape[0] * rows_all * offsets_all))
    tiles, grad, sums = pl.pallas_call(
        functools.partial(net_kernel, rows_all, offsets_all, scale),
        out_shape=(
            jax.ShapeDtypeStruct((HALF, BLOCK, LANES), BF16),
            jax.ShapeDtypeStruct((HALF, BLOCK, LANES), F32),
            jax.ShapeDtypeStruct((group, *shard), F32),
        ),
        in_specs=[smem, smem, vmem, vmem, vmem, vmem],
        out_specs=(vmem, vmem, vmem),
        scratch_shapes=[
            pltpu.VMEM((64, WIDE, LANES), F32),
            pltpu.VMEM((group, *shard), BF16),
            pltpu.VMEM((group, *shard), BF16),
            pltpu.VMEM((many, *shard), F32),
            pltpu.VMEM((group, *shard), BF16),
            pltpu.VMEM((LAYERS, 64, BLOCK, 3 * LANES), BF16),
            pltpu.VMEM((LAYERS, HALF, BLOCK, 2 * LANES), F32),
            pltpu.VMEM((64, BLOCK, 2 * LANES), BF16),
            pltpu.VMEM((SLOTS, 3, BWD, 128, LANES), F32),
            pltpu.VMEM((HALF, BLOCK, LANES), F32),
            pltpu.VMEM((8, WIDE, LANES), F32),
            pltpu.VMEM((8, WIDE, LANES), F32),
            pltpu.VMEM((2 * LANES, 9 * LANES), F32),
            pltpu.VMEM((LAYERS, 9 * LANES, 2 * LANES), BF16),
            pltpu.VMEM((LAYERS, 6 * LANES, 3 * LANES), BF16),
            pltpu.VMEM((512, LANES), F32),
            pltpu.VMEM((4, 8, BLOCK, LANES), BF16),
            pltpu.VMEM((4, 8, BLOCK, LANES), BF16),
            pltpu.VMEM((4, HALF, DMAX, LANES), BF16),
            pltpu.VMEM((4, HALF, DMAX, LANES), BF16),
            pltpu.VMEM((2, 4, 8, DMAX, LANES), BF16),
            pltpu.VMEM((4, 8, BLOCK, LANES), BF16),
            pltpu.VMEM((4, 8, BLOCK, LANES), BF16),
            pltpu.VMEM((4, HALF, DMAX, LANES), BF16),
            pltpu.VMEM((4, HALF, DMAX, LANES), BF16),
            pltpu.VMEM((4, 4, 8, DMAX, LANES), BF16),
            pltpu.SemaphoreType.DMA((4, 8)),
            pltpu.SemaphoreType.DMA((4, 8)),
            pltpu.SemaphoreType.DMA((3, 16)),
            pltpu.SemaphoreType.DMA((3, 16)),
        ],
        compiler_params=pltpu.CompilerParams(collective_id=0, has_side_effects=True),
        name="net",
    )(
        band_width,
        dilation,
        input_map.reshape(CH, bins),
        cotangent.reshape(CH, bins),
        conv_weight,
        conv_bias,
    )
    anywhere = pl.BlockSpec(memory_space=pl.ANY)
    output, input_grad, weight_grad, bias_grad = pl.pallas_call(
        finish_kernel,
        out_shape=(
            jax.ShapeDtypeStruct((CH, bins), BF16),
            jax.ShapeDtypeStruct((CH, bins), F32),
            jax.ShapeDtypeStruct((LAYERS, CH, 576), F32),
            jax.ShapeDtypeStruct((LAYERS, CH), F32),
        ),
        in_specs=[anywhere, anywhere, vmem],
        out_specs=(anywhere, anywhere, vmem, vmem),
        scratch_shapes=[
            pltpu.VMEM((HALF, BLOCK, LANES), BF16),
            pltpu.VMEM((HALF, BLOCK, LANES), F32),
            pltpu.VMEM((CH, bins), BF16),
            pltpu.VMEM((CH, bins), F32),
            pltpu.SemaphoreType.DMA((6, 4)),
        ],
        name="finish",
    )(tiles, grad, sums)
    return (
        output.reshape(input_map.shape),
        input_grad.reshape(input_map.shape),
        weight_grad,
        bias_grad,
    )


def solution(mesh):
    split = P(None, "pos", "band", None, None)
    return jax.shard_map(
        per_device,
        mesh=mesh,
        in_specs=(split, split, P("pos"), P(), P(), P()),
        out_specs=(split, split, P(), P()),
        check_vma=False,
    )
```

```python
import functools
import math

import jax
import jax.numpy as jnp
from jax import lax
from jax.experimental import pallas as pl
from jax.experimental.pallas import tpu as pltpu
from jax.sharding import PartitionSpec as P

BLOCK = 64
DMAX = 16
LAYERS = 2
BWD = 8
SLOTS = 2
CH = 64
LANES = 128
HALF = 32
WIDE = BLOCK + 2 * DMAX
F32 = jnp.float32
BF16 = jnp.bfloat16
MESH = pl.DeviceIdType.MESH

STEPS = ((1, -1), (0, -1), (0, 1), (-1, 1), (1, 0), (1, -2), (-1, 2), (-1, 0))
ABOVE, RIGHT, LEFT, BELOW, CORNER_ABOVE, FAR_ABOVE, FAR_BELOW, CORNER_BELOW = range(8)
EDGE_LOW = slice(0, DMAX)
CENTRE = slice(DMAX, DMAX + BLOCK)
EDGE_HIGH = slice(DMAX + BLOCK, WIDE)
SQRT_2_PI = math.sqrt(2.0 / math.pi)
CUBIC = 0.044715


def is_low(shape):
    return lax.broadcasted_iota(jnp.int32, shape, len(shape) - 1) < CH


def swap(value):
    return pltpu.roll(value, CH, value.ndim - 1)


def pick(low_value, high_value):
    return jnp.where(is_low(low_value.shape), low_value, high_value)


def merge(first, second):
    return jnp.concatenate([pick(first, swap(second)), pick(swap(first), second)], axis=0)


def both_gelu(value):
    square = value * value
    inner = SQRT_2_PI * (value + CUBIC * (square * value))
    bend = jnp.tanh(inner)
    cdf = 0.5 * (1.0 + bend)
    slope = cdf + 0.5 * value * (1.0 - bend * bend) * (SQRT_2_PI * (1.0 + 3.0 * CUBIC * square))
    return value * cdf, slope


def net_kernel(
    rows_all,
    offsets_all,
    scale,
    width_ref,
    dilation_ref,
    input_ref,
    cot_ref,
    weight_ref,
    bias_ref,
    out_ref,
    grad_ref,
    weight_grad_ref,
    bias_grad_ref,
    frame,
    last,
    term_ref,
    slots,
    shards,
    whole,
    cols,
    slopes,
    slope_low,
    padded,
    grad,
    above,
    below,
    pair_grad,
    w_fwd,
    w_bwd,
    turn,
    send_a,
    send_b,
    send_l,
    send_r,
    send_c,
    recv_a,
    recv_b,
    recv_l,
    recv_r,
    recv_c,
    send_sem,
    recv_sem,
    sum_send,
    sum_recv,
):
    row = lax.axis_index("pos")
    off = lax.axis_index("band")

    def exists(di, do):
        return (row + di >= 0) & (row + di < rows_all) & (off + do >= 0) & (off + do < offsets_all)

    group = whole.shape[0]
    many = shards.shape[0]
    rows = term_ref.shape[1]
    inner = lax.rem(row, group)
    high = lax.div(row, group)
    mine = high * offsets_all + off

    def in_plane(step):
        other = lax.rem(inner + step, group)
        return other, {"pos": high * group + other, "band": off}

    def across(step):
        other = lax.rem(mine + step, many)
        return other, {
            "pos": lax.div(other, offsets_all) * group + inner,
            "band": lax.rem(other, offsets_all),
        }

    kept = jnp.where(
        (off <= width_ref[0]) & (row + off < rows_all), jnp.float32(1.0), jnp.float32(0.0)
    )

    first, final = slice(0, DMAX), slice(BLOCK - DMAX, BLOCK)
    strips = {
        ABOVE: (send_a, recv_a),
        RIGHT: (send_r, recv_r),
        LEFT: (send_l, recv_l),
        BELOW: (send_b, recv_b),
    }
    corners = {
        CORNER_ABOVE: (send_a, final),
        FAR_ABOVE: (send_a, first),
        FAR_BELOW: (send_b, final),
        CORNER_BELOW: (send_b, first),
    }

    def arrival(index, piece):
        if piece in corners:
            return recv_c.at[index, piece - 4]
        return strips[piece][1].at[index]

    def departure(index, piece):
        if piece in strips:
            return strips[piece][0].at[index]
        if index < LAYERS:
            source, part = corners[piece]
            return source.at[index, :, part, :]
        return send_c.at[index - LAYERS, piece - 4]

    for piece in range(8):
        di, do = STEPS[piece]
        for sign, indices in ((1, (0, 1)), (-1, (2, 3))):

            @pl.when(jnp.logical_not(exists(-sign * di, -sign * do)))
            def _():
                for index in indices:
                    there = arrival(index, piece)
                    there[...] = jnp.zeros(there.shape, BF16)

    barrier = pltpu.get_barrier_semaphore()
    count = jnp.int32(0)
    for di, do in STEPS:
        count = count + exists(di, do).astype(jnp.int32)

        @pl.when(exists(di, do))
        def _():
            pl.semaphore_signal(
                barrier,
                inc=1,
                device_id={"pos": row + di, "band": off + do},
                device_id_type=MESH,
            )

    for step in range(1, group):
        pl.semaphore_signal(barrier, inc=1, device_id=in_plane(step)[1], device_id_type=MESH)
    for step in range(1, many):
        pl.semaphore_signal(barrier, inc=1, device_id=across(step)[1], device_id_type=MESH)
    count = count + (group + many - 2)

    def piece_copy(index, piece):
        di, do = STEPS[piece]
        sign = 1 if index < LAYERS else -1
        return pltpu.make_async_remote_copy(
            src_ref=departure(index, piece),
            dst_ref=arrival(index, piece),
            send_sem=send_sem.at[index, piece],
            recv_sem=recv_sem.at[index, piece],
            device_id={"pos": row + sign * di, "band": off + sign * do},
            device_id_type=MESH,
        )

    def send(index, pieces):
        sign = 1 if index < LAYERS else -1
        for piece in pieces:
            di, do = STEPS[piece]

            @pl.when(exists(sign * di, sign * do))
            def _():
                piece_copy(index, piece).start()

    def wait(index, pieces):
        sign = 1 if index < LAYERS else -1
        for piece in pieces:
            di, do = STEPS[piece]

            @pl.when(exists(-sign * di, -sign * do))
            def _():
                piece_copy(index, piece).wait_recv()

    def finish(index):
        sign = 1 if index < LAYERS else -1
        for piece in range(8):
            di, do = STEPS[piece]

            @pl.when(exists(sign * di, sign * do))
            def _():
                piece_copy(index, piece).wait_send()

    def to_tiles(source, k):
        first = source[:, pl.ds(pl.multiple_of(k * LANES, LANES), LANES)].astype(F32)
        second = source[:, pl.ds(pl.multiple_of((k + 16) * LANES, LANES), LANES)].astype(F32)
        return jnp.concatenate([first, second], axis=0).T

    def from_tiles(target, k, first, second):
        turned = jnp.concatenate([first, second], axis=0).T.astype(target.dtype)
        target[:, pl.ds(pl.multiple_of(k * LANES, LANES), LANES)] = turned[:CH]
        target[:, pl.ds(pl.multiple_of((k + 16) * LANES, LANES), LANES)] = turned[CH:]

    def rows_to_cols(load, store):
        @pl.loop(0, 8, unroll=8)
        def _(k):
            turn[pl.ds(pl.multiple_of(k * 64, 64), 64), :] = load(k)

        for t in range(HALF):
            store(t, merge(turn[pl.ds(t, 8, stride=64), :], turn[pl.ds(HALF + t, 8, stride=64), :]))

    def cols_to_rows(load, store):
        @pl.loop(0, HALF, unroll=8)
        def _(t):
            turn[pl.ds(pl.multiple_of(t * 16, 16), 16), :] = load(t)

        for k in range(8):
            store(
                k,
                merge(turn[pl.ds(k, HALF, stride=16), :], turn[pl.ds(8 + k, HALF, stride=16), :]),
            )

    def turn_corner(load, store):
        for k in range(8):
            turn[pl.ds(k * 16, 16), :] = load(k)
        for k in range(8):
            store(k, merge(turn[pl.ds(k, 8, stride=16), :], turn[pl.ds(8 + k, 8, stride=16), :]))

    def pack_forward(index):
        @pl.loop(0, 8, unroll=8)
        def _(k):
            send_a[index, k] = pick(
                swap(frame[32 + k, CENTRE, :]), frame[40 + k, CENTRE, :]
            ).astype(BF16)
            send_b[index, k] = pick(
                frame[16 + k, CENTRE, :], swap(frame[24 + k, CENTRE, :])
            ).astype(BF16)

        @pl.loop(0, HALF, unroll=8)
        def _(t):
            send_l[index, t] = frame[16 + t, slice(64, 80), :].astype(BF16)
            send_r[index, t] = frame[16 + t, slice(16, 32), :].astype(BF16)

    def unpack_forward(index):
        def put_down_left(k, value):
            recv_c[index, FAR_BELOW - 4, k] = value.astype(BF16)

        @pl.when(off == 0)
        def _():
            def put_left(t, value):
                recv_l[index, t] = value.astype(BF16)

            def put_below(k, value):
                recv_b[index, k] = value.astype(BF16)

            rows_to_cols(lambda k: recv_a[index, k].astype(F32), put_left)
            cols_to_rows(lambda t: recv_r[index, t].astype(F32), put_below)
            turn_corner(
                lambda k: recv_c[index, FAR_ABOVE - 4, k].astype(F32), put_down_left
            )

        @pl.when(off == 1)
        def _():
            turn_corner(
                lambda k: send_a[index, k, first, :].astype(F32), put_down_left
            )

        @pl.loop(0, HALF, unroll=8)
        def _(t):
            frame[16 + t, EDGE_LOW, :] = recv_l[index, t].astype(F32)
            frame[16 + t, EDGE_HIGH, :] = recv_r[index, t].astype(F32)

        @pl.loop(0, 8, unroll=8)
        def _(k):
            above, below = (
                jnp.concatenate(
                    [recv_c[index, low - 4, k], strip[index, k], recv_c[index, high - 4, k]], axis=0
                ).astype(F32)
                for low, strip, high in (
                    (CORNER_ABOVE, recv_a, FAR_ABOVE),
                    (FAR_BELOW, recv_b, CORNER_BELOW),
                )
            )
            frame[k] = pick(above, swap(frame[32 + k]))
            frame[8 + k] = swap(pick(frame[40 + k], above))
            frame[48 + k] = swap(pick(below, frame[16 + k]))
            frame[56 + k] = pick(swap(frame[24 + k]), below)

    def prepare_weights(layer):
        weight = weight_ref[layer].astype(F32)
        pieces = [weight[:, j * LANES : (j + 1) * LANES] for j in range(4)]
        pieces.append(
            jnp.concatenate([weight[:, 512:576], jnp.zeros((CH, CH), F32)], axis=1)
        )
        turned = [jnp.concatenate([piece, piece], axis=0).T for piece in pieces]
        for a in range(3):
            for b in range(3):
                for pair, tap in enumerate((3 * a + b, 3 * b + a)):
                    plain = turned[tap // 2][(tap % 2) * CH : (tap % 2) * CH + CH]
                    low = is_low(plain.shape)
                    at = (3 * a + b) * LANES
                    lane = pair * LANES
                    w_fwd[layer, at : at + CH, lane : lane + LANES] = jnp.where(
                        low, plain, 0.0
                    ).astype(BF16)
                    w_fwd[layer, at + CH : at + LANES, lane : lane + LANES] = jnp.where(
                        low, 0.0, plain
                    ).astype(BF16)
                    own = pieces[tap // 2]
                    other = swap(own)
                    if tap % 2:
                        own, other = other, own
                    at = a * 2 * LANES + pair * LANES
                    lane = b * LANES
                    w_bwd[layer, at : at + CH, lane : lane + LANES] = jnp.where(
                        low, own, 0.0
                    ).astype(BF16)
                    w_bwd[layer, at + CH : at + LANES, lane : lane + LANES] = jnp.where(
                        low, 0.0, other
                    ).astype(BF16)

    def shift_columns(layer):
        spread = dilation_ref[layer]

        @pl.loop(0, 64, unroll=4)
        def _(t):
            for b in range(3):
                cols[layer, t, :, b * LANES : (b + 1) * LANES] = frame[
                    t, pl.ds(DMAX + (b - 1) * spread, BLOCK), :
                ].astype(BF16)

    def taps(layer, t, tiles):
        spread = dilation_ref[layer]
        return [
            cols[layer, pl.ds(DMAX + t + (a - 1) * spread, tiles)].reshape(tiles * BLOCK, 3 * LANES)
            for a in range(3)
        ]

    FWD = 8

    def forward(layer):
        bias = bias_ref[layer : layer + 1, :]
        bias = jnp.concatenate([bias, bias, bias, bias], axis=1)

        @pl.loop(0, HALF // FWD, unroll=4)
        def _(step):
            t = step * FWD
            mixed = (
                jnp.dot(
                    jnp.concatenate(taps(layer, t, FWD), axis=1),
                    w_fwd[layer],
                    preferred_element_type=F32,
                )
                + bias
            )
            value, slope = both_gelu(mixed)
            slopes[layer, pl.ds(t, FWD)] = slope.reshape(FWD, BLOCK, 2 * LANES)
            active = 0.5 * (value[:, :LANES] + value[:, LANES:])
            stored = frame[pl.ds(16 + t, FWD), CENTRE, :].reshape(FWD * BLOCK, LANES)
            result = (kept * (stored + active)).astype(BF16).astype(F32)
            result = result.reshape(FWD, BLOCK, LANES)
            if layer == LAYERS - 1:
                last[pl.ds(t, FWD)] = result
            else:
                frame[pl.ds(16 + t, FWD), CENTRE, :] = result

    @pl.loop(0, 16, unroll=4)
    def _(k):
        tiles = (to_tiles(input_ref, k) * kept).astype(BF16).astype(F32)
        frame[16 + 2 * k, CENTRE, :] = tiles[:BLOCK]
        frame[17 + 2 * k, CENTRE, :] = tiles[BLOCK:]

    pack_forward(0)
    pl.semaphore_wait(barrier, count)
    send(0, range(8))
    for layer in range(LAYERS):
        prepare_weights(layer)

    @pl.loop(0, 16, unroll=4)
    def _(k):
        tiles = to_tiles(cot_ref, k)
        grad[2 * k] = tiles[:BLOCK]
        grad[2 * k + 1] = tiles[BLOCK:]

    for layer in range(LAYERS):
        wait(layer, range(8))
        unpack_forward(layer)
        shift_columns(layer)
        forward(layer)
        if layer < LAYERS - 1:
            pack_forward(layer + 1)
            send(layer + 1, range(8))

    @pl.loop(0, 16, unroll=4)
    def _(t):
        slope_low[t] = jnp.zeros((BLOCK, 2 * LANES), BF16)
        slope_low[48 + t] = jnp.zeros((BLOCK, 2 * LANES), BF16)

    @pl.loop(0, BWD, unroll=4)
    def _(t):
        for b in range(3):
            for slot in range(SLOTS):
                padded[slot, b, t, 0:32, :] = jnp.zeros((32, LANES), F32)
                padded[slot, b, t, 96:128, :] = jnp.zeros((32, LANES), F32)

    def slope_step(layer):
        def step(t, total):
            masked = kept * grad[t]
            grad[t] = masked
            half = 0.5 * masked
            slope = slopes[layer, t] * jnp.concatenate([half, half], axis=1)
            slope_low[16 + t] = slope.astype(BF16)
            return total + jnp.sum(slope.reshape(8, 8, 2 * LANES), axis=0)

        return lax.fori_loop(0, HALF, step, jnp.zeros((8, 2 * LANES), F32), unroll=4)

    def tile_grad(layer, steps):
        spread = dilation_ref[layer]

        def part(step, which, slot):
            first = step * BWD
            held = [
                slope_low[pl.ds(first - (a - 1) * spread, BWD)].reshape(BWD * BLOCK, 2 * LANES)
                for a in which
            ]
            left = held[0] if len(held) == 1 else jnp.concatenate(held, axis=1)
            rows = w_bwd[layer, which[0] * 2 * LANES : (which[-1] + 1) * 2 * LANES, :]
            result = jnp.dot(left, rows, preferred_element_type=F32)
            for b in range(3):
                padded[slot, b, :, 32:96, :] = result[:, b * LANES : (b + 1) * LANES].reshape(
                    BWD, BLOCK, LANES
                )
            for at in range(BWD):
                total = None
                for b in range(3):
                    term = padded[slot, b, at, pl.ds(DMAX - (b - 1) * spread, WIDE), :]
                    total = term if total is None else total + term
                frame[first + at] = total

        for count, step in enumerate(steps):
            at = step * BWD
            which = (0,) if at < 16 else (2,) if at >= 48 else (0, 1, 2)
            part(step, which, count % SLOTS)

    def pack_outer(index):
        @pl.loop(0, 8, unroll=8)
        def _(k):
            above[k] = pick(frame[k], swap(frame[8 + k]))
            below[k] = pick(swap(frame[48 + k]), frame[56 + k])

        @pl.when(off == 0)
        def _():
            def add_far(k, value):
                above[k, EDGE_HIGH, :] = above[k, EDGE_HIGH, :] + value

            turn_corner(lambda k: below[k, EDGE_LOW, :], add_far)

        @pl.loop(0, 8, unroll=8)
        def _(k):
            send_b[index, k] = below[k, CENTRE, :].astype(BF16)
            for piece, strip, part in (
                (CORNER_ABOVE, above, EDGE_LOW),
                (FAR_ABOVE, above, EDGE_HIGH),
                (FAR_BELOW, below, EDGE_LOW),
                (CORNER_BELOW, below, EDGE_HIGH),
            ):
                send_c[index - LAYERS, piece - 4, k] = strip[k, part, :].astype(BF16)

        @pl.when(off > 0)
        def _():
            send_above(index)

        send(index, (BELOW, CORNER_ABOVE, FAR_ABOVE, FAR_BELOW, CORNER_BELOW))

    def send_above(index):
        @pl.loop(0, 8, unroll=8)
        def _(k):
            send_a[index, k] = above[k, CENTRE, :].astype(BF16)

        send(index, (ABOVE,))

    def pack_centre(index):
        @pl.when(off == 0)
        def _():
            @pl.loop(0, 8, unroll=8)
            def _(k):
                share(k, EDGE_LOW)

            def add_above(k, value):
                above[k, CENTRE, :] = above[k, CENTRE, :] + value

            cols_to_rows(lambda t: frame[16 + t, EDGE_LOW, :], add_above)
            send_above(index)

            @pl.loop(0, 8, unroll=8)
            def _(k):
                share(k, slice(DMAX, WIDE))

            def add_right(t, value):
                frame[16 + t, EDGE_HIGH, :] = frame[16 + t, EDGE_HIGH, :] + value

            rows_to_cols(lambda k: below[k, CENTRE, :], add_right)

        @pl.when(off > 0)
        def _():
            @pl.loop(0, 8, unroll=8)
            def _(k):
                share(k, slice(0, WIDE))

        @pl.when(off == 1)
        def _():
            def add_own(k, value):
                low = is_low(value.shape)
                at = slice(16, 32)
                frame[32 + k, at, :] = frame[32 + k, at, :] + jnp.where(low, 0.0, swap(value))
                frame[40 + k, at, :] = frame[40 + k, at, :] + jnp.where(low, 0.0, value)

            turn_corner(lambda k: below[k, EDGE_LOW, :], add_own)

        @pl.loop(0, HALF, unroll=8)
        def _(t):
            send_l[index, t] = frame[16 + t, EDGE_LOW, :].astype(BF16)
            send_r[index, t] = frame[16 + t, EDGE_HIGH, :].astype(BF16)

        send(index, (LEFT, RIGHT))

    def share(k, part):
        def add(to, value, keep_low):
            low = is_low(value.shape)
            moved = swap(value)
            moved = jnp.where(low, moved, 0.0) if keep_low else jnp.where(low, 0.0, moved)
            frame[to, part, :] = frame[to, part, :] + moved

        add(16 + k, frame[48 + k, part, :], False)
        add(24 + k, frame[56 + k, part, :], False)
        add(32 + k, frame[k, part, :], True)
        add(40 + k, frame[8 + k, part, :], True)

    def unpack_backward(index):
        @pl.loop(0, HALF, unroll=8)
        def _(t):
            total = grad[t] + frame[16 + t, CENTRE, :]
            right = recv_r[index, t].astype(F32)
            left = recv_l[index, t].astype(F32)
            edge = jnp.concatenate([right, jnp.zeros((32, LANES), F32), left], axis=0)
            grad[t] = total + edge

        @pl.loop(0, 8, unroll=8)
        def _(k):
            def strip(ref, low, high):
                corners = [
                    recv_c[index, high - 4, k].astype(F32),
                    jnp.zeros((32, LANES), F32),
                    recv_c[index, low - 4, k].astype(F32),
                ]
                return ref[index, k].astype(F32) + jnp.concatenate(corners, axis=0)

            top = strip(recv_b, FAR_BELOW, CORNER_BELOW)
            bottom = strip(recv_a, CORNER_ABOVE, FAR_ABOVE)
            low = is_low(top.shape)
            grad[k] = grad[k] + jnp.where(low, top, 0.0)
            grad[8 + k] = grad[8 + k] + jnp.where(low, swap(top), 0.0)
            grad[16 + k] = grad[16 + k] + jnp.where(low, 0.0, swap(bottom))
            grad[24 + k] = grad[24 + k] + jnp.where(low, 0.0, bottom)

    def weight_terms(layer, bias_rows):
        left = slope_low[16:48].reshape(HALF * BLOCK, 2 * LANES)
        for a, part in enumerate(taps(layer, 0, HALF)):
            lane = a * 3 * LANES
            pair_grad[:, lane : lane + 3 * LANES] = lax.dot_general(
                left, part, (((0,), (0,)), ((), ())), preferred_element_type=F32
            )

        def tap_part(tap, half):
            turned = 3 * (tap % 3) + tap // 3
            first = pair_grad[half * CH : half * CH + CH, tap * LANES : (tap + 1) * LANES]
            at = LANES + half * CH
            second = pair_grad[at : at + CH, turned * LANES : (turned + 1) * LANES]
            return first + second

        for j in range(5):
            low_part = tap_part(2 * j, 0) + swap(tap_part(2 * j, 1))
            if j < 4:
                high_part = tap_part(2 * j + 1, 1) + swap(tap_part(2 * j + 1, 0))
            else:
                total = jnp.sum(bias_rows, axis=0, keepdims=True)
                total = total[:, :LANES] + total[:, LANES:]
                total = total + swap(total)
                high_part = jnp.broadcast_to(total, (LANES, LANES)).T[:CH]
            part = pick(low_part, high_part).astype(BF16)
            for at in range(CH // rows):
                term_ref[layer * (CH // rows) + at, :, j * LANES : (j + 1) * LANES] = part[
                    at * rows : (at + 1) * rows
                ]

    def sum_copy(stage, step):
        if stage == 1:
            other, device = across(step)
            source, target = shards.at[mine], shards.at[mine]
        else:
            other, device = in_plane(step)
            if stage == 0:
                source, target = term_ref.at[other], slots.at[step]
            else:
                source, target = whole.at[inner], whole.at[inner]
        return pltpu.make_async_remote_copy(
            src_ref=source,
            dst_ref=target,
            send_sem=sum_send.at[stage, step],
            recv_sem=sum_recv.at[stage, step],
            device_id=device,
            device_id_type=MESH,
        )

    def peers(stage):
        return range(1, many if stage == 1 else group)

    def sum_start(stage):
        if stage == 1:
            total = term_ref[inner].astype(F32)
            for step in peers(0):
                sum_copy(0, step).wait_recv()
                total = total + slots[step].astype(F32)
            shards[mine] = total
        elif stage == 2:
            for step in peers(1):
                sum_copy(1, step).wait_recv()
            total = shards[0]
            for at in range(1, many):
                total = total + shards[at]
            whole[inner] = (total * scale).astype(BF16)
        for step in peers(stage):
            sum_copy(stage, step).start()

    def sum_end():
        for step in peers(2):
            sum_copy(2, step).wait_recv()
        total = jnp.concatenate([whole[at].astype(F32) for at in range(group)], axis=0)
        for layer in range(LAYERS):
            weight_grad_ref[layer] = total[layer * CH : (layer + 1) * CH, :576]
        column = total[:, 4 * LANES :].T[CH : CH + 1]
        bias_grad_ref[0:1, :] = column[:, :CH]
        bias_grad_ref[1:2, :] = swap(column)[:, :CH]
        for stage in range(3):
            for step in peers(stage):
                sum_copy(stage, step).wait_send()

    for layer in reversed(range(LAYERS)):
        index = 2 * LAYERS - 1 - layer
        bias_rows = slope_step(layer)
        if layer == 0:
            weight_terms(layer, bias_rows)
            sum_start(0)
        edge = 64 // BWD // 4
        tile_grad(layer, (*range(edge), *range(3 * edge, 4 * edge)))
        pack_outer(index)
        tile_grad(layer, range(edge, 3 * edge))
        pack_centre(index)
        if layer == 0:
            sum_start(1)
            sum_start(2)
        else:
            weight_terms(layer, bias_rows)

            @pl.loop(0, 16, unroll=4)
            def _(k):
                from_tiles(out_ref, k, last[2 * k], last[2 * k + 1])

        wait(index, range(8))
        unpack_backward(index)

    @pl.loop(0, 16, unroll=4)
    def _(k):
        from_tiles(grad_ref, k, kept * grad[2 * k], kept * grad[2 * k + 1])

    sum_end()
    for index in range(2 * LAYERS):
        finish(index)


def finish_kernel(*refs):
    sources, targets, sems = refs[:4], refs[4:8], refs[8]
    copies = []
    for at, (source, target) in enumerate(zip(sources, targets)):
        parts = 4 if at < 2 else 1
        for part in range(parts):
            if parts > 1:
                lanes = source.shape[1] // parts
                span = pl.ds(part * lanes, lanes)
                pair = source.at[:, span], target.at[:, span]
            else:
                pair = source, target
            copies.append(pltpu.make_async_copy(*pair, sems.at[at, part]))
            copies[-1].start()
    for copy in copies:
        copy.wait()


def per_device(input_map, cotangent, band_width, dilation, conv_weight, conv_bias):
    rows_all = lax.axis_size("pos")
    offsets_all = lax.axis_size("band")
    bins = BLOCK * BLOCK
    vmem = pl.BlockSpec(memory_space=pltpu.VMEM)
    smem = pl.BlockSpec(memory_space=pltpu.SMEM)
    group = 16 if rows_all % 16 == 0 else rows_all
    many = rows_all // group * offsets_all
    shard = (LAYERS * CH // group, 5 * LANES)
    scale = 1.0 / (BLOCK * math.sqrt(input_map.shape[0] * rows_all * offsets_all))
    shapes = (
        jax.ShapeDtypeStruct((CH, bins), BF16),
        jax.ShapeDtypeStruct((CH, bins), F32),
        jax.ShapeDtypeStruct((LAYERS, CH, 576), F32),
        jax.ShapeDtypeStruct((LAYERS, CH), F32),
    )
    results = pl.pallas_call(
        functools.partial(net_kernel, rows_all, offsets_all, scale),
        out_shape=shapes,
        in_specs=[smem, smem, vmem, vmem, vmem, vmem],
        out_specs=(vmem, vmem, vmem, vmem),
        scratch_shapes=[
            pltpu.VMEM((64, WIDE, LANES), F32),
            pltpu.VMEM((HALF, BLOCK, LANES), F32),
            pltpu.VMEM((group, *shard), BF16),
            pltpu.VMEM((group, *shard), BF16),
            pltpu.VMEM((many, *shard), F32),
            pltpu.VMEM((group, *shard), BF16),
            pltpu.VMEM((LAYERS, 64, BLOCK, 3 * LANES), BF16),
            pltpu.VMEM((LAYERS, HALF, BLOCK, 2 * LANES), F32),
            pltpu.VMEM((64, BLOCK, 2 * LANES), BF16),
            pltpu.VMEM((SLOTS, 3, BWD, 128, LANES), F32),
            pltpu.VMEM((HALF, BLOCK, LANES), F32),
            pltpu.VMEM((8, WIDE, LANES), F32),
            pltpu.VMEM((8, WIDE, LANES), F32),
            pltpu.VMEM((2 * LANES, 9 * LANES), F32),
            pltpu.VMEM((LAYERS, 9 * LANES, 2 * LANES), BF16),
            pltpu.VMEM((LAYERS, 6 * LANES, 3 * LANES), BF16),
            pltpu.VMEM((512, LANES), F32),
            pltpu.VMEM((4, 8, BLOCK, LANES), BF16),
            pltpu.VMEM((4, 8, BLOCK, LANES), BF16),
            pltpu.VMEM((4, HALF, DMAX, LANES), BF16),
            pltpu.VMEM((4, HALF, DMAX, LANES), BF16),
            pltpu.VMEM((2, 4, 8, DMAX, LANES), BF16),
            pltpu.VMEM((4, 8, BLOCK, LANES), BF16),
            pltpu.VMEM((4, 8, BLOCK, LANES), BF16),
            pltpu.VMEM((4, HALF, DMAX, LANES), BF16),
            pltpu.VMEM((4, HALF, DMAX, LANES), BF16),
            pltpu.VMEM((4, 4, 8, DMAX, LANES), BF16),
            pltpu.SemaphoreType.DMA((4, 8)),
            pltpu.SemaphoreType.DMA((4, 8)),
            pltpu.SemaphoreType.DMA((3, 16)),
            pltpu.SemaphoreType.DMA((3, 16)),
        ],
        compiler_params=pltpu.CompilerParams(
            collective_id=0, has_side_effects=True, vmem_limit_bytes=46 * 2**20
        ),
        name="net",
    )(
        band_width,
        dilation,
        input_map.reshape(CH, bins),
        cotangent.reshape(CH, bins),
        conv_weight,
        conv_bias,
    )
    anywhere = pl.BlockSpec(memory_space=pl.ANY)
    output, input_grad, weight_grad, bias_grad = pl.pallas_call(
        finish_kernel,
        out_shape=shapes,
        in_specs=[vmem] * 4,
        out_specs=(anywhere,) * 4,
        scratch_shapes=[pltpu.SemaphoreType.DMA((4, 4))],
        compiler_params=pltpu.CompilerParams(vmem_limit_bytes=4 * 2**20),
        name="finish",
    )(*results)
    return (
        output.reshape(input_map.shape),
        input_grad.reshape(input_map.shape),
        weight_grad,
        bias_grad,
    )


def solution(mesh):
    split = P(None, "pos", "band", None, None)
    return jax.shard_map(
        per_device,
        mesh=mesh,
        in_specs=(split, split, P("pos"), P(), P(), P()),
        out_specs=(split, split, P(), P()),
        check_vma=False,
    )
```

```python
import functools
import math

import jax
import jax.numpy as jnp
from jax import lax
from jax.experimental import pallas as pl
from jax.experimental.pallas import tpu as pltpu
from jax.sharding import PartitionSpec as P

BLOCK = 64
DMAX = 16
LAYERS = 2
BWD = 8
SLOTS = 2
CH = 64
LANES = 128
HALF = 32
WIDE = BLOCK + 2 * DMAX
F32 = jnp.float32
BF16 = jnp.bfloat16
MESH = pl.DeviceIdType.MESH

STEPS = ((1, -1), (0, -1), (0, 1), (-1, 1), (1, 0), (1, -2), (-1, 2), (-1, 0))
ABOVE, RIGHT, LEFT, BELOW, CORNER_ABOVE, FAR_ABOVE, FAR_BELOW, CORNER_BELOW = range(8)
EDGE_LOW = slice(0, DMAX)
CENTRE = slice(DMAX, DMAX + BLOCK)
EDGE_HIGH = slice(DMAX + BLOCK, WIDE)
SQRT_2_PI = math.sqrt(2.0 / math.pi)
CUBIC = 0.044715


def is_low(shape):
    return lax.broadcasted_iota(jnp.int32, shape, len(shape) - 1) < CH


def swap(value):
    return pltpu.roll(value, CH, value.ndim - 1)


def pick(low_value, high_value):
    return jnp.where(is_low(low_value.shape), low_value, high_value)


def merge(first, second):
    return jnp.concatenate([pick(first, swap(second)), pick(swap(first), second)], axis=0)


def both_gelu(value):
    square = value * value
    inner = SQRT_2_PI * (value + CUBIC * (square * value))
    bend = jnp.tanh(inner)
    cdf = 0.5 * (1.0 + bend)
    slope = cdf + 0.5 * value * (1.0 - bend * bend) * (SQRT_2_PI * (1.0 + 3.0 * CUBIC * square))
    return value * cdf, slope


def net_kernel(
    rows_all,
    offsets_all,
    scale,
    width_ref,
    dilation_ref,
    input_hbm,
    cot_hbm,
    weight_hbm,
    bias_hbm,
    out_ref,
    grad_ref,
    weight_grad_ref,
    bias_grad_ref,
    input_ref,
    cot_ref,
    weight_ref,
    bias_ref,
    load_sem,
    frame,
    last,
    term_ref,
    slots,
    shards,
    whole,
    cols,
    slopes,
    slope_low,
    padded,
    grad,
    above,
    below,
    pair_grad,
    w_fwd,
    w_bwd,
    turn,
    send_a,
    send_b,
    send_l,
    send_r,
    send_c,
    recv_a,
    recv_b,
    recv_l,
    recv_r,
    recv_c,
    send_sem,
    recv_sem,
    sum_send,
    sum_recv,
):
    row = lax.axis_index("pos")
    off = lax.axis_index("band")
    loads = [
        pltpu.make_async_copy(source, target, load_sem.at[at])
        for at, (source, target) in enumerate(
            (
                (input_hbm, input_ref),
                (weight_hbm, weight_ref),
                (bias_hbm, bias_ref),
                (cot_hbm, cot_ref),
            )
        )
    ]
    for load in loads:
        load.start()

    def exists(di, do):
        return (row + di >= 0) & (row + di < rows_all) & (off + do >= 0) & (off + do < offsets_all)

    group = whole.shape[0]
    many = shards.shape[0]
    rows = term_ref.shape[1]
    inner = lax.rem(row, group)
    high = lax.div(row, group)
    mine = high * offsets_all + off

    def in_plane(step):
        other = lax.rem(inner + step, group)
        return other, {"pos": high * group + other, "band": off}

    def across(step):
        other = lax.rem(mine + step, many)
        return other, {
            "pos": lax.div(other, offsets_all) * group + inner,
            "band": lax.rem(other, offsets_all),
        }

    kept = jnp.where(
        (off <= width_ref[0]) & (row + off < rows_all), jnp.float32(1.0), jnp.float32(0.0)
    )

    first, final = slice(0, DMAX), slice(BLOCK - DMAX, BLOCK)
    strips = {
        ABOVE: (send_a, recv_a),
        RIGHT: (send_r, recv_r),
        LEFT: (send_l, recv_l),
        BELOW: (send_b, recv_b),
    }
    corners = {
        CORNER_ABOVE: (send_a, final),
        FAR_ABOVE: (send_a, first),
        FAR_BELOW: (send_b, final),
        CORNER_BELOW: (send_b, first),
    }

    def arrival(index, piece):
        if piece in corners:
            return recv_c.at[index, piece - 4]
        return strips[piece][1].at[index]

    def departure(index, piece):
        if piece in strips:
            return strips[piece][0].at[index]
        if index < LAYERS:
            source, part = corners[piece]
            return source.at[index, :, part, :]
        return send_c.at[index - LAYERS, piece - 4]

    for piece in range(8):
        di, do = STEPS[piece]
        for sign, indices in ((1, (0, 1)), (-1, (2, 3))):

            @pl.when(jnp.logical_not(exists(-sign * di, -sign * do)))
            def _():
                for index in indices:
                    there = arrival(index, piece)
                    there[...] = jnp.zeros(there.shape, BF16)

    barrier = pltpu.get_barrier_semaphore()
    count = jnp.int32(0)
    for di, do in STEPS:
        count = count + exists(di, do).astype(jnp.int32)

        @pl.when(exists(di, do))
        def _():
            pl.semaphore_signal(
                barrier,
                inc=1,
                device_id={"pos": row + di, "band": off + do},
                device_id_type=MESH,
            )

    for step in range(1, group):
        pl.semaphore_signal(barrier, inc=1, device_id=in_plane(step)[1], device_id_type=MESH)
    for step in range(1, many):
        pl.semaphore_signal(barrier, inc=1, device_id=across(step)[1], device_id_type=MESH)
    count = count + (group + many - 2)

    def piece_copy(index, piece):
        di, do = STEPS[piece]
        sign = 1 if index < LAYERS else -1
        return pltpu.make_async_remote_copy(
            src_ref=departure(index, piece),
            dst_ref=arrival(index, piece),
            send_sem=send_sem.at[index, piece],
            recv_sem=recv_sem.at[index, piece],
            device_id={"pos": row + sign * di, "band": off + sign * do},
            device_id_type=MESH,
        )

    def send(index, pieces):
        sign = 1 if index < LAYERS else -1
        for piece in pieces:
            di, do = STEPS[piece]

            @pl.when(exists(sign * di, sign * do))
            def _():
                piece_copy(index, piece).start()

    def wait(index, pieces):
        sign = 1 if index < LAYERS else -1
        for piece in pieces:
            di, do = STEPS[piece]

            @pl.when(exists(-sign * di, -sign * do))
            def _():
                piece_copy(index, piece).wait_recv()

    def finish(index):
        sign = 1 if index < LAYERS else -1
        for piece in range(8):
            di, do = STEPS[piece]

            @pl.when(exists(sign * di, sign * do))
            def _():
                piece_copy(index, piece).wait_send()

    def to_tiles(source, k):
        first = source[:, pl.ds(pl.multiple_of(k * LANES, LANES), LANES)].astype(F32)
        second = source[:, pl.ds(pl.multiple_of((k + 16) * LANES, LANES), LANES)].astype(F32)
        return jnp.concatenate([first, second], axis=0).T

    def from_tiles(target, k, first, second):
        turned = jnp.concatenate([first, second], axis=0).T.astype(target.dtype)
        target[:, pl.ds(pl.multiple_of(k * LANES, LANES), LANES)] = turned[:CH]
        target[:, pl.ds(pl.multiple_of((k + 16) * LANES, LANES), LANES)] = turned[CH:]

    def rows_to_cols(load, store):
        @pl.loop(0, 8, unroll=8)
        def _(k):
            turn[pl.ds(pl.multiple_of(k * 64, 64), 64), :] = load(k)

        for t in range(HALF):
            store(t, merge(turn[pl.ds(t, 8, stride=64), :], turn[pl.ds(HALF + t, 8, stride=64), :]))

    def cols_to_rows(load, store):
        @pl.loop(0, HALF, unroll=8)
        def _(t):
            turn[pl.ds(pl.multiple_of(t * 16, 16), 16), :] = load(t)

        for k in range(8):
            store(
                k,
                merge(turn[pl.ds(k, HALF, stride=16), :], turn[pl.ds(8 + k, HALF, stride=16), :]),
            )

    def turn_corner(load, store):
        for k in range(8):
            turn[pl.ds(k * 16, 16), :] = load(k)
        for k in range(8):
            store(k, merge(turn[pl.ds(k, 8, stride=16), :], turn[pl.ds(8 + k, 8, stride=16), :]))

    def pack_forward(index):
        @pl.loop(0, 8, unroll=8)
        def _(k):
            send_a[index, k] = pick(
                swap(frame[32 + k, CENTRE, :]), frame[40 + k, CENTRE, :]
            ).astype(BF16)
            send_b[index, k] = pick(
                frame[16 + k, CENTRE, :], swap(frame[24 + k, CENTRE, :])
            ).astype(BF16)

        @pl.loop(0, HALF, unroll=8)
        def _(t):
            send_l[index, t] = frame[16 + t, slice(64, 80), :].astype(BF16)
            send_r[index, t] = frame[16 + t, slice(16, 32), :].astype(BF16)

    def unpack_forward(index):
        def put_down_left(k, value):
            recv_c[index, FAR_BELOW - 4, k] = value.astype(BF16)

        @pl.when(off == 0)
        def _():
            def put_left(t, value):
                recv_l[index, t] = value.astype(BF16)

            def put_below(k, value):
                recv_b[index, k] = value.astype(BF16)

            rows_to_cols(lambda k: recv_a[index, k].astype(F32), put_left)
            cols_to_rows(lambda t: recv_r[index, t].astype(F32), put_below)
            turn_corner(
                lambda k: recv_c[index, FAR_ABOVE - 4, k].astype(F32), put_down_left
            )

        @pl.when(off == 1)
        def _():
            turn_corner(
                lambda k: send_a[index, k, first, :].astype(F32), put_down_left
            )

        @pl.loop(0, HALF, unroll=8)
        def _(t):
            frame[16 + t, EDGE_LOW, :] = recv_l[index, t].astype(F32)
            frame[16 + t, EDGE_HIGH, :] = recv_r[index, t].astype(F32)

        @pl.loop(0, 8, unroll=8)
        def _(k):
            above, below = (
                jnp.concatenate(
                    [recv_c[index, low - 4, k], strip[index, k], recv_c[index, high - 4, k]], axis=0
                ).astype(F32)
                for low, strip, high in (
                    (CORNER_ABOVE, recv_a, FAR_ABOVE),
                    (FAR_BELOW, recv_b, CORNER_BELOW),
                )
            )
            frame[k] = pick(above, swap(frame[32 + k]))
            frame[8 + k] = swap(pick(frame[40 + k], above))
            frame[48 + k] = swap(pick(below, frame[16 + k]))
            frame[56 + k] = pick(swap(frame[24 + k]), below)

    def prepare_weights(layer):
        weight = weight_ref[layer].astype(F32)
        pieces = [weight[:, j * LANES : (j + 1) * LANES] for j in range(4)]
        pieces.append(
            jnp.concatenate([weight[:, 512:576], jnp.zeros((CH, CH), F32)], axis=1)
        )
        turned = [jnp.concatenate([piece, piece], axis=0).T for piece in pieces]
        for a in range(3):
            for b in range(3):
                for pair, tap in enumerate((3 * a + b, 3 * b + a)):
                    plain = turned[tap // 2][(tap % 2) * CH : (tap % 2) * CH + CH]
                    low = is_low(plain.shape)
                    at = (3 * a + b) * LANES
                    lane = pair * LANES
                    w_fwd[layer, at : at + CH, lane : lane + LANES] = jnp.where(
                        low, plain, 0.0
                    ).astype(BF16)
                    w_fwd[layer, at + CH : at + LANES, lane : lane + LANES] = jnp.where(
                        low, 0.0, plain
                    ).astype(BF16)
                    own = pieces[tap // 2]
                    other = swap(own)
                    if tap % 2:
                        own, other = other, own
                    at = a * 2 * LANES + pair * LANES
                    lane = b * LANES
                    w_bwd[layer, at : at + CH, lane : lane + LANES] = jnp.where(
                        low, own, 0.0
                    ).astype(BF16)
                    w_bwd[layer, at + CH : at + LANES, lane : lane + LANES] = jnp.where(
                        low, 0.0, other
                    ).astype(BF16)

    def shift_columns(layer):
        spread = dilation_ref[layer]

        @pl.loop(0, 64, unroll=4)
        def _(t):
            for b in range(3):
                cols[layer, t, :, b * LANES : (b + 1) * LANES] = frame[
                    t, pl.ds(DMAX + (b - 1) * spread, BLOCK), :
                ].astype(BF16)

    def taps(layer, t, tiles):
        spread = dilation_ref[layer]
        return [
            cols[layer, pl.ds(DMAX + t + (a - 1) * spread, tiles)].reshape(tiles * BLOCK, 3 * LANES)
            for a in range(3)
        ]

    FWD = 8

    def forward(layer):
        bias = bias_ref[layer : layer + 1, :]
        bias = jnp.concatenate([bias, bias, bias, bias], axis=1)

        @pl.loop(0, HALF // FWD, unroll=4)
        def _(step):
            t = step * FWD
            mixed = (
                jnp.dot(
                    jnp.concatenate(taps(layer, t, FWD), axis=1),
                    w_fwd[layer],
                    preferred_element_type=F32,
                )
                + bias
            )
            value, slope = both_gelu(mixed)
            slopes[layer, pl.ds(t, FWD)] = slope.reshape(FWD, BLOCK, 2 * LANES)
            active = 0.5 * (value[:, :LANES] + value[:, LANES:])
            stored = frame[pl.ds(16 + t, FWD), CENTRE, :].reshape(FWD * BLOCK, LANES)
            result = (kept * (stored + active)).astype(BF16).astype(F32)
            result = result.reshape(FWD, BLOCK, LANES)
            if layer == LAYERS - 1:
                last[pl.ds(t, FWD)] = result
            else:
                frame[pl.ds(16 + t, FWD), CENTRE, :] = result

    loads[0].wait()

    @pl.loop(0, 16, unroll=4)
    def _(k):
        tiles = (to_tiles(input_ref, k) * kept).astype(BF16).astype(F32)
        frame[16 + 2 * k, CENTRE, :] = tiles[:BLOCK]
        frame[17 + 2 * k, CENTRE, :] = tiles[BLOCK:]

    pack_forward(0)
    pl.semaphore_wait(barrier, count)
    send(0, range(8))
    loads[1].wait()
    loads[2].wait()
    for layer in range(LAYERS):
        prepare_weights(layer)
    loads[3].wait()

    @pl.loop(0, 16, unroll=4)
    def _(k):
        tiles = to_tiles(cot_ref, k)
        grad[2 * k] = tiles[:BLOCK]
        grad[2 * k + 1] = tiles[BLOCK:]

    for layer in range(LAYERS):
        wait(layer, range(8))
        unpack_forward(layer)
        shift_columns(layer)
        forward(layer)
        if layer < LAYERS - 1:
            pack_forward(layer + 1)
            send(layer + 1, range(8))

    @pl.loop(0, 16, unroll=4)
    def _(t):
        slope_low[t] = jnp.zeros((BLOCK, 2 * LANES), BF16)
        slope_low[48 + t] = jnp.zeros((BLOCK, 2 * LANES), BF16)

    @pl.loop(0, BWD, unroll=4)
    def _(t):
        for b in range(3):
            for slot in range(SLOTS):
                padded[slot, b, t, 0:32, :] = jnp.zeros((32, LANES), F32)
                padded[slot, b, t, 96:128, :] = jnp.zeros((32, LANES), F32)

    def slope_step(layer):
        def step(t, total):
            masked = kept * grad[t]
            grad[t] = masked
            half = 0.5 * masked
            slope = slopes[layer, t] * jnp.concatenate([half, half], axis=1)
            slope_low[16 + t] = slope.astype(BF16)
            return total + jnp.sum(slope.reshape(8, 8, 2 * LANES), axis=0)

        return lax.fori_loop(0, HALF, step, jnp.zeros((8, 2 * LANES), F32), unroll=4)

    def tile_grad(layer, steps):
        spread = dilation_ref[layer]

        def part(step, which, slot):
            first = step * BWD
            held = [
                slope_low[pl.ds(first - (a - 1) * spread, BWD)].reshape(BWD * BLOCK, 2 * LANES)
                for a in which
            ]
            left = held[0] if len(held) == 1 else jnp.concatenate(held, axis=1)
            rows = w_bwd[layer, which[0] * 2 * LANES : (which[-1] + 1) * 2 * LANES, :]
            result = jnp.dot(left, rows, preferred_element_type=F32)
            for b in range(3):
                padded[slot, b, :, 32:96, :] = result[:, b * LANES : (b + 1) * LANES].reshape(
                    BWD, BLOCK, LANES
                )
            for at in range(BWD):
                total = None
                for b in range(3):
                    term = padded[slot, b, at, pl.ds(DMAX - (b - 1) * spread, WIDE), :]
                    total = term if total is None else total + term
                frame[first + at] = total

        for count, step in enumerate(steps):
            at = step * BWD
            which = (0,) if at < 16 else (2,) if at >= 48 else (0, 1, 2)
            part(step, which, count % SLOTS)

    def pack_outer(index):
        @pl.loop(0, 8, unroll=8)
        def _(k):
            above[k] = pick(frame[k], swap(frame[8 + k]))
            below[k] = pick(swap(frame[48 + k]), frame[56 + k])

        @pl.when(off == 0)
        def _():
            def add_far(k, value):
                above[k, EDGE_HIGH, :] = above[k, EDGE_HIGH, :] + value

            turn_corner(lambda k: below[k, EDGE_LOW, :], add_far)

        @pl.loop(0, 8, unroll=8)
        def _(k):
            send_b[index, k] = below[k, CENTRE, :].astype(BF16)
            for piece, strip, part in (
                (CORNER_ABOVE, above, EDGE_LOW),
                (FAR_ABOVE, above, EDGE_HIGH),
                (FAR_BELOW, below, EDGE_LOW),
                (CORNER_BELOW, below, EDGE_HIGH),
            ):
                send_c[index - LAYERS, piece - 4, k] = strip[k, part, :].astype(BF16)

        @pl.when(off > 0)
        def _():
            send_above(index)

        send(index, (BELOW, CORNER_ABOVE, FAR_ABOVE, FAR_BELOW, CORNER_BELOW))

    def send_above(index):
        @pl.loop(0, 8, unroll=8)
        def _(k):
            send_a[index, k] = above[k, CENTRE, :].astype(BF16)

        send(index, (ABOVE,))

    def pack_centre(index):
        @pl.when(off == 0)
        def _():
            @pl.loop(0, 8, unroll=8)
            def _(k):
                share(k, EDGE_LOW)

            def add_above(k, value):
                above[k, CENTRE, :] = above[k, CENTRE, :] + value

            cols_to_rows(lambda t: frame[16 + t, EDGE_LOW, :], add_above)
            send_above(index)

            @pl.loop(0, 8, unroll=8)
            def _(k):
                share(k, slice(DMAX, WIDE))

            def add_right(t, value):
                frame[16 + t, EDGE_HIGH, :] = frame[16 + t, EDGE_HIGH, :] + value

            rows_to_cols(lambda k: below[k, CENTRE, :], add_right)

        @pl.when(off > 0)
        def _():
            @pl.loop(0, 8, unroll=8)
            def _(k):
                share(k, slice(0, WIDE))

        @pl.when(off == 1)
        def _():
            def add_own(k, value):
                low = is_low(value.shape)
                at = slice(16, 32)
                frame[32 + k, at, :] = frame[32 + k, at, :] + jnp.where(low, 0.0, swap(value))
                frame[40 + k, at, :] = frame[40 + k, at, :] + jnp.where(low, 0.0, value)

            turn_corner(lambda k: below[k, EDGE_LOW, :], add_own)

        @pl.loop(0, HALF, unroll=8)
        def _(t):
            send_l[index, t] = frame[16 + t, EDGE_LOW, :].astype(BF16)
            send_r[index, t] = frame[16 + t, EDGE_HIGH, :].astype(BF16)

        send(index, (LEFT, RIGHT))

    def share(k, part):
        def add(to, value, keep_low):
            low = is_low(value.shape)
            moved = swap(value)
            moved = jnp.where(low, moved, 0.0) if keep_low else jnp.where(low, 0.0, moved)
            frame[to, part, :] = frame[to, part, :] + moved

        add(16 + k, frame[48 + k, part, :], False)
        add(24 + k, frame[56 + k, part, :], False)
        add(32 + k, frame[k, part, :], True)
        add(40 + k, frame[8 + k, part, :], True)

    def unpack_backward(index):
        @pl.loop(0, HALF, unroll=8)
        def _(t):
            total = grad[t] + frame[16 + t, CENTRE, :]
            right = recv_r[index, t].astype(F32)
            left = recv_l[index, t].astype(F32)
            edge = jnp.concatenate([right, jnp.zeros((32, LANES), F32), left], axis=0)
            grad[t] = total + edge

        @pl.loop(0, 8, unroll=8)
        def _(k):
            def strip(ref, low, high):
                corners = [
                    recv_c[index, high - 4, k].astype(F32),
                    jnp.zeros((32, LANES), F32),
                    recv_c[index, low - 4, k].astype(F32),
                ]
                return ref[index, k].astype(F32) + jnp.concatenate(corners, axis=0)

            top = strip(recv_b, FAR_BELOW, CORNER_BELOW)
            bottom = strip(recv_a, CORNER_ABOVE, FAR_ABOVE)
            low = is_low(top.shape)
            grad[k] = grad[k] + jnp.where(low, top, 0.0)
            grad[8 + k] = grad[8 + k] + jnp.where(low, swap(top), 0.0)
            grad[16 + k] = grad[16 + k] + jnp.where(low, 0.0, swap(bottom))
            grad[24 + k] = grad[24 + k] + jnp.where(low, 0.0, bottom)

    def weight_terms(layer, bias_rows):
        left = slope_low[16:48].reshape(HALF * BLOCK, 2 * LANES)
        for a, part in enumerate(taps(layer, 0, HALF)):
            lane = a * 3 * LANES
            pair_grad[:, lane : lane + 3 * LANES] = lax.dot_general(
                left, part, (((0,), (0,)), ((), ())), preferred_element_type=F32
            )

        def tap_part(tap, half):
            turned = 3 * (tap % 3) + tap // 3
            first = pair_grad[half * CH : half * CH + CH, tap * LANES : (tap + 1) * LANES]
            at = LANES + half * CH
            second = pair_grad[at : at + CH, turned * LANES : (turned + 1) * LANES]
            return first + second

        for j in range(5):
            low_part = tap_part(2 * j, 0) + swap(tap_part(2 * j, 1))
            if j < 4:
                high_part = tap_part(2 * j + 1, 1) + swap(tap_part(2 * j + 1, 0))
            else:
                total = jnp.sum(bias_rows, axis=0, keepdims=True)
                total = total[:, :LANES] + total[:, LANES:]
                total = total + swap(total)
                high_part = jnp.broadcast_to(total, (LANES, LANES)).T[:CH]
            part = pick(low_part, high_part).astype(BF16)
            for at in range(CH // rows):
                term_ref[layer * (CH // rows) + at, :, j * LANES : (j + 1) * LANES] = part[
                    at * rows : (at + 1) * rows
                ]

    def sum_copy(stage, step):
        if stage == 1:
            other, device = across(step)
            source, target = shards.at[mine], shards.at[mine]
        else:
            other, device = in_plane(step)
            if stage == 0:
                source, target = term_ref.at[other], slots.at[step]
            else:
                source, target = whole.at[inner], whole.at[inner]
        return pltpu.make_async_remote_copy(
            src_ref=source,
            dst_ref=target,
            send_sem=sum_send.at[stage, step],
            recv_sem=sum_recv.at[stage, step],
            device_id=device,
            device_id_type=MESH,
        )

    def peers(stage):
        return range(1, many if stage == 1 else group)

    def sum_start(stage):
        if stage == 1:
            total = term_ref[inner].astype(F32)
            for step in peers(0):
                sum_copy(0, step).wait_recv()
                total = total + slots[step].astype(F32)
            shards[mine] = total
        elif stage == 2:
            for step in peers(1):
                sum_copy(1, step).wait_recv()
            total = shards[0]
            for at in range(1, many):
                total = total + shards[at]
            whole[inner] = (total * scale).astype(BF16)
        for step in peers(stage):
            sum_copy(stage, step).start()

    def sum_end():
        for step in peers(2):
            sum_copy(2, step).wait_recv()
        total = jnp.concatenate([whole[at].astype(F32) for at in range(group)], axis=0)
        for layer in range(LAYERS):
            weight_grad_ref[layer] = total[layer * CH : (layer + 1) * CH, :576]
        column = total[:, 4 * LANES :].T[CH : CH + 1]
        bias_grad_ref[0:1, :] = column[:, :CH]
        bias_grad_ref[1:2, :] = swap(column)[:, :CH]
        for stage in range(3):
            for step in peers(stage):
                sum_copy(stage, step).wait_send()

    for layer in reversed(range(LAYERS)):
        index = 2 * LAYERS - 1 - layer
        bias_rows = slope_step(layer)
        if layer == 0:
            weight_terms(layer, bias_rows)
            sum_start(0)
        edge = 64 // BWD // 4
        tile_grad(layer, (*range(edge), *range(3 * edge, 4 * edge)))
        pack_outer(index)
        tile_grad(layer, range(edge, 3 * edge))
        pack_centre(index)
        if layer == 0:
            sum_start(1)
            sum_start(2)
        else:
            weight_terms(layer, bias_rows)

            @pl.loop(0, 16, unroll=4)
            def _(k):
                from_tiles(out_ref, k, last[2 * k], last[2 * k + 1])

        wait(index, range(8))
        unpack_backward(index)

    @pl.loop(0, 16, unroll=4)
    def _(k):
        from_tiles(grad_ref, k, kept * grad[2 * k], kept * grad[2 * k + 1])

    sum_end()
    for index in range(2 * LAYERS):
        finish(index)


def finish_kernel(*refs):
    sources, targets, sems = refs[:4], refs[4:8], refs[8]
    copies = []
    for at, (source, target) in enumerate(zip(sources, targets)):
        parts = 4 if at < 2 else 1
        for part in range(parts):
            if parts > 1:
                lanes = source.shape[1] // parts
                span = pl.ds(part * lanes, lanes)
                pair = source.at[:, span], target.at[:, span]
            else:
                pair = source, target
            copies.append(pltpu.make_async_copy(*pair, sems.at[at, part]))
            copies[-1].start()
    for copy in copies:
        copy.wait()


def per_device(input_map, cotangent, band_width, dilation, conv_weight, conv_bias):
    rows_all = lax.axis_size("pos")
    offsets_all = lax.axis_size("band")
    bins = BLOCK * BLOCK
    vmem = pl.BlockSpec(memory_space=pltpu.VMEM)
    smem = pl.BlockSpec(memory_space=pltpu.SMEM)
    hbm = pl.BlockSpec(memory_space=pltpu.HBM)
    group = 16 if rows_all % 16 == 0 else rows_all
    many = rows_all // group * offsets_all
    shard = (LAYERS * CH // group, 5 * LANES)
    scale = 1.0 / (BLOCK * math.sqrt(input_map.shape[0] * rows_all * offsets_all))
    shapes = (
        jax.ShapeDtypeStruct((CH, bins), BF16),
        jax.ShapeDtypeStruct((CH, bins), F32),
        jax.ShapeDtypeStruct((LAYERS, CH, 576), F32),
        jax.ShapeDtypeStruct((LAYERS, CH), F32),
    )
    results = pl.pallas_call(
        functools.partial(net_kernel, rows_all, offsets_all, scale),
        out_shape=shapes,
        in_specs=[smem, smem, hbm, hbm, hbm, hbm],
        out_specs=(vmem, vmem, vmem, vmem),
        scratch_shapes=[
            pltpu.VMEM((CH, bins), BF16),
            pltpu.VMEM((CH, bins), BF16),
            pltpu.VMEM((LAYERS, CH, 576), BF16),
            pltpu.VMEM((LAYERS, CH), F32),
            pltpu.SemaphoreType.DMA((4,)),
            pltpu.VMEM((64, WIDE, LANES), F32),
            pltpu.VMEM((HALF, BLOCK, LANES), F32),
            pltpu.VMEM((group, *shard), BF16),
            pltpu.VMEM((group, *shard), BF16),
            pltpu.VMEM((many, *shard), F32),
            pltpu.VMEM((group, *shard), BF16),
            pltpu.VMEM((LAYERS, 64, BLOCK, 3 * LANES), BF16),
            pltpu.VMEM((LAYERS, HALF, BLOCK, 2 * LANES), F32),
            pltpu.VMEM((64, BLOCK, 2 * LANES), BF16),
            pltpu.VMEM((SLOTS, 3, BWD, 128, LANES), F32),
            pltpu.VMEM((HALF, BLOCK, LANES), F32),
            pltpu.VMEM((8, WIDE, LANES), F32),
            pltpu.VMEM((8, WIDE, LANES), F32),
            pltpu.VMEM((2 * LANES, 9 * LANES), F32),
            pltpu.VMEM((LAYERS, 9 * LANES, 2 * LANES), BF16),
            pltpu.VMEM((LAYERS, 6 * LANES, 3 * LANES), BF16),
            pltpu.VMEM((512, LANES), F32),
            pltpu.VMEM((4, 8, BLOCK, LANES), BF16),
            pltpu.VMEM((4, 8, BLOCK, LANES), BF16),
            pltpu.VMEM((4, HALF, DMAX, LANES), BF16),
            pltpu.VMEM((4, HALF, DMAX, LANES), BF16),
            pltpu.VMEM((2, 4, 8, DMAX, LANES), BF16),
            pltpu.VMEM((4, 8, BLOCK, LANES), BF16),
            pltpu.VMEM((4, 8, BLOCK, LANES), BF16),
            pltpu.VMEM((4, HALF, DMAX, LANES), BF16),
            pltpu.VMEM((4, HALF, DMAX, LANES), BF16),
            pltpu.VMEM((4, 4, 8, DMAX, LANES), BF16),
            pltpu.SemaphoreType.DMA((4, 8)),
            pltpu.SemaphoreType.DMA((4, 8)),
            pltpu.SemaphoreType.DMA((3, 16)),
            pltpu.SemaphoreType.DMA((3, 16)),
        ],
        compiler_params=pltpu.CompilerParams(
            collective_id=0, has_side_effects=True, vmem_limit_bytes=46 * 2**20
        ),
        name="net",
    )(
        band_width,
        dilation,
        pltpu.with_memory_space_constraint(input_map.reshape(CH, bins), pltpu.HBM),
        pltpu.with_memory_space_constraint(cotangent.reshape(CH, bins), pltpu.HBM),
        pltpu.with_memory_space_constraint(conv_weight, pltpu.HBM),
        pltpu.with_memory_space_constraint(conv_bias, pltpu.HBM),
    )
    anywhere = pl.BlockSpec(memory_space=pl.ANY)
    output, input_grad, weight_grad, bias_grad = pl.pallas_call(
        finish_kernel,
        out_shape=shapes,
        in_specs=[vmem] * 4,
        out_specs=(anywhere,) * 4,
        scratch_shapes=[pltpu.SemaphoreType.DMA((4, 4))],
        compiler_params=pltpu.CompilerParams(vmem_limit_bytes=4 * 2**20),
        name="finish",
    )(*results)
    return (
        output.reshape(input_map.shape),
        input_grad.reshape(input_map.shape),
        weight_grad,
        bias_grad,
    )


def solution(mesh):
    split = P(None, "pos", "band", None, None)
    return jax.shard_map(
        per_device,
        mesh=mesh,
        in_specs=(split, split, P("pos"), P(), P(), P()),
        out_specs=(split, split, P(), P()),
        check_vma=False,
    )
```

```python
import functools
import math

import jax
import jax.numpy as jnp
from jax import lax
from jax.experimental import pallas as pl
from jax.experimental.pallas import tpu as pltpu
from jax.sharding import PartitionSpec as P

BLOCK = 64
DMAX = 16
LAYERS = 2
BWD = 8
SLOTS = 2
CH = 64
LANES = 128
HALF = 32
WIDE = BLOCK + 2 * DMAX
F32 = jnp.float32
BF16 = jnp.bfloat16
MESH = pl.DeviceIdType.MESH

STEPS = ((1, -1), (0, -1), (0, 1), (-1, 1), (1, 0), (1, -2), (-1, 2), (-1, 0))
ABOVE, RIGHT, LEFT, BELOW, CORNER_ABOVE, FAR_ABOVE, FAR_BELOW, CORNER_BELOW = range(8)
EDGE_LOW = slice(0, DMAX)
CENTRE = slice(DMAX, DMAX + BLOCK)
EDGE_HIGH = slice(DMAX + BLOCK, WIDE)
SQRT_2_PI = math.sqrt(2.0 / math.pi)
CUBIC = 0.044715


def is_low(shape):
    return lax.broadcasted_iota(jnp.int32, shape, len(shape) - 1) < CH


def swap(value):
    return pltpu.roll(value, CH, value.ndim - 1)


def pick(low_value, high_value):
    return jnp.where(is_low(low_value.shape), low_value, high_value)


def merge(first, second):
    return jnp.concatenate([pick(first, swap(second)), pick(swap(first), second)], axis=0)


def both_gelu(value):
    square = value * value
    inner = SQRT_2_PI * (value + CUBIC * (square * value))
    bend = jnp.tanh(inner)
    cdf = 0.5 * (1.0 + bend)
    slope = cdf + 0.5 * value * (1.0 - bend * bend) * (SQRT_2_PI * (1.0 + 3.0 * CUBIC * square))
    return value * cdf, slope


def net_kernel(
    rows_all,
    offsets_all,
    scale,
    width_ref,
    dilation_ref,
    input_hbm,
    cot_hbm,
    weight_hbm,
    bias_hbm,
    out_ref,
    grad_ref,
    weight_grad_ref,
    bias_grad_ref,
    input_ref,
    cot_ref,
    weight_ref,
    bias_ref,
    load_sem,
    frame,
    last,
    term_ref,
    slots,
    shards,
    whole,
    cols,
    slopes,
    slope_low,
    padded,
    grad,
    above,
    below,
    pair_grad,
    w_fwd,
    w_bwd,
    turn,
    send_a,
    send_b,
    send_l,
    send_r,
    send_c,
    recv_a,
    recv_b,
    recv_l,
    recv_r,
    recv_c,
    send_sem,
    recv_sem,
    sum_send,
    sum_recv,
):
    row = lax.axis_index("pos")
    off = lax.axis_index("band")
    loads = [
        pltpu.make_async_copy(source, target, load_sem.at[at])
        for at, (source, target) in enumerate(
            (
                (input_hbm, input_ref),
                (weight_hbm, weight_ref),
                (bias_hbm, bias_ref),
                (cot_hbm, cot_ref),
            )
        )
    ]
    for load in loads:
        load.start()

    def exists(di, do):
        return (row + di >= 0) & (row + di < rows_all) & (off + do >= 0) & (off + do < offsets_all)

    group = whole.shape[0]
    many = shards.shape[0]
    rows = term_ref.shape[1]
    inner = lax.rem(row, group)
    high = lax.div(row, group)
    mine = high * offsets_all + off

    def in_plane(step):
        other = lax.rem(inner + step, group)
        return other, {"pos": high * group + other, "band": off}

    def across(step):
        other = lax.rem(mine + step, many)
        return other, {
            "pos": lax.div(other, offsets_all) * group + inner,
            "band": lax.rem(other, offsets_all),
        }

    kept = jnp.where(
        (off <= width_ref[0]) & (row + off < rows_all), jnp.float32(1.0), jnp.float32(0.0)
    )

    first, final = slice(0, DMAX), slice(BLOCK - DMAX, BLOCK)
    strips = {
        ABOVE: (send_a, recv_a),
        RIGHT: (send_r, recv_r),
        LEFT: (send_l, recv_l),
        BELOW: (send_b, recv_b),
    }
    corners = {
        CORNER_ABOVE: (send_a, final),
        FAR_ABOVE: (send_a, first),
        FAR_BELOW: (send_b, final),
        CORNER_BELOW: (send_b, first),
    }

    def arrival(index, piece):
        if piece in corners:
            return recv_c.at[index, piece - 4]
        return strips[piece][1].at[index]

    def departure(index, piece):
        if piece in strips:
            return strips[piece][0].at[index]
        if index < LAYERS:
            source, part = corners[piece]
            return source.at[index, :, part, :]
        return send_c.at[index - LAYERS, piece - 4]

    for piece in range(8):
        di, do = STEPS[piece]
        for sign, indices in ((1, (0, 1)), (-1, (2, 3))):

            @pl.when(jnp.logical_not(exists(-sign * di, -sign * do)))
            def _():
                for index in indices:
                    there = arrival(index, piece)
                    there[...] = jnp.zeros(there.shape, BF16)

    barrier = pltpu.get_barrier_semaphore()
    count = jnp.int32(0)
    for di, do in STEPS:
        count = count + exists(di, do).astype(jnp.int32)

        @pl.when(exists(di, do))
        def _():
            pl.semaphore_signal(
                barrier,
                inc=1,
                device_id={"pos": row + di, "band": off + do},
                device_id_type=MESH,
            )

    for step in range(1, group):
        pl.semaphore_signal(barrier, inc=1, device_id=in_plane(step)[1], device_id_type=MESH)
    for step in range(1, many):
        pl.semaphore_signal(barrier, inc=1, device_id=across(step)[1], device_id_type=MESH)
    count = count + (group + many - 2)

    def piece_copy(index, piece):
        di, do = STEPS[piece]
        sign = 1 if index < LAYERS else -1
        return pltpu.make_async_remote_copy(
            src_ref=departure(index, piece),
            dst_ref=arrival(index, piece),
            send_sem=send_sem.at[index, piece],
            recv_sem=recv_sem.at[index, piece],
            device_id={"pos": row + sign * di, "band": off + sign * do},
            device_id_type=MESH,
        )

    def send(index, pieces):
        sign = 1 if index < LAYERS else -1
        for piece in pieces:
            di, do = STEPS[piece]

            @pl.when(exists(sign * di, sign * do))
            def _():
                piece_copy(index, piece).start()

    def wait(index, pieces):
        sign = 1 if index < LAYERS else -1
        for piece in pieces:
            di, do = STEPS[piece]

            @pl.when(exists(-sign * di, -sign * do))
            def _():
                piece_copy(index, piece).wait_recv()

    def finish(index):
        sign = 1 if index < LAYERS else -1
        for piece in range(8):
            di, do = STEPS[piece]

            @pl.when(exists(sign * di, sign * do))
            def _():
                piece_copy(index, piece).wait_send()

    def to_tiles(source, k):
        first = source[:, pl.ds(pl.multiple_of(k * LANES, LANES), LANES)].astype(F32)
        second = source[:, pl.ds(pl.multiple_of((k + 16) * LANES, LANES), LANES)].astype(F32)
        return jnp.concatenate([first, second], axis=0).T

    def from_tiles(target, k, first, second):
        turned = jnp.concatenate([first, second], axis=0).T.astype(target.dtype)
        target[:, pl.ds(pl.multiple_of(k * LANES, LANES), LANES)] = turned[:CH]
        target[:, pl.ds(pl.multiple_of((k + 16) * LANES, LANES), LANES)] = turned[CH:]

    def rows_to_cols(load, store):
        @pl.loop(0, 8, unroll=8)
        def _(k):
            turn[pl.ds(pl.multiple_of(k * 64, 64), 64), :] = load(k)

        for t in range(HALF):
            store(t, merge(turn[pl.ds(t, 8, stride=64), :], turn[pl.ds(HALF + t, 8, stride=64), :]))

    def cols_to_rows(load, store):
        @pl.loop(0, HALF, unroll=8)
        def _(t):
            turn[pl.ds(pl.multiple_of(t * 16, 16), 16), :] = load(t)

        for k in range(8):
            store(
                k,
                merge(turn[pl.ds(k, HALF, stride=16), :], turn[pl.ds(8 + k, HALF, stride=16), :]),
            )

    def turn_corner(load, store):
        for k in range(8):
            turn[pl.ds(k * 16, 16), :] = load(k)
        for k in range(8):
            store(k, merge(turn[pl.ds(k, 8, stride=16), :], turn[pl.ds(8 + k, 8, stride=16), :]))

    def pack_forward(index):
        @pl.loop(0, 8, unroll=8)
        def _(k):
            send_a[index, k] = pick(
                swap(frame[32 + k, CENTRE, :]), frame[40 + k, CENTRE, :]
            ).astype(BF16)
            send_b[index, k] = pick(
                frame[16 + k, CENTRE, :], swap(frame[24 + k, CENTRE, :])
            ).astype(BF16)

        @pl.loop(0, HALF, unroll=8)
        def _(t):
            send_l[index, t] = frame[16 + t, slice(64, 80), :].astype(BF16)
            send_r[index, t] = frame[16 + t, slice(16, 32), :].astype(BF16)

    def unpack_sides(index):
        @pl.when(off == 0)
        def _():
            def put_below(k, value):
                recv_b[index, k] = value.astype(BF16)

            cols_to_rows(lambda t: recv_r[index, t].astype(F32), put_below)

        @pl.when(off == 1)
        def _():
            turn_corner(
                lambda k: send_a[index, k, first, :].astype(F32),
                functools.partial(put_down_left, index),
            )

        @pl.when(off > 0)
        def _():
            @pl.loop(0, HALF, unroll=8)
            def _(t):
                frame[16 + t, EDGE_LOW, :] = recv_l[index, t].astype(F32)

        @pl.loop(0, HALF, unroll=8)
        def _(t):
            frame[16 + t, EDGE_HIGH, :] = recv_r[index, t].astype(F32)

    def put_down_left(index, k, value):
        recv_c[index, FAR_BELOW - 4, k] = value.astype(BF16)

    def unpack_forward(index):
        @pl.when(off == 0)
        def _():
            def put_left(t, value):
                frame[16 + t, EDGE_LOW, :] = value

            rows_to_cols(lambda k: recv_a[index, k].astype(F32), put_left)
            turn_corner(
                lambda k: recv_c[index, FAR_ABOVE - 4, k].astype(F32),
                functools.partial(put_down_left, index),
            )

        @pl.loop(0, 8, unroll=8)
        def _(k):
            above, below = (
                jnp.concatenate(
                    [recv_c[index, low - 4, k], strip[index, k], recv_c[index, high - 4, k]], axis=0
                ).astype(F32)
                for low, strip, high in (
                    (CORNER_ABOVE, recv_a, FAR_ABOVE),
                    (FAR_BELOW, recv_b, CORNER_BELOW),
                )
            )
            frame[k] = pick(above, swap(frame[32 + k]))
            frame[8 + k] = swap(pick(frame[40 + k], above))
            frame[48 + k] = swap(pick(below, frame[16 + k]))
            frame[56 + k] = pick(swap(frame[24 + k]), below)

    def prepare_weights(layer):
        weight = weight_ref[layer].astype(F32)
        pieces = [weight[:, j * LANES : (j + 1) * LANES] for j in range(4)]
        pieces.append(
            jnp.concatenate([weight[:, 512:576], jnp.zeros((CH, CH), F32)], axis=1)
        )
        turned = [jnp.concatenate([piece, piece], axis=0).T for piece in pieces]
        for a in range(3):
            for b in range(3):
                for pair, tap in enumerate((3 * a + b, 3 * b + a)):
                    plain = turned[tap // 2][(tap % 2) * CH : (tap % 2) * CH + CH]
                    low = is_low(plain.shape)
                    at = (3 * a + b) * LANES
                    lane = pair * LANES
                    w_fwd[layer, at : at + CH, lane : lane + LANES] = jnp.where(
                        low, plain, 0.0
                    ).astype(BF16)
                    w_fwd[layer, at + CH : at + LANES, lane : lane + LANES] = jnp.where(
                        low, 0.0, plain
                    ).astype(BF16)
                    own = pieces[tap // 2]
                    other = swap(own)
                    if tap % 2:
                        own, other = other, own
                    at = a * 2 * LANES + pair * LANES
                    lane = b * LANES
                    w_bwd[layer, at : at + CH, lane : lane + LANES] = jnp.where(
                        low, own, 0.0
                    ).astype(BF16)
                    w_bwd[layer, at + CH : at + LANES, lane : lane + LANES] = jnp.where(
                        low, 0.0, other
                    ).astype(BF16)

    def shift_columns(layer, tiles, which):
        spread = dilation_ref[layer]

        @pl.loop(*tiles, unroll=4)
        def _(t):
            for b in which:
                cols[layer, t, :, b * LANES : (b + 1) * LANES] = frame[
                    t, pl.ds(DMAX + (b - 1) * spread, BLOCK), :
                ].astype(BF16)

    def taps(layer, t, tiles):
        spread = dilation_ref[layer]
        return [
            cols[layer, pl.ds(DMAX + t + (a - 1) * spread, tiles)].reshape(tiles * BLOCK, 3 * LANES)
            for a in range(3)
        ]

    FWD = 8

    def forward(layer):
        bias = bias_ref[layer : layer + 1, :]
        bias = jnp.concatenate([bias, bias, bias, bias], axis=1)

        @pl.loop(0, HALF // FWD, unroll=4)
        def _(step):
            t = step * FWD
            mixed = (
                jnp.dot(
                    jnp.concatenate(taps(layer, t, FWD), axis=1),
                    w_fwd[layer],
                    preferred_element_type=F32,
                )
                + bias
            )
            value, slope = both_gelu(mixed)
            slopes[layer, pl.ds(t, FWD)] = slope.reshape(FWD, BLOCK, 2 * LANES)
            active = 0.5 * (value[:, :LANES] + value[:, LANES:])
            stored = frame[pl.ds(16 + t, FWD), CENTRE, :].reshape(FWD * BLOCK, LANES)
            result = (kept * (stored + active)).astype(BF16).astype(F32)
            result = result.reshape(FWD, BLOCK, LANES)
            if layer == LAYERS - 1:
                last[pl.ds(t, FWD)] = result
            else:
                frame[pl.ds(16 + t, FWD), CENTRE, :] = result

    loads[0].wait()

    @pl.loop(0, 16, unroll=4)
    def _(k):
        tiles = (to_tiles(input_ref, k) * kept).astype(BF16).astype(F32)
        frame[16 + 2 * k, CENTRE, :] = tiles[:BLOCK]
        frame[17 + 2 * k, CENTRE, :] = tiles[BLOCK:]

    pack_forward(0)
    pl.semaphore_wait(barrier, count)
    send(0, range(8))
    loads[1].wait()
    loads[2].wait()
    for layer in range(LAYERS):
        prepare_weights(layer)
    loads[3].wait()

    @pl.loop(0, 16, unroll=4)
    def _(k):
        tiles = to_tiles(cot_ref, k)
        grad[2 * k] = tiles[:BLOCK]
        grad[2 * k + 1] = tiles[BLOCK:]

    for layer in range(LAYERS):
        wait(layer, (RIGHT, LEFT))
        unpack_sides(layer)
        shift_columns(layer, (16, 48), (1, 2))
        wait(layer, (ABOVE, BELOW, CORNER_ABOVE, FAR_ABOVE, FAR_BELOW, CORNER_BELOW))
        unpack_forward(layer)
        shift_columns(layer, (16, 48), (0,))
        shift_columns(layer, (0, 16), range(3))
        shift_columns(layer, (48, 64), range(3))
        forward(layer)
        if layer < LAYERS - 1:
            pack_forward(layer + 1)
            send(layer + 1, range(8))

    @pl.loop(0, 16, unroll=4)
    def _(t):
        slope_low[t] = jnp.zeros((BLOCK, 2 * LANES), BF16)
        slope_low[48 + t] = jnp.zeros((BLOCK, 2 * LANES), BF16)

    @pl.loop(0, BWD, unroll=4)
    def _(t):
        for b in range(3):
            for slot in range(SLOTS):
                padded[slot, b, t, 0:32, :] = jnp.zeros((32, LANES), F32)
                padded[slot, b, t, 96:128, :] = jnp.zeros((32, LANES), F32)

    def slope_step(layer):
        def step(t, total):
            masked = kept * grad[t]
            grad[t] = masked
            half = 0.5 * masked
            slope = slopes[layer, t] * jnp.concatenate([half, half], axis=1)
            slope_low[16 + t] = slope.astype(BF16)
            return total + jnp.sum(slope.reshape(8, 8, 2 * LANES), axis=0)

        return lax.fori_loop(0, HALF, step, jnp.zeros((8, 2 * LANES), F32), unroll=4)

    def tile_grad(layer, steps):
        spread = dilation_ref[layer]

        def part(step, which, slot):
            first = step * BWD
            held = [
                slope_low[pl.ds(first - (a - 1) * spread, BWD)].reshape(BWD * BLOCK, 2 * LANES)
                for a in which
            ]
            left = held[0] if len(held) == 1 else jnp.concatenate(held, axis=1)
            rows = w_bwd[layer, which[0] * 2 * LANES : (which[-1] + 1) * 2 * LANES, :]
            result = jnp.dot(left, rows, preferred_element_type=F32)
            for b in range(3):
                padded[slot, b, :, 32:96, :] = result[:, b * LANES : (b + 1) * LANES].reshape(
                    BWD, BLOCK, LANES
                )
            for at in range(BWD):
                total = None
                for b in range(3):
                    term = padded[slot, b, at, pl.ds(DMAX - (b - 1) * spread, WIDE), :]
                    total = term if total is None else total + term
                frame[first + at] = total

        for count, step in enumerate(steps):
            at = step * BWD
            which = (0,) if at < 16 else (2,) if at >= 48 else (0, 1, 2)
            part(step, which, count % SLOTS)

    def pack_outer(index):
        @pl.loop(0, 8, unroll=8)
        def _(k):
            above[k] = pick(frame[k], swap(frame[8 + k]))
            below[k] = pick(swap(frame[48 + k]), frame[56 + k])

        @pl.when(off == 0)
        def _():
            def add_far(k, value):
                above[k, EDGE_HIGH, :] = above[k, EDGE_HIGH, :] + value

            turn_corner(lambda k: below[k, EDGE_LOW, :], add_far)

        @pl.loop(0, 8, unroll=8)
        def _(k):
            send_b[index, k] = below[k, CENTRE, :].astype(BF16)
            for piece, strip, part in (
                (CORNER_ABOVE, above, EDGE_LOW),
                (FAR_ABOVE, above, EDGE_HIGH),
                (FAR_BELOW, below, EDGE_LOW),
                (CORNER_BELOW, below, EDGE_HIGH),
            ):
                send_c[index - LAYERS, piece - 4, k] = strip[k, part, :].astype(BF16)

        @pl.when(off > 0)
        def _():
            send_above(index)

        send(index, (BELOW, CORNER_ABOVE, FAR_ABOVE, FAR_BELOW, CORNER_BELOW))

    def send_above(index):
        @pl.loop(0, 8, unroll=8)
        def _(k):
            send_a[index, k] = above[k, CENTRE, :].astype(BF16)

        send(index, (ABOVE,))

    def pack_centre(index):
        @pl.when(off == 0)
        def _():
            @pl.loop(0, 8, unroll=8)
            def _(k):
                share(k, EDGE_LOW)

            def add_above(k, value):
                above[k, CENTRE, :] = above[k, CENTRE, :] + value

            cols_to_rows(lambda t: frame[16 + t, EDGE_LOW, :], add_above)
            send_above(index)

            @pl.loop(0, 8, unroll=8)
            def _(k):
                share(k, slice(DMAX, WIDE))

            def add_right(t, value):
                frame[16 + t, EDGE_HIGH, :] = frame[16 + t, EDGE_HIGH, :] + value

            rows_to_cols(lambda k: below[k, CENTRE, :], add_right)

        @pl.when(off > 0)
        def _():
            @pl.loop(0, 8, unroll=8)
            def _(k):
                share(k, slice(0, WIDE))

        @pl.when(off == 1)
        def _():
            def add_own(k, value):
                low = is_low(value.shape)
                at = slice(16, 32)
                frame[32 + k, at, :] = frame[32 + k, at, :] + jnp.where(low, 0.0, swap(value))
                frame[40 + k, at, :] = frame[40 + k, at, :] + jnp.where(low, 0.0, value)

            turn_corner(lambda k: below[k, EDGE_LOW, :], add_own)

        @pl.loop(0, HALF, unroll=8)
        def _(t):
            send_l[index, t] = frame[16 + t, EDGE_LOW, :].astype(BF16)
            send_r[index, t] = frame[16 + t, EDGE_HIGH, :].astype(BF16)

        send(index, (LEFT, RIGHT))

    def share(k, part):
        def add(to, value, keep_low):
            low = is_low(value.shape)
            moved = swap(value)
            moved = jnp.where(low, moved, 0.0) if keep_low else jnp.where(low, 0.0, moved)
            frame[to, part, :] = frame[to, part, :] + moved

        add(16 + k, frame[48 + k, part, :], False)
        add(24 + k, frame[56 + k, part, :], False)
        add(32 + k, frame[k, part, :], True)
        add(40 + k, frame[8 + k, part, :], True)

    def unpack_back_sides(index):
        @pl.loop(0, HALF, unroll=8)
        def _(t):
            total = grad[t] + frame[16 + t, CENTRE, :]
            right = recv_r[index, t].astype(F32)
            left = recv_l[index, t].astype(F32)
            edge = jnp.concatenate([right, jnp.zeros((32, LANES), F32), left], axis=0)
            grad[t] = total + edge

    def unpack_backward(index):
        @pl.loop(0, 8, unroll=8)
        def _(k):
            def strip(ref, low, high):
                corners = [
                    recv_c[index, high - 4, k].astype(F32),
                    jnp.zeros((32, LANES), F32),
                    recv_c[index, low - 4, k].astype(F32),
                ]
                return ref[index, k].astype(F32) + jnp.concatenate(corners, axis=0)

            top = strip(recv_b, FAR_BELOW, CORNER_BELOW)
            bottom = strip(recv_a, CORNER_ABOVE, FAR_ABOVE)
            low = is_low(top.shape)
            grad[k] = grad[k] + jnp.where(low, top, 0.0)
            grad[8 + k] = grad[8 + k] + jnp.where(low, swap(top), 0.0)
            grad[16 + k] = grad[16 + k] + jnp.where(low, 0.0, swap(bottom))
            grad[24 + k] = grad[24 + k] + jnp.where(low, 0.0, bottom)

    def weight_terms(layer, bias_rows):
        left = slope_low[16:48].reshape(HALF * BLOCK, 2 * LANES)
        for a, part in enumerate(taps(layer, 0, HALF)):
            lane = a * 3 * LANES
            pair_grad[:, lane : lane + 3 * LANES] = lax.dot_general(
                left, part, (((0,), (0,)), ((), ())), preferred_element_type=F32
            )

        def tap_part(tap, half):
            turned = 3 * (tap % 3) + tap // 3
            first = pair_grad[half * CH : half * CH + CH, tap * LANES : (tap + 1) * LANES]
            at = LANES + half * CH
            second = pair_grad[at : at + CH, turned * LANES : (turned + 1) * LANES]
            return first + second

        for j in range(5):
            low_part = tap_part(2 * j, 0) + swap(tap_part(2 * j, 1))
            if j < 4:
                high_part = tap_part(2 * j + 1, 1) + swap(tap_part(2 * j + 1, 0))
            else:
                total = jnp.sum(bias_rows, axis=0, keepdims=True)
                total = total[:, :LANES] + total[:, LANES:]
                total = total + swap(total)
                high_part = jnp.broadcast_to(total, (LANES, LANES)).T[:CH]
            part = pick(low_part, high_part).astype(BF16)
            for at in range(CH // rows):
                term_ref[layer * (CH // rows) + at, :, j * LANES : (j + 1) * LANES] = part[
                    at * rows : (at + 1) * rows
                ]

    def sum_copy(stage, step):
        if stage == 1:
            other, device = across(step)
            source, target = shards.at[mine], shards.at[mine]
        else:
            other, device = in_plane(step)
            if stage == 0:
                source, target = term_ref.at[other], slots.at[step]
            else:
                source, target = whole.at[inner], whole.at[inner]
        return pltpu.make_async_remote_copy(
            src_ref=source,
            dst_ref=target,
            send_sem=sum_send.at[stage, step],
            recv_sem=sum_recv.at[stage, step],
            device_id=device,
            device_id_type=MESH,
        )

    def peers(stage):
        return range(1, many if stage == 1 else group)

    def sum_start(stage):
        if stage == 1:
            total = term_ref[inner].astype(F32)
            for step in peers(0):
                sum_copy(0, step).wait_recv()
                total = total + slots[step].astype(F32)
            shards[mine] = total.astype(BF16)
        elif stage == 2:
            for step in peers(1):
                sum_copy(1, step).wait_recv()
            total = shards[0].astype(F32)
            for at in range(1, many):
                total = total + shards[at].astype(F32)
            whole[inner] = (total * scale).astype(BF16)
        for step in peers(stage):
            sum_copy(stage, step).start()

    def sum_end():
        for step in peers(2):
            sum_copy(2, step).wait_recv()
        total = jnp.concatenate([whole[at].astype(F32) for at in range(group)], axis=0)
        for layer in range(LAYERS):
            weight_grad_ref[layer] = total[layer * CH : (layer + 1) * CH, :576]
        column = total[:, 4 * LANES :].T[CH : CH + 1]
        bias_grad_ref[0:1, :] = column[:, :CH]
        bias_grad_ref[1:2, :] = swap(column)[:, :CH]
        for stage in range(3):
            for step in peers(stage):
                sum_copy(stage, step).wait_send()

    for layer in reversed(range(LAYERS)):
        index = 2 * LAYERS - 1 - layer
        bias_rows = slope_step(layer)
        if layer == 0:
            weight_terms(layer, bias_rows)
            sum_start(0)
        edge = 64 // BWD // 4
        tile_grad(layer, (*range(edge), *range(3 * edge, 4 * edge)))
        pack_outer(index)
        tile_grad(layer, range(edge, 3 * edge))
        pack_centre(index)
        if layer == 0:
            sum_start(1)
            sum_start(2)
        else:
            weight_terms(layer, bias_rows)

            @pl.loop(0, 16, unroll=4)
            def _(k):
                from_tiles(out_ref, k, last[2 * k], last[2 * k + 1])

        wait(index, (RIGHT, LEFT))
        unpack_back_sides(index)
        wait(index, (ABOVE, BELOW, CORNER_ABOVE, FAR_ABOVE, FAR_BELOW, CORNER_BELOW))
        unpack_backward(index)

    @pl.loop(0, 16, unroll=4)
    def _(k):
        from_tiles(grad_ref, k, kept * grad[2 * k], kept * grad[2 * k + 1])

    sum_end()
    for index in range(2 * LAYERS):
        finish(index)


def finish_kernel(*refs):
    sources, targets, sems = refs[:4], refs[4:8], refs[8]
    copies = []
    for at, (source, target) in enumerate(zip(sources, targets)):
        parts = 4 if at < 2 else 1
        for part in range(parts):
            if parts > 1:
                lanes = source.shape[1] // parts
                span = pl.ds(part * lanes, lanes)
                pair = source.at[:, span], target.at[:, span]
            else:
                pair = source, target
            copies.append(pltpu.make_async_copy(*pair, sems.at[at, part]))
            copies[-1].start()
    for copy in copies:
        copy.wait()


def per_device(input_map, cotangent, band_width, dilation, conv_weight, conv_bias):
    rows_all = lax.axis_size("pos")
    offsets_all = lax.axis_size("band")
    bins = BLOCK * BLOCK
    vmem = pl.BlockSpec(memory_space=pltpu.VMEM)
    smem = pl.BlockSpec(memory_space=pltpu.SMEM)
    hbm = pl.BlockSpec(memory_space=pltpu.HBM)
    group = 16 if rows_all % 16 == 0 else rows_all
    many = rows_all // group * offsets_all
    shard = (LAYERS * CH // group, 5 * LANES)
    scale = 1.0 / (BLOCK * math.sqrt(input_map.shape[0] * rows_all * offsets_all))
    shapes = (
        jax.ShapeDtypeStruct((CH, bins), BF16),
        jax.ShapeDtypeStruct((CH, bins), F32),
        jax.ShapeDtypeStruct((LAYERS, CH, 576), F32),
        jax.ShapeDtypeStruct((LAYERS, CH), F32),
    )
    results = pl.pallas_call(
        functools.partial(net_kernel, rows_all, offsets_all, scale),
        out_shape=shapes,
        in_specs=[smem, smem, hbm, hbm, hbm, hbm],
        out_specs=(vmem, vmem, vmem, vmem),
        scratch_shapes=[
            pltpu.VMEM((CH, bins), BF16),
            pltpu.VMEM((CH, bins), BF16),
            pltpu.VMEM((LAYERS, CH, 576), BF16),
            pltpu.VMEM((LAYERS, CH), F32),
            pltpu.SemaphoreType.DMA((4,)),
            pltpu.VMEM((64, WIDE, LANES), F32),
            pltpu.VMEM((HALF, BLOCK, LANES), F32),
            pltpu.VMEM((group, *shard), BF16),
            pltpu.VMEM((group, *shard), BF16),
            pltpu.VMEM((many, *shard), BF16),
            pltpu.VMEM((group, *shard), BF16),
            pltpu.VMEM((LAYERS, 64, BLOCK, 3 * LANES), BF16),
            pltpu.VMEM((LAYERS, HALF, BLOCK, 2 * LANES), F32),
            pltpu.VMEM((64, BLOCK, 2 * LANES), BF16),
            pltpu.VMEM((SLOTS, 3, BWD, 128, LANES), F32),
            pltpu.VMEM((HALF, BLOCK, LANES), F32),
            pltpu.VMEM((8, WIDE, LANES), F32),
            pltpu.VMEM((8, WIDE, LANES), F32),
            pltpu.VMEM((2 * LANES, 9 * LANES), F32),
            pltpu.VMEM((LAYERS, 9 * LANES, 2 * LANES), BF16),
            pltpu.VMEM((LAYERS, 6 * LANES, 3 * LANES), BF16),
            pltpu.VMEM((512, LANES), F32),
            pltpu.VMEM((4, 8, BLOCK, LANES), BF16),
            pltpu.VMEM((4, 8, BLOCK, LANES), BF16),
            pltpu.VMEM((4, HALF, DMAX, LANES), BF16),
            pltpu.VMEM((4, HALF, DMAX, LANES), BF16),
            pltpu.VMEM((2, 4, 8, DMAX, LANES), BF16),
            pltpu.VMEM((4, 8, BLOCK, LANES), BF16),
            pltpu.VMEM((4, 8, BLOCK, LANES), BF16),
            pltpu.VMEM((4, HALF, DMAX, LANES), BF16),
            pltpu.VMEM((4, HALF, DMAX, LANES), BF16),
            pltpu.VMEM((4, 4, 8, DMAX, LANES), BF16),
            pltpu.SemaphoreType.DMA((4, 8)),
            pltpu.SemaphoreType.DMA((4, 8)),
            pltpu.SemaphoreType.DMA((3, 16)),
            pltpu.SemaphoreType.DMA((3, 16)),
        ],
        compiler_params=pltpu.CompilerParams(
            collective_id=0, has_side_effects=True, vmem_limit_bytes=46 * 2**20
        ),
        name="net",
    )(
        band_width,
        pltpu.with_memory_space_constraint(dilation, pltpu.HBM),
        pltpu.with_memory_space_constraint(input_map.reshape(CH, bins), pltpu.HBM),
        pltpu.with_memory_space_constraint(cotangent.reshape(CH, bins), pltpu.HBM),
        pltpu.with_memory_space_constraint(conv_weight, pltpu.HBM),
        pltpu.with_memory_space_constraint(conv_bias, pltpu.HBM),
    )
    anywhere = pl.BlockSpec(memory_space=pl.ANY)
    output, input_grad, weight_grad, bias_grad = pl.pallas_call(
        finish_kernel,
        out_shape=shapes,
        in_specs=[vmem] * 4,
        out_specs=(anywhere,) * 4,
        scratch_shapes=[pltpu.SemaphoreType.DMA((4, 4))],
        compiler_params=pltpu.CompilerParams(vmem_limit_bytes=4 * 2**20),
        name="finish",
    )(*results)
    return (
        output.reshape(input_map.shape),
        input_grad.reshape(input_map.shape),
        weight_grad,
        bias_grad,
    )


def solution(mesh):
    split = P(None, "pos", "band", None, None)
    return jax.shard_map(
        per_device,
        mesh=mesh,
        in_specs=(split, split, P("pos"), P(), P(), P()),
        out_specs=(split, split, P(), P()),
        check_vma=False,
    )
```

```python
import functools
import math

import jax
import jax.numpy as jnp
from jax import lax
from jax.experimental import pallas as pl
from jax.experimental.pallas import tpu as pltpu
from jax.sharding import PartitionSpec as P

BLOCK = 64
DMAX = 16
LAYERS = 2
BWD = 8
SLOTS = 2
CH = 64
LANES = 128
HALF = 32
WIDE = BLOCK + 2 * DMAX
F32 = jnp.float32
BF16 = jnp.bfloat16
MESH = pl.DeviceIdType.MESH

STEPS = ((1, -1), (0, -1), (0, 1), (-1, 1), (1, 0), (1, -2), (-1, 2), (-1, 0))
ABOVE, RIGHT, LEFT, BELOW, CORNER_ABOVE, FAR_ABOVE, FAR_BELOW, CORNER_BELOW = range(8)
EDGE_LOW = slice(0, DMAX)
CENTRE = slice(DMAX, DMAX + BLOCK)
EDGE_HIGH = slice(DMAX + BLOCK, WIDE)
SQRT_2_PI = math.sqrt(2.0 / math.pi)
CUBIC = 0.044715


def is_low(shape):
    return lax.broadcasted_iota(jnp.int32, shape, len(shape) - 1) < CH


def swap(value):
    return pltpu.roll(value, CH, value.ndim - 1)


def pick(low_value, high_value):
    return jnp.where(is_low(low_value.shape), low_value, high_value)


def merge(first, second):
    return jnp.concatenate([pick(first, swap(second)), pick(swap(first), second)], axis=0)


def both_gelu(value):
    square = value * value
    inner = SQRT_2_PI * (value + CUBIC * (square * value))
    bend = jnp.tanh(inner)
    cdf = 0.5 * (1.0 + bend)
    slope = cdf + 0.5 * value * (1.0 - bend * bend) * (SQRT_2_PI * (1.0 + 3.0 * CUBIC * square))
    return value * cdf, slope


def net_kernel(
    rows_all,
    offsets_all,
    scale,
    width_ref,
    dilation_ref,
    input_hbm,
    cot_hbm,
    weight_hbm,
    bias_hbm,
    out_ref,
    grad_ref,
    weight_grad_ref,
    bias_grad_ref,
    input_ref,
    cot_ref,
    weight_ref,
    bias_ref,
    load_sem,
    frame,
    last,
    term_ref,
    slots,
    shards,
    whole,
    cols,
    slopes,
    slope_low,
    padded,
    grad,
    above,
    below,
    pair_grad,
    w_fwd,
    w_bwd,
    turn,
    send_a,
    send_b,
    send_l,
    send_r,
    send_c,
    recv_a,
    recv_b,
    recv_l,
    recv_r,
    recv_c,
    send_sem,
    recv_sem,
    sum_send,
    sum_recv,
):
    row = lax.axis_index("pos")
    off = lax.axis_index("band")
    loads = [
        pltpu.make_async_copy(source, target, load_sem.at[at])
        for at, (source, target) in enumerate(
            (
                (input_hbm, input_ref),
                (weight_hbm, weight_ref),
                (bias_hbm, bias_ref),
                (cot_hbm, cot_ref),
            )
        )
    ]
    for load in loads:
        load.start()

    def exists(di, do):
        return (row + di >= 0) & (row + di < rows_all) & (off + do >= 0) & (off + do < offsets_all)

    group = whole.shape[0]
    many = shards.shape[0]
    rows = term_ref.shape[1]
    inner = lax.rem(row, group)
    high = lax.div(row, group)
    mine = high * offsets_all + off

    def in_plane(step):
        other = lax.rem(inner + step, group)
        return other, {"pos": high * group + other, "band": off}

    def across(step):
        other = lax.rem(mine + step, many)
        return other, {
            "pos": lax.div(other, offsets_all) * group + inner,
            "band": lax.rem(other, offsets_all),
        }

    kept = jnp.where(
        (off <= width_ref[0]) & (row + off < rows_all), jnp.float32(1.0), jnp.float32(0.0)
    )

    first, final = slice(0, DMAX), slice(BLOCK - DMAX, BLOCK)
    strips = {
        ABOVE: (send_a, recv_a),
        RIGHT: (send_r, recv_r),
        LEFT: (send_l, recv_l),
        BELOW: (send_b, recv_b),
    }
    corners = {
        CORNER_ABOVE: (send_a, final),
        FAR_ABOVE: (send_a, first),
        FAR_BELOW: (send_b, final),
        CORNER_BELOW: (send_b, first),
    }

    def arrival(index, piece):
        if piece in corners:
            return recv_c.at[index, piece - 4]
        return strips[piece][1].at[index]

    def departure(index, piece):
        if piece in strips:
            return strips[piece][0].at[index]
        if index < LAYERS:
            source, part = corners[piece]
            return source.at[index, :, part, :]
        return send_c.at[index - LAYERS, piece - 4]

    for piece in range(8):
        di, do = STEPS[piece]
        for sign, indices in ((1, (0, 1)), (-1, (2, 3))):

            @pl.when(jnp.logical_not(exists(-sign * di, -sign * do)))
            def _():
                for index in indices:
                    there = arrival(index, piece)
                    there[...] = jnp.zeros(there.shape, BF16)

    barrier = pltpu.get_barrier_semaphore()
    count = jnp.int32(0)
    for di, do in STEPS:
        count = count + exists(di, do).astype(jnp.int32)

        @pl.when(exists(di, do))
        def _():
            pl.semaphore_signal(
                barrier,
                inc=1,
                device_id={"pos": row + di, "band": off + do},
                device_id_type=MESH,
            )

    for step in range(1, group):
        pl.semaphore_signal(barrier, inc=1, device_id=in_plane(step)[1], device_id_type=MESH)
    for step in range(1, many):
        pl.semaphore_signal(barrier, inc=1, device_id=across(step)[1], device_id_type=MESH)
    count = count + (group + many - 2)

    def piece_copy(index, piece):
        di, do = STEPS[piece]
        sign = 1 if index < LAYERS else -1
        return pltpu.make_async_remote_copy(
            src_ref=departure(index, piece),
            dst_ref=arrival(index, piece),
            send_sem=send_sem.at[index, piece],
            recv_sem=recv_sem.at[index, piece],
            device_id={"pos": row + sign * di, "band": off + sign * do},
            device_id_type=MESH,
        )

    def send(index, pieces):
        sign = 1 if index < LAYERS else -1
        for piece in pieces:
            di, do = STEPS[piece]

            @pl.when(exists(sign * di, sign * do))
            def _():
                piece_copy(index, piece).start()

    def wait(index, pieces):
        sign = 1 if index < LAYERS else -1
        for piece in pieces:
            di, do = STEPS[piece]

            @pl.when(exists(-sign * di, -sign * do))
            def _():
                piece_copy(index, piece).wait_recv()

    def finish(index):
        sign = 1 if index < LAYERS else -1
        for piece in range(8):
            di, do = STEPS[piece]

            @pl.when(exists(sign * di, sign * do))
            def _():
                piece_copy(index, piece).wait_send()

    def to_tiles(source, k):
        first = source[:, pl.ds(pl.multiple_of(k * LANES, LANES), LANES)].astype(F32)
        second = source[:, pl.ds(pl.multiple_of((k + 16) * LANES, LANES), LANES)].astype(F32)
        return jnp.concatenate([first, second], axis=0).T

    def from_tiles(target, k, first, second):
        turned = jnp.concatenate([first, second], axis=0).T.astype(target.dtype)
        target[:, pl.ds(pl.multiple_of(k * LANES, LANES), LANES)] = turned[:CH]
        target[:, pl.ds(pl.multiple_of((k + 16) * LANES, LANES), LANES)] = turned[CH:]

    def rows_to_cols(load, store):
        @pl.loop(0, 8, unroll=8)
        def _(k):
            turn[pl.ds(pl.multiple_of(k * 64, 64), 64), :] = load(k)

        for t in range(HALF):
            store(t, merge(turn[pl.ds(t, 8, stride=64), :], turn[pl.ds(HALF + t, 8, stride=64), :]))

    def cols_to_rows(load, store):
        @pl.loop(0, HALF, unroll=8)
        def _(t):
            turn[pl.ds(pl.multiple_of(t * 16, 16), 16), :] = load(t)

        for k in range(8):
            store(
                k,
                merge(turn[pl.ds(k, HALF, stride=16), :], turn[pl.ds(8 + k, HALF, stride=16), :]),
            )

    def turn_corner(load, store):
        for k in range(8):
            turn[pl.ds(k * 16, 16), :] = load(k)
        for k in range(8):
            store(k, merge(turn[pl.ds(k, 8, stride=16), :], turn[pl.ds(8 + k, 8, stride=16), :]))

    def pack_forward(index):
        @pl.loop(0, 8, unroll=8)
        def _(k):
            send_a[index, k] = pick(
                swap(frame[32 + k, CENTRE, :]), frame[40 + k, CENTRE, :]
            ).astype(BF16)
            send_b[index, k] = pick(
                frame[16 + k, CENTRE, :], swap(frame[24 + k, CENTRE, :])
            ).astype(BF16)

        @pl.loop(0, HALF, unroll=8)
        def _(t):
            send_l[index, t] = frame[16 + t, slice(64, 80), :].astype(BF16)
            send_r[index, t] = frame[16 + t, slice(16, 32), :].astype(BF16)

    def unpack_sides(index):
        @pl.when(off == 0)
        def _():
            def put_below(k, value):
                recv_b[index, k] = value.astype(BF16)

            cols_to_rows(lambda t: recv_r[index, t].astype(F32), put_below)

        @pl.when(off == 1)
        def _():
            turn_corner(
                lambda k: send_a[index, k, first, :].astype(F32),
                functools.partial(put_down_left, index),
            )

        @pl.when(off > 0)
        def _():
            @pl.loop(0, HALF, unroll=8)
            def _(t):
                frame[16 + t, EDGE_LOW, :] = recv_l[index, t].astype(F32)

        @pl.loop(0, HALF, unroll=8)
        def _(t):
            frame[16 + t, EDGE_HIGH, :] = recv_r[index, t].astype(F32)

    def put_down_left(index, k, value):
        recv_c[index, FAR_BELOW - 4, k] = value.astype(BF16)

    def unpack_forward(index):
        @pl.when(off == 0)
        def _():
            def put_left(t, value):
                frame[16 + t, EDGE_LOW, :] = value

            rows_to_cols(lambda k: recv_a[index, k].astype(F32), put_left)
            turn_corner(
                lambda k: recv_c[index, FAR_ABOVE - 4, k].astype(F32),
                functools.partial(put_down_left, index),
            )

        @pl.loop(0, 8, unroll=8)
        def _(k):
            above, below = (
                jnp.concatenate(
                    [recv_c[index, low - 4, k], strip[index, k], recv_c[index, high - 4, k]], axis=0
                ).astype(F32)
                for low, strip, high in (
                    (CORNER_ABOVE, recv_a, FAR_ABOVE),
                    (FAR_BELOW, recv_b, CORNER_BELOW),
                )
            )
            frame[k] = pick(above, swap(frame[32 + k]))
            frame[8 + k] = swap(pick(frame[40 + k], above))
            frame[48 + k] = swap(pick(below, frame[16 + k]))
            frame[56 + k] = pick(swap(frame[24 + k]), below)

    def prepare_weights(layer):
        weight = weight_ref[layer].astype(F32)
        pieces = [weight[:, j * LANES : (j + 1) * LANES] for j in range(4)]
        pieces.append(
            jnp.concatenate([weight[:, 512:576], jnp.zeros((CH, CH), F32)], axis=1)
        )
        turned = [jnp.concatenate([piece, piece], axis=0).T for piece in pieces]
        for a in range(3):
            for b in range(3):
                for pair, tap in enumerate((3 * a + b, 3 * b + a)):
                    plain = turned[tap // 2][(tap % 2) * CH : (tap % 2) * CH + CH]
                    low = is_low(plain.shape)
                    at = (3 * a + b) * LANES
                    lane = pair * LANES
                    w_fwd[layer, at : at + CH, lane : lane + LANES] = jnp.where(
                        low, plain, 0.0
                    ).astype(BF16)
                    w_fwd[layer, at + CH : at + LANES, lane : lane + LANES] = jnp.where(
                        low, 0.0, plain
                    ).astype(BF16)
                    own = pieces[tap // 2]
                    other = swap(own)
                    if tap % 2:
                        own, other = other, own
                    at = a * 2 * LANES + pair * LANES
                    lane = b * LANES
                    w_bwd[layer, at : at + CH, lane : lane + LANES] = jnp.where(
                        low, own, 0.0
                    ).astype(BF16)
                    w_bwd[layer, at + CH : at + LANES, lane : lane + LANES] = jnp.where(
                        low, 0.0, other
                    ).astype(BF16)

    def shift_columns(layer, tiles, which):
        spread = dilation_ref[layer]

        @pl.loop(*tiles, unroll=4)
        def _(t):
            for b in which:
                cols[layer, t, :, b * LANES : (b + 1) * LANES] = frame[
                    t, pl.ds(DMAX + (b - 1) * spread, BLOCK), :
                ].astype(BF16)

    def taps(layer, t, tiles):
        spread = dilation_ref[layer]
        return [
            cols[layer, pl.ds(DMAX + t + (a - 1) * spread, tiles)].reshape(tiles * BLOCK, 3 * LANES)
            for a in range(3)
        ]

    FWD = 8

    def forward(layer):
        bias = bias_ref[layer : layer + 1, :]
        bias = jnp.concatenate([bias, bias, bias, bias], axis=1)

        @pl.loop(0, HALF // FWD, unroll=4)
        def _(step):
            t = step * FWD
            mixed = (
                jnp.dot(
                    jnp.concatenate(taps(layer, t, FWD), axis=1),
                    w_fwd[layer],
                    preferred_element_type=F32,
                )
                + bias
            )
            value, slope = both_gelu(mixed)
            slopes[layer, pl.ds(t, FWD)] = slope.reshape(FWD, BLOCK, 2 * LANES)
            active = 0.5 * (value[:, :LANES] + value[:, LANES:])
            stored = frame[pl.ds(16 + t, FWD), CENTRE, :].reshape(FWD * BLOCK, LANES)
            result = (kept * (stored + active)).astype(BF16).astype(F32)
            result = result.reshape(FWD, BLOCK, LANES)
            if layer == LAYERS - 1:
                last[pl.ds(t, FWD)] = result
            else:
                frame[pl.ds(16 + t, FWD), CENTRE, :] = result

    loads[0].wait()

    @pl.loop(0, 16, unroll=4)
    def _(k):
        tiles = (to_tiles(input_ref, k) * kept).astype(BF16).astype(F32)
        frame[16 + 2 * k, CENTRE, :] = tiles[:BLOCK]
        frame[17 + 2 * k, CENTRE, :] = tiles[BLOCK:]

    pack_forward(0)
    pl.semaphore_wait(barrier, count)
    send(0, range(8))
    loads[1].wait()
    loads[2].wait()
    for layer in range(LAYERS):
        prepare_weights(layer)
    loads[3].wait()

    @pl.loop(0, 16, unroll=4)
    def _(k):
        tiles = to_tiles(cot_ref, k)
        grad[2 * k] = tiles[:BLOCK]
        grad[2 * k + 1] = tiles[BLOCK:]

    for layer in range(LAYERS):
        wait(layer, (RIGHT, LEFT))
        unpack_sides(layer)
        shift_columns(layer, (16, 48), (1, 2))
        wait(layer, (ABOVE, BELOW, CORNER_ABOVE, FAR_ABOVE, FAR_BELOW, CORNER_BELOW))
        unpack_forward(layer)
        shift_columns(layer, (16, 48), (0,))
        shift_columns(layer, (0, 16), range(3))
        shift_columns(layer, (48, 64), range(3))
        forward(layer)
        if layer < LAYERS - 1:
            pack_forward(layer + 1)
            send(layer + 1, range(8))

    @pl.loop(0, 16, unroll=4)
    def _(t):
        slope_low[t] = jnp.zeros((BLOCK, 2 * LANES), BF16)
        slope_low[48 + t] = jnp.zeros((BLOCK, 2 * LANES), BF16)

    @pl.loop(0, BWD, unroll=4)
    def _(t):
        for b in range(3):
            for slot in range(SLOTS):
                padded[slot, b, t, 0:32, :] = jnp.zeros((32, LANES), F32)
                padded[slot, b, t, 96:128, :] = jnp.zeros((32, LANES), F32)

    def slope_step(layer):
        def step(t, total):
            masked = kept * grad[t]
            grad[t] = masked
            half = 0.5 * masked
            slope = slopes[layer, t] * jnp.concatenate([half, half], axis=1)
            slope_low[16 + t] = slope.astype(BF16)
            return total + jnp.sum(slope.reshape(8, 8, 2 * LANES), axis=0)

        return lax.fori_loop(0, HALF, step, jnp.zeros((8, 2 * LANES), F32), unroll=4)

    def tile_grad(layer, steps):
        spread = dilation_ref[layer]

        def part(step, which, slot):
            first = step * BWD
            held = [
                slope_low[pl.ds(first - (a - 1) * spread, BWD)].reshape(BWD * BLOCK, 2 * LANES)
                for a in which
            ]
            left = held[0] if len(held) == 1 else jnp.concatenate(held, axis=1)
            rows = w_bwd[layer, which[0] * 2 * LANES : (which[-1] + 1) * 2 * LANES, :]
            result = jnp.dot(left, rows, preferred_element_type=F32)
            for b in range(3):
                padded[slot, b, :, 32:96, :] = result[:, b * LANES : (b + 1) * LANES].reshape(
                    BWD, BLOCK, LANES
                )
            for at in range(BWD):
                total = None
                for b in range(3):
                    term = padded[slot, b, at, pl.ds(DMAX - (b - 1) * spread, WIDE), :]
                    total = term if total is None else total + term
                frame[first + at] = total

        for count, step in enumerate(steps):
            at = step * BWD
            which = (0,) if at < 16 else (2,) if at >= 48 else (0, 1, 2)
            part(step, which, count % SLOTS)

    def pack_outer(index):
        @pl.loop(0, 8, unroll=8)
        def _(k):
            above[k] = pick(frame[k], swap(frame[8 + k]))
            below[k] = pick(swap(frame[48 + k]), frame[56 + k])

        @pl.when(off == 0)
        def _():
            def add_far(k, value):
                above[k, EDGE_HIGH, :] = above[k, EDGE_HIGH, :] + value

            turn_corner(lambda k: below[k, EDGE_LOW, :], add_far)

        @pl.loop(0, 8, unroll=8)
        def _(k):
            send_b[index, k] = below[k, CENTRE, :].astype(BF16)
            for piece, strip, part in (
                (CORNER_ABOVE, above, EDGE_LOW),
                (FAR_ABOVE, above, EDGE_HIGH),
                (FAR_BELOW, below, EDGE_LOW),
                (CORNER_BELOW, below, EDGE_HIGH),
            ):
                send_c[index - LAYERS, piece - 4, k] = strip[k, part, :].astype(BF16)

        @pl.when(off > 0)
        def _():
            send_above(index)

        send(index, (BELOW, CORNER_ABOVE, FAR_ABOVE, FAR_BELOW, CORNER_BELOW))

    def send_above(index):
        @pl.loop(0, 8, unroll=8)
        def _(k):
            send_a[index, k] = above[k, CENTRE, :].astype(BF16)

        send(index, (ABOVE,))

    def pack_centre(index):
        @pl.when(off == 0)
        def _():
            @pl.loop(0, 8, unroll=8)
            def _(k):
                share(k, EDGE_LOW)

            def add_above(k, value):
                above[k, CENTRE, :] = above[k, CENTRE, :] + value

            cols_to_rows(lambda t: frame[16 + t, EDGE_LOW, :], add_above)
            send_above(index)

            @pl.loop(0, 8, unroll=8)
            def _(k):
                share(k, slice(DMAX, WIDE))

            def add_right(t, value):
                frame[16 + t, EDGE_HIGH, :] = frame[16 + t, EDGE_HIGH, :] + value

            rows_to_cols(lambda k: below[k, CENTRE, :], add_right)

        @pl.when(off > 0)
        def _():
            @pl.loop(0, 8, unroll=8)
            def _(k):
                share(k, slice(0, WIDE))

        @pl.when(off == 1)
        def _():
            def add_own(k, value):
                low = is_low(value.shape)
                at = slice(16, 32)
                frame[32 + k, at, :] = frame[32 + k, at, :] + jnp.where(low, 0.0, swap(value))
                frame[40 + k, at, :] = frame[40 + k, at, :] + jnp.where(low, 0.0, value)

            turn_corner(lambda k: below[k, EDGE_LOW, :], add_own)

        @pl.loop(0, HALF, unroll=8)
        def _(t):
            send_l[index, t] = frame[16 + t, EDGE_LOW, :].astype(BF16)
            send_r[index, t] = frame[16 + t, EDGE_HIGH, :].astype(BF16)

        send(index, (LEFT, RIGHT))

    def share(k, part):
        def add(to, value, keep_low):
            low = is_low(value.shape)
            moved = swap(value)
            moved = jnp.where(low, moved, 0.0) if keep_low else jnp.where(low, 0.0, moved)
            frame[to, part, :] = frame[to, part, :] + moved

        add(16 + k, frame[48 + k, part, :], False)
        add(24 + k, frame[56 + k, part, :], False)
        add(32 + k, frame[k, part, :], True)
        add(40 + k, frame[8 + k, part, :], True)

    def unpack_back_sides(index):
        @pl.loop(0, HALF, unroll=8)
        def _(t):
            total = grad[t] + frame[16 + t, CENTRE, :]
            right = recv_r[index, t].astype(F32)
            left = recv_l[index, t].astype(F32)
            edge = jnp.concatenate([right, jnp.zeros((32, LANES), F32), left], axis=0)
            grad[t] = total + edge

    def unpack_backward(index):
        @pl.loop(0, 8, unroll=8)
        def _(k):
            def strip(ref, low, high):
                corners = [
                    recv_c[index, high - 4, k].astype(F32),
                    jnp.zeros((32, LANES), F32),
                    recv_c[index, low - 4, k].astype(F32),
                ]
                return ref[index, k].astype(F32) + jnp.concatenate(corners, axis=0)

            top = strip(recv_b, FAR_BELOW, CORNER_BELOW)
            bottom = strip(recv_a, CORNER_ABOVE, FAR_ABOVE)
            low = is_low(top.shape)
            grad[k] = grad[k] + jnp.where(low, top, 0.0)
            grad[8 + k] = grad[8 + k] + jnp.where(low, swap(top), 0.0)
            grad[16 + k] = grad[16 + k] + jnp.where(low, 0.0, swap(bottom))
            grad[24 + k] = grad[24 + k] + jnp.where(low, 0.0, bottom)

    def weight_terms(layer, bias_rows):
        left = slope_low[16:48].reshape(HALF * BLOCK, 2 * LANES)
        for a, part in enumerate(taps(layer, 0, HALF)):
            lane = a * 3 * LANES
            pair_grad[:, lane : lane + 3 * LANES] = lax.dot_general(
                left, part, (((0,), (0,)), ((), ())), preferred_element_type=F32
            )

        def tap_part(tap, half):
            turned = 3 * (tap % 3) + tap // 3
            first = pair_grad[half * CH : half * CH + CH, tap * LANES : (tap + 1) * LANES]
            at = LANES + half * CH
            second = pair_grad[at : at + CH, turned * LANES : (turned + 1) * LANES]
            return first + second

        for j in range(5):
            low_part = tap_part(2 * j, 0) + swap(tap_part(2 * j, 1))
            if j < 4:
                high_part = tap_part(2 * j + 1, 1) + swap(tap_part(2 * j + 1, 0))
            else:
                total = jnp.sum(bias_rows, axis=0, keepdims=True)
                total = total[:, :LANES] + total[:, LANES:]
                total = total + swap(total)
                high_part = jnp.broadcast_to(total, (LANES, LANES)).T[:CH]
            part = pick(low_part, high_part).astype(BF16)
            for at in range(CH // rows):
                term_ref[layer * (CH // rows) + at, :, j * LANES : (j + 1) * LANES] = part[
                    at * rows : (at + 1) * rows
                ]

    def sum_copy(stage, step):
        if stage == 1:
            other, device = across(step)
            source, target = shards.at[mine], shards.at[mine]
        else:
            other, device = in_plane(step)
            if stage == 0:
                source, target = term_ref.at[other], slots.at[step]
            else:
                source, target = whole.at[inner], whole.at[inner]
        return pltpu.make_async_remote_copy(
            src_ref=source,
            dst_ref=target,
            send_sem=sum_send.at[stage, step],
            recv_sem=sum_recv.at[stage, step],
            device_id=device,
            device_id_type=MESH,
        )

    def peers(stage):
        return range(1, many if stage == 1 else group)

    def of_layer(slab, layer):
        return lax.div(slab, group // LAYERS) == layer

    def sum_start(stage, layer):
        if stage == 0:
            for step in peers(0):

                @pl.when(of_layer(in_plane(step)[0], layer))
                def _():
                    sum_copy(0, step).start()

            return

        @pl.when(of_layer(inner, layer))
        def _():
            if stage == 1:
                total = term_ref[inner].astype(F32)
                for step in peers(0):
                    sum_copy(0, step).wait_recv()
                    total = total + slots[step].astype(F32)
                shards[mine] = total.astype(BF16)
            else:
                for step in peers(1):
                    sum_copy(1, step).wait_recv()
                total = shards[0].astype(F32)
                for at in range(1, many):
                    total = total + shards[at].astype(F32)
                whole[inner] = (total * scale).astype(BF16)
            for step in peers(stage):
                sum_copy(stage, step).start()

    def sum_end():
        for step in peers(2):
            sum_copy(2, step).wait_recv()
        total = jnp.concatenate([whole[at].astype(F32) for at in range(group)], axis=0)
        for layer in range(LAYERS):
            weight_grad_ref[layer] = total[layer * CH : (layer + 1) * CH, :576]
        column = total[:, 4 * LANES :].T[CH : CH + 1]
        bias_grad_ref[0:1, :] = column[:, :CH]
        bias_grad_ref[1:2, :] = swap(column)[:, :CH]
        for stage in range(3):
            for step in peers(stage):
                sum_copy(stage, step).wait_send()

    for layer in reversed(range(LAYERS)):
        index = 2 * LAYERS - 1 - layer
        bias_rows = slope_step(layer)
        if layer == 0:
            weight_terms(layer, bias_rows)
            sum_start(0, 0)
        edge = 64 // BWD // 4
        tile_grad(layer, (*range(edge), *range(3 * edge, 4 * edge)))
        pack_outer(index)
        if layer == 0:
            sum_start(1, 1)
        tile_grad(layer, range(edge, 3 * edge))
        pack_centre(index)
        if layer == 0:
            sum_start(2, 1)
            sum_start(1, 0)
            sum_start(2, 0)
        else:
            weight_terms(layer, bias_rows)
            sum_start(0, 1)

            @pl.loop(0, 16, unroll=4)
            def _(k):
                from_tiles(out_ref, k, last[2 * k], last[2 * k + 1])

        wait(index, (RIGHT, LEFT))
        unpack_back_sides(index)
        wait(index, (ABOVE, BELOW, CORNER_ABOVE, FAR_ABOVE, FAR_BELOW, CORNER_BELOW))
        unpack_backward(index)

    @pl.loop(0, 16, unroll=4)
    def _(k):
        from_tiles(grad_ref, k, kept * grad[2 * k], kept * grad[2 * k + 1])

    sum_end()
    for index in range(2 * LAYERS):
        finish(index)


def finish_kernel(*refs):
    sources, targets, sems = refs[:4], refs[4:8], refs[8]
    copies = []
    for at, (source, target) in enumerate(zip(sources, targets)):
        parts = 4 if at < 2 else 1
        for part in range(parts):
            if parts > 1:
                lanes = source.shape[1] // parts
                span = pl.ds(part * lanes, lanes)
                pair = source.at[:, span], target.at[:, span]
            else:
                pair = source, target
            copies.append(pltpu.make_async_copy(*pair, sems.at[at, part]))
            copies[-1].start()
    for copy in copies:
        copy.wait()


def per_device(input_map, cotangent, band_width, dilation, conv_weight, conv_bias):
    rows_all = lax.axis_size("pos")
    offsets_all = lax.axis_size("band")
    bins = BLOCK * BLOCK
    vmem = pl.BlockSpec(memory_space=pltpu.VMEM)
    smem = pl.BlockSpec(memory_space=pltpu.SMEM)
    hbm = pl.BlockSpec(memory_space=pltpu.HBM)
    group = 16 if rows_all % 16 == 0 else rows_all
    many = rows_all // group * offsets_all
    shard = (LAYERS * CH // group, 5 * LANES)
    scale = 1.0 / (BLOCK * math.sqrt(input_map.shape[0] * rows_all * offsets_all))
    shapes = (
        jax.ShapeDtypeStruct((CH, bins), BF16),
        jax.ShapeDtypeStruct((CH, bins), F32),
        jax.ShapeDtypeStruct((LAYERS, CH, 576), F32),
        jax.ShapeDtypeStruct((LAYERS, CH), F32),
    )
    results = pl.pallas_call(
        functools.partial(net_kernel, rows_all, offsets_all, scale),
        out_shape=shapes,
        in_specs=[smem, smem, hbm, hbm, hbm, hbm],
        out_specs=(vmem, vmem, vmem, vmem),
        scratch_shapes=[
            pltpu.VMEM((CH, bins), BF16),
            pltpu.VMEM((CH, bins), BF16),
            pltpu.VMEM((LAYERS, CH, 576), BF16),
            pltpu.VMEM((LAYERS, CH), F32),
            pltpu.SemaphoreType.DMA((4,)),
            pltpu.VMEM((64, WIDE, LANES), F32),
            pltpu.VMEM((HALF, BLOCK, LANES), F32),
            pltpu.VMEM((group, *shard), BF16),
            pltpu.VMEM((group, *shard), BF16),
            pltpu.VMEM((many, *shard), BF16),
            pltpu.VMEM((group, *shard), BF16),
            pltpu.VMEM((LAYERS, 64, BLOCK, 3 * LANES), BF16),
            pltpu.VMEM((LAYERS, HALF, BLOCK, 2 * LANES), F32),
            pltpu.VMEM((64, BLOCK, 2 * LANES), BF16),
            pltpu.VMEM((SLOTS, 3, BWD, 128, LANES), F32),
            pltpu.VMEM((HALF, BLOCK, LANES), F32),
            pltpu.VMEM((8, WIDE, LANES), F32),
            pltpu.VMEM((8, WIDE, LANES), F32),
            pltpu.VMEM((2 * LANES, 9 * LANES), F32),
            pltpu.VMEM((LAYERS, 9 * LANES, 2 * LANES), BF16),
            pltpu.VMEM((LAYERS, 6 * LANES, 3 * LANES), BF16),
            pltpu.VMEM((512, LANES), F32),
            pltpu.VMEM((4, 8, BLOCK, LANES), BF16),
            pltpu.VMEM((4, 8, BLOCK, LANES), BF16),
            pltpu.VMEM((4, HALF, DMAX, LANES), BF16),
            pltpu.VMEM((4, HALF, DMAX, LANES), BF16),
            pltpu.VMEM((2, 4, 8, DMAX, LANES), BF16),
            pltpu.VMEM((4, 8, BLOCK, LANES), BF16),
            pltpu.VMEM((4, 8, BLOCK, LANES), BF16),
            pltpu.VMEM((4, HALF, DMAX, LANES), BF16),
            pltpu.VMEM((4, HALF, DMAX, LANES), BF16),
            pltpu.VMEM((4, 4, 8, DMAX, LANES), BF16),
            pltpu.SemaphoreType.DMA((4, 8)),
            pltpu.SemaphoreType.DMA((4, 8)),
            pltpu.SemaphoreType.DMA((3, 16)),
            pltpu.SemaphoreType.DMA((3, 16)),
        ],
        compiler_params=pltpu.CompilerParams(
            collective_id=0, has_side_effects=True, vmem_limit_bytes=46 * 2**20
        ),
        name="net",
    )(
        band_width,
        pltpu.with_memory_space_constraint(dilation, pltpu.HBM),
        pltpu.with_memory_space_constraint(input_map.reshape(CH, bins), pltpu.HBM),
        pltpu.with_memory_space_constraint(cotangent.reshape(CH, bins), pltpu.HBM),
        pltpu.with_memory_space_constraint(conv_weight, pltpu.HBM),
        pltpu.with_memory_space_constraint(conv_bias, pltpu.HBM),
    )
    anywhere = pl.BlockSpec(memory_space=pl.ANY)
    output, input_grad, weight_grad, bias_grad = pl.pallas_call(
        finish_kernel,
        out_shape=shapes,
        in_specs=[vmem] * 4,
        out_specs=(anywhere,) * 4,
        scratch_shapes=[pltpu.SemaphoreType.DMA((4, 4))],
        compiler_params=pltpu.CompilerParams(vmem_limit_bytes=4 * 2**20),
        name="finish",
    )(*results)
    return (
        output.reshape(input_map.shape),
        input_grad.reshape(input_map.shape),
        weight_grad,
        bias_grad,
    )


def solution(mesh):
    split = P(None, "pos", "band", None, None)
    return jax.shard_map(
        per_device,
        mesh=mesh,
        in_specs=(split, split, P("pos"), P(), P(), P()),
        out_specs=(split, split, P(), P()),
        check_vma=False,
    )
```

```python
import functools
import math

import jax
import jax.numpy as jnp
from jax import lax
from jax.experimental import pallas as pl
from jax.experimental.pallas import tpu as pltpu
from jax.sharding import PartitionSpec as P

BLOCK = 64
DMAX = 16
LAYERS = 2
BWD = 8
SLOTS = 2
CH = 64
LANES = 128
HALF = 32
WIDE = BLOCK + 2 * DMAX
F32 = jnp.float32
BF16 = jnp.bfloat16
MESH = pl.DeviceIdType.MESH

STEPS = ((1, -1), (0, -1), (0, 1), (-1, 1), (1, 0), (1, -2), (-1, 2), (-1, 0))
ABOVE, RIGHT, LEFT, BELOW, CORNER_ABOVE, FAR_ABOVE, FAR_BELOW, CORNER_BELOW = range(8)
EDGE_LOW = slice(0, DMAX)
CENTRE = slice(DMAX, DMAX + BLOCK)
EDGE_HIGH = slice(DMAX + BLOCK, WIDE)
SQRT_2_PI = math.sqrt(2.0 / math.pi)
CUBIC = 0.044715


def is_low(shape):
    return lax.broadcasted_iota(jnp.int32, shape, len(shape) - 1) < CH


def swap(value):
    return pltpu.roll(value, CH, value.ndim - 1)


def pick(low_value, high_value):
    return jnp.where(is_low(low_value.shape), low_value, high_value)


def merge(first, second):
    return jnp.concatenate([pick(first, swap(second)), pick(swap(first), second)], axis=0)


def both_gelu(value):
    square = value * value
    inner = SQRT_2_PI * (value + CUBIC * (square * value))
    bend = jnp.tanh(inner)
    cdf = 0.5 * (1.0 + bend)
    slope = cdf + 0.5 * value * (1.0 - bend * bend) * (SQRT_2_PI * (1.0 + 3.0 * CUBIC * square))
    return value * cdf, slope


def net_kernel(
    rows_all,
    offsets_all,
    scale,
    width_ref,
    dilation_ref,
    input_hbm,
    cot_hbm,
    weight_hbm,
    bias_hbm,
    out_ref,
    grad_ref,
    weight_grad_ref,
    bias_grad_ref,
    input_ref,
    cot_ref,
    weight_ref,
    bias_ref,
    load_sem,
    frame,
    last,
    term_ref,
    slots,
    shards,
    whole,
    cols,
    slopes,
    slope_low,
    padded,
    grad,
    above,
    below,
    pair_grad,
    w_fwd,
    w_bwd,
    turn,
    send_a,
    send_b,
    send_l,
    send_r,
    send_c,
    recv_a,
    recv_b,
    recv_l,
    recv_r,
    recv_c,
    send_sem,
    recv_sem,
    sum_send,
    sum_recv,
):
    row = lax.axis_index("pos")
    off = lax.axis_index("band")
    loads = [
        pltpu.make_async_copy(source, target, load_sem.at[at])
        for at, (source, target) in enumerate(
            (
                (input_hbm, input_ref),
                (weight_hbm, weight_ref),
                (bias_hbm, bias_ref),
                (cot_hbm, cot_ref),
            )
        )
    ]
    for load in loads:
        load.start()

    def exists(di, do):
        return (row + di >= 0) & (row + di < rows_all) & (off + do >= 0) & (off + do < offsets_all)

    group = whole.shape[0]
    many = shards.shape[0]
    rows = term_ref.shape[1]
    inner = lax.rem(row, group)
    high = lax.div(row, group)
    mine = high * offsets_all + off

    def in_plane(step):
        other = lax.rem(inner + step, group)
        return other, {"pos": high * group + other, "band": off}

    def across(step):
        other = lax.rem(mine + step, many)
        return other, {
            "pos": lax.div(other, offsets_all) * group + inner,
            "band": lax.rem(other, offsets_all),
        }

    kept = jnp.where(
        (off <= width_ref[0]) & (row + off < rows_all), jnp.float32(1.0), jnp.float32(0.0)
    )

    first, final = slice(0, DMAX), slice(BLOCK - DMAX, BLOCK)
    strips = {
        ABOVE: (send_a, recv_a),
        RIGHT: (send_r, recv_r),
        LEFT: (send_l, recv_l),
        BELOW: (send_b, recv_b),
    }
    corners = {
        CORNER_ABOVE: (send_a, final),
        FAR_ABOVE: (send_a, first),
        FAR_BELOW: (send_b, final),
        CORNER_BELOW: (send_b, first),
    }

    def arrival(index, piece):
        if piece in corners:
            return recv_c.at[index, piece - 4]
        return strips[piece][1].at[index]

    def departure(index, piece):
        if piece in strips:
            return strips[piece][0].at[index]
        if index < LAYERS:
            source, part = corners[piece]
            return source.at[index, :, part, :]
        return send_c.at[index - LAYERS, piece - 4]

    for piece in range(8):
        di, do = STEPS[piece]
        for sign, indices in ((1, (0, 1)), (-1, (2, 3))):

            @pl.when(jnp.logical_not(exists(-sign * di, -sign * do)))
            def _():
                for index in indices:
                    there = arrival(index, piece)
                    there[...] = jnp.zeros(there.shape, BF16)

    barrier = pltpu.get_barrier_semaphore()
    count = jnp.int32(0)
    for di, do in STEPS:
        count = count + exists(di, do).astype(jnp.int32)

        @pl.when(exists(di, do))
        def _():
            pl.semaphore_signal(
                barrier,
                inc=1,
                device_id={"pos": row + di, "band": off + do},
                device_id_type=MESH,
            )

    for step in range(1, group):
        pl.semaphore_signal(barrier, inc=1, device_id=in_plane(step)[1], device_id_type=MESH)
    for step in range(1, many):
        pl.semaphore_signal(barrier, inc=1, device_id=across(step)[1], device_id_type=MESH)
    count = count + (group + many - 2)

    def piece_copy(index, piece):
        di, do = STEPS[piece]
        sign = 1 if index < LAYERS else -1
        return pltpu.make_async_remote_copy(
            src_ref=departure(index, piece),
            dst_ref=arrival(index, piece),
            send_sem=send_sem.at[index, piece],
            recv_sem=recv_sem.at[index, piece],
            device_id={"pos": row + sign * di, "band": off + sign * do},
            device_id_type=MESH,
        )

    def send(index, pieces):
        sign = 1 if index < LAYERS else -1
        for piece in pieces:
            di, do = STEPS[piece]

            @pl.when(exists(sign * di, sign * do))
            def _():
                piece_copy(index, piece).start()

    def wait(index, pieces):
        sign = 1 if index < LAYERS else -1
        for piece in pieces:
            di, do = STEPS[piece]

            @pl.when(exists(-sign * di, -sign * do))
            def _():
                piece_copy(index, piece).wait_recv()

    def finish(index):
        sign = 1 if index < LAYERS else -1
        for piece in range(8):
            di, do = STEPS[piece]

            @pl.when(exists(sign * di, sign * do))
            def _():
                piece_copy(index, piece).wait_send()

    def to_tiles(source, k):
        first = source[:, pl.ds(pl.multiple_of(k * LANES, LANES), LANES)].astype(F32)
        second = source[:, pl.ds(pl.multiple_of((k + 16) * LANES, LANES), LANES)].astype(F32)
        return jnp.concatenate([first, second], axis=0).T

    def from_tiles(target, k, first, second):
        turned = jnp.concatenate([first, second], axis=0).T.astype(target.dtype)
        target[:, pl.ds(pl.multiple_of(k * LANES, LANES), LANES)] = turned[:CH]
        target[:, pl.ds(pl.multiple_of((k + 16) * LANES, LANES), LANES)] = turned[CH:]

    def rows_to_cols(load, store):
        @pl.loop(0, 8, unroll=8)
        def _(k):
            turn[pl.ds(pl.multiple_of(k * 64, 64), 64), :] = load(k)

        for t in range(HALF):
            store(t, merge(turn[pl.ds(t, 8, stride=64), :], turn[pl.ds(HALF + t, 8, stride=64), :]))

    def cols_to_rows(load, store):
        @pl.loop(0, HALF, unroll=8)
        def _(t):
            turn[pl.ds(pl.multiple_of(t * 16, 16), 16), :] = load(t)

        for k in range(8):
            store(
                k,
                merge(turn[pl.ds(k, HALF, stride=16), :], turn[pl.ds(8 + k, HALF, stride=16), :]),
            )

    def turn_corner(load, store):
        for k in range(8):
            turn[pl.ds(k * 16, 16), :] = load(k)
        for k in range(8):
            store(k, merge(turn[pl.ds(k, 8, stride=16), :], turn[pl.ds(8 + k, 8, stride=16), :]))

    def pack_forward(index):
        @pl.loop(0, 8, unroll=8)
        def _(k):
            send_a[index, k] = pick(
                swap(frame[32 + k, CENTRE, :]), frame[40 + k, CENTRE, :]
            ).astype(BF16)
            send_b[index, k] = pick(
                frame[16 + k, CENTRE, :], swap(frame[24 + k, CENTRE, :])
            ).astype(BF16)

        @pl.loop(0, HALF, unroll=8)
        def _(t):
            send_l[index, t] = frame[16 + t, slice(64, 80), :].astype(BF16)
            send_r[index, t] = frame[16 + t, slice(16, 32), :].astype(BF16)

    def unpack_sides(index):
        @pl.when(off == 0)
        def _():
            def put_below(k, value):
                recv_b[index, k] = value.astype(BF16)

            cols_to_rows(lambda t: recv_r[index, t].astype(F32), put_below)

        @pl.when(off == 1)
        def _():
            turn_corner(
                lambda k: send_a[index, k, first, :].astype(F32),
                functools.partial(put_down_left, index),
            )

        @pl.when(off > 0)
        def _():
            @pl.loop(0, HALF, unroll=8)
            def _(t):
                frame[16 + t, EDGE_LOW, :] = recv_l[index, t].astype(F32)

        @pl.loop(0, HALF, unroll=8)
        def _(t):
            frame[16 + t, EDGE_HIGH, :] = recv_r[index, t].astype(F32)

    def put_down_left(index, k, value):
        recv_c[index, FAR_BELOW - 4, k] = value.astype(BF16)

    def unpack_forward(index):
        @pl.when(off == 0)
        def _():
            def put_left(t, value):
                frame[16 + t, EDGE_LOW, :] = value

            rows_to_cols(lambda k: recv_a[index, k].astype(F32), put_left)
            turn_corner(
                lambda k: recv_c[index, FAR_ABOVE - 4, k].astype(F32),
                functools.partial(put_down_left, index),
            )

        @pl.loop(0, 8, unroll=8)
        def _(k):
            above, below = (
                jnp.concatenate(
                    [recv_c[index, low - 4, k], strip[index, k], recv_c[index, high - 4, k]], axis=0
                ).astype(F32)
                for low, strip, high in (
                    (CORNER_ABOVE, recv_a, FAR_ABOVE),
                    (FAR_BELOW, recv_b, CORNER_BELOW),
                )
            )
            frame[k] = pick(above, swap(frame[32 + k]))
            frame[8 + k] = swap(pick(frame[40 + k], above))
            frame[48 + k] = swap(pick(below, frame[16 + k]))
            frame[56 + k] = pick(swap(frame[24 + k]), below)

    def prepare_weights(layer):
        weight = weight_ref[layer].astype(F32)
        pieces = [weight[:, j * LANES : (j + 1) * LANES] for j in range(4)]
        pieces.append(
            jnp.concatenate([weight[:, 512:576], jnp.zeros((CH, CH), F32)], axis=1)
        )
        turned = [jnp.concatenate([piece, piece], axis=0).T for piece in pieces]
        for a in range(3):
            for b in range(3):
                for pair, tap in enumerate((3 * a + b, 3 * b + a)):
                    plain = turned[tap // 2][(tap % 2) * CH : (tap % 2) * CH + CH]
                    low = is_low(plain.shape)
                    at = (3 * a + b) * LANES
                    lane = pair * LANES
                    w_fwd[layer, at : at + CH, lane : lane + LANES] = jnp.where(
                        low, plain, 0.0
                    ).astype(BF16)
                    w_fwd[layer, at + CH : at + LANES, lane : lane + LANES] = jnp.where(
                        low, 0.0, plain
                    ).astype(BF16)
                    own = pieces[tap // 2]
                    other = swap(own)
                    if tap % 2:
                        own, other = other, own
                    at = a * 2 * LANES + pair * LANES
                    lane = b * LANES
                    w_bwd[layer, at : at + CH, lane : lane + LANES] = jnp.where(
                        low, own, 0.0
                    ).astype(BF16)
                    w_bwd[layer, at + CH : at + LANES, lane : lane + LANES] = jnp.where(
                        low, 0.0, other
                    ).astype(BF16)

    def shift_columns(layer, tiles, which):
        spread = dilation_ref[layer]

        @pl.loop(*tiles, unroll=4)
        def _(t):
            for b in which:
                cols[layer, t, :, b * LANES : (b + 1) * LANES] = frame[
                    t, pl.ds(DMAX + (b - 1) * spread, BLOCK), :
                ].astype(BF16)

    def taps(layer, t, tiles):
        spread = dilation_ref[layer]
        return [
            cols[layer, pl.ds(DMAX + t + (a - 1) * spread, tiles)].reshape(tiles * BLOCK, 3 * LANES)
            for a in range(3)
        ]

    FWD = 8

    def forward(layer):
        bias = bias_ref[layer : layer + 1, :]
        bias = jnp.concatenate([bias, bias, bias, bias], axis=1)

        @pl.loop(0, HALF // FWD, unroll=4)
        def _(step):
            t = step * FWD
            mixed = (
                jnp.dot(
                    jnp.concatenate(taps(layer, t, FWD), axis=1),
                    w_fwd[layer],
                    preferred_element_type=F32,
                )
                + bias
            )
            value, slope = both_gelu(mixed)
            slopes[layer, pl.ds(t, FWD)] = slope.reshape(FWD, BLOCK, 2 * LANES)
            active = 0.5 * (value[:, :LANES] + value[:, LANES:])
            stored = frame[pl.ds(16 + t, FWD), CENTRE, :].reshape(FWD * BLOCK, LANES)
            result = (kept * (stored + active)).astype(BF16).astype(F32)
            result = result.reshape(FWD, BLOCK, LANES)
            if layer == LAYERS - 1:
                last[pl.ds(t, FWD)] = result
            else:
                frame[pl.ds(16 + t, FWD), CENTRE, :] = result

    loads[0].wait()

    @pl.loop(0, 16, unroll=4)
    def _(k):
        tiles = (to_tiles(input_ref, k) * kept).astype(BF16).astype(F32)
        frame[16 + 2 * k, CENTRE, :] = tiles[:BLOCK]
        frame[17 + 2 * k, CENTRE, :] = tiles[BLOCK:]

    pack_forward(0)
    pl.semaphore_wait(barrier, count)
    send(0, range(8))
    loads[1].wait()
    loads[2].wait()
    for layer in range(LAYERS):
        prepare_weights(layer)
    loads[3].wait()

    @pl.loop(0, 16, unroll=4)
    def _(k):
        tiles = to_tiles(cot_ref, k)
        grad[2 * k] = tiles[:BLOCK]
        grad[2 * k + 1] = tiles[BLOCK:]

    for layer in range(LAYERS):
        wait(layer, (RIGHT, LEFT))
        unpack_sides(layer)
        shift_columns(layer, (16, 48), (1, 2))
        wait(layer, (ABOVE, BELOW, CORNER_ABOVE, FAR_ABOVE, FAR_BELOW, CORNER_BELOW))
        unpack_forward(layer)
        shift_columns(layer, (16, 48), (0,))
        shift_columns(layer, (0, 16), range(3))
        shift_columns(layer, (48, 64), range(3))
        forward(layer)
        if layer < LAYERS - 1:
            pack_forward(layer + 1)
            send(layer + 1, range(8))

    @pl.loop(0, 16, unroll=4)
    def _(t):
        slope_low[t] = jnp.zeros((BLOCK, 2 * LANES), BF16)
        slope_low[48 + t] = jnp.zeros((BLOCK, 2 * LANES), BF16)

    @pl.loop(0, BWD, unroll=4)
    def _(t):
        for b in range(3):
            for slot in range(SLOTS):
                padded[slot, b, t, 0:32, :] = jnp.zeros((32, LANES), F32)
                padded[slot, b, t, 96:128, :] = jnp.zeros((32, LANES), F32)

    def slope_step(layer):
        def step(t, total):
            masked = kept * grad[t]
            grad[t] = masked
            half = 0.5 * masked
            slope = slopes[layer, t] * jnp.concatenate([half, half], axis=1)
            slope_low[16 + t] = slope.astype(BF16)
            return total + jnp.sum(slope.reshape(8, 8, 2 * LANES), axis=0)

        return lax.fori_loop(0, HALF, step, jnp.zeros((8, 2 * LANES), F32), unroll=4)

    def tile_grad(layer, steps):
        spread = dilation_ref[layer]

        def part(step, which, slot):
            first = step * BWD
            held = [
                slope_low[pl.ds(first - (a - 1) * spread, BWD)].reshape(BWD * BLOCK, 2 * LANES)
                for a in which
            ]
            left = held[0] if len(held) == 1 else jnp.concatenate(held, axis=1)
            rows = w_bwd[layer, which[0] * 2 * LANES : (which[-1] + 1) * 2 * LANES, :]
            result = jnp.dot(left, rows, preferred_element_type=F32)
            for b in range(3):
                padded[slot, b, :, 32:96, :] = result[:, b * LANES : (b + 1) * LANES].reshape(
                    BWD, BLOCK, LANES
                )
            for at in range(BWD):
                total = None
                for b in range(3):
                    term = padded[slot, b, at, pl.ds(DMAX - (b - 1) * spread, WIDE), :]
                    total = term if total is None else total + term
                frame[first + at] = total

        for count, step in enumerate(steps):
            at = step * BWD
            which = (0,) if at < 16 else (2,) if at >= 48 else (0, 1, 2)
            part(step, which, count % SLOTS)

    def pack_outer(index):
        @pl.loop(0, 8, unroll=8)
        def _(k):
            above[k] = pick(frame[k], swap(frame[8 + k]))
            below[k] = pick(swap(frame[48 + k]), frame[56 + k])

        @pl.when(off == 0)
        def _():
            def add_far(k, value):
                above[k, EDGE_HIGH, :] = above[k, EDGE_HIGH, :] + value

            turn_corner(lambda k: below[k, EDGE_LOW, :], add_far)

        @pl.loop(0, 8, unroll=8)
        def _(k):
            send_b[index, k] = below[k, CENTRE, :].astype(BF16)
            for piece, strip, part in (
                (CORNER_ABOVE, above, EDGE_LOW),
                (FAR_ABOVE, above, EDGE_HIGH),
                (FAR_BELOW, below, EDGE_LOW),
                (CORNER_BELOW, below, EDGE_HIGH),
            ):
                send_c[index - LAYERS, piece - 4, k] = strip[k, part, :].astype(BF16)

        @pl.when(off > 0)
        def _():
            send_above(index)

        send(index, (BELOW, CORNER_ABOVE, FAR_ABOVE, FAR_BELOW, CORNER_BELOW))

    def send_above(index):
        @pl.loop(0, 8, unroll=8)
        def _(k):
            send_a[index, k] = above[k, CENTRE, :].astype(BF16)

        send(index, (ABOVE,))

    def pack_centre(index):
        @pl.when(off == 0)
        def _():
            @pl.loop(0, 8, unroll=8)
            def _(k):
                share(k, EDGE_LOW)

            def add_above(k, value):
                above[k, CENTRE, :] = above[k, CENTRE, :] + value

            cols_to_rows(lambda t: frame[16 + t, EDGE_LOW, :], add_above)
            send_above(index)

            @pl.loop(0, 8, unroll=8)
            def _(k):
                share(k, slice(DMAX, WIDE))

            def add_right(t, value):
                frame[16 + t, EDGE_HIGH, :] = frame[16 + t, EDGE_HIGH, :] + value

            rows_to_cols(lambda k: below[k, CENTRE, :], add_right)

        @pl.when(off > 0)
        def _():
            @pl.loop(0, 8, unroll=8)
            def _(k):
                share(k, slice(0, WIDE))

        @pl.when(off == 1)
        def _():
            def add_own(k, value):
                low = is_low(value.shape)
                at = slice(16, 32)
                frame[32 + k, at, :] = frame[32 + k, at, :] + jnp.where(low, 0.0, swap(value))
                frame[40 + k, at, :] = frame[40 + k, at, :] + jnp.where(low, 0.0, value)

            turn_corner(lambda k: below[k, EDGE_LOW, :], add_own)

        @pl.loop(0, HALF, unroll=8)
        def _(t):
            send_l[index, t] = frame[16 + t, EDGE_LOW, :].astype(BF16)
            send_r[index, t] = frame[16 + t, EDGE_HIGH, :].astype(BF16)

        send(index, (LEFT, RIGHT))

    def share(k, part):
        def add(to, value, keep_low):
            low = is_low(value.shape)
            moved = swap(value)
            moved = jnp.where(low, moved, 0.0) if keep_low else jnp.where(low, 0.0, moved)
            frame[to, part, :] = frame[to, part, :] + moved

        add(16 + k, frame[48 + k, part, :], False)
        add(24 + k, frame[56 + k, part, :], False)
        add(32 + k, frame[k, part, :], True)
        add(40 + k, frame[8 + k, part, :], True)

    def unpack_back_sides(index):
        @pl.loop(0, HALF, unroll=8)
        def _(t):
            total = grad[t] + frame[16 + t, CENTRE, :]
            right = recv_r[index, t].astype(F32)
            left = recv_l[index, t].astype(F32)
            edge = jnp.concatenate([right, jnp.zeros((32, LANES), F32), left], axis=0)
            grad[t] = total + edge

    def unpack_backward(index):
        @pl.loop(0, 8, unroll=8)
        def _(k):
            def strip(ref, low, high):
                corners = [
                    recv_c[index, high - 4, k].astype(F32),
                    jnp.zeros((32, LANES), F32),
                    recv_c[index, low - 4, k].astype(F32),
                ]
                return ref[index, k].astype(F32) + jnp.concatenate(corners, axis=0)

            top = strip(recv_b, FAR_BELOW, CORNER_BELOW)
            bottom = strip(recv_a, CORNER_ABOVE, FAR_ABOVE)
            low = is_low(top.shape)
            grad[k] = grad[k] + jnp.where(low, top, 0.0)
            grad[8 + k] = grad[8 + k] + jnp.where(low, swap(top), 0.0)
            grad[16 + k] = grad[16 + k] + jnp.where(low, 0.0, swap(bottom))
            grad[24 + k] = grad[24 + k] + jnp.where(low, 0.0, bottom)

    def weight_terms(layer, bias_rows):
        left = slope_low[16:48].reshape(HALF * BLOCK, 2 * LANES)
        for a, part in enumerate(taps(layer, 0, HALF)):
            lane = a * 3 * LANES
            pair_grad[:, lane : lane + 3 * LANES] = lax.dot_general(
                left, part, (((0,), (0,)), ((), ())), preferred_element_type=F32
            )

        def tap_part(tap, half):
            turned = 3 * (tap % 3) + tap // 3
            first = pair_grad[half * CH : half * CH + CH, tap * LANES : (tap + 1) * LANES]
            at = LANES + half * CH
            second = pair_grad[at : at + CH, turned * LANES : (turned + 1) * LANES]
            return first + second

        for j in range(5):
            low_part = tap_part(2 * j, 0) + swap(tap_part(2 * j, 1))
            if j < 4:
                high_part = tap_part(2 * j + 1, 1) + swap(tap_part(2 * j + 1, 0))
            else:
                total = jnp.sum(bias_rows, axis=0, keepdims=True)
                total = total[:, :LANES] + total[:, LANES:]
                total = total + swap(total)
                high_part = jnp.broadcast_to(total, (LANES, LANES)).T[:CH]
            part = pick(low_part, high_part).astype(BF16)
            for at in range(CH // rows):
                term_ref[layer * (CH // rows) + at, :, j * LANES : (j + 1) * LANES] = part[
                    at * rows : (at + 1) * rows
                ]

    def sum_copy(stage, step):
        if stage == 1:
            other, device = across(step)
            source, target = shards.at[mine], shards.at[mine]
        else:
            other, device = in_plane(step)
            if stage == 0:
                source, target = term_ref.at[other], slots.at[step]
            else:
                source, target = whole.at[inner], whole.at[inner]
        return pltpu.make_async_remote_copy(
            src_ref=source,
            dst_ref=target,
            send_sem=sum_send.at[stage, step],
            recv_sem=sum_recv.at[stage, step],
            device_id=device,
            device_id_type=MESH,
        )

    def peers(stage):
        return range(1, many if stage == 1 else group)

    def of_layer(slab, layer):
        return lax.div(slab, group // LAYERS) == layer

    def sum_start(stage, layer):
        if stage == 0:
            for step in far_first(0):

                @pl.when(of_layer(in_plane(step)[0], layer))
                def _():
                    sum_copy(0, step).start()

            return

        @pl.when(of_layer(inner, layer))
        def _():
            if stage == 1:
                total = term_ref[inner].astype(F32)
                for step in peers(0):
                    sum_copy(0, step).wait_recv()
                    total = total + slots[step].astype(F32)
                shards[mine] = total.astype(BF16)
            else:
                for step in peers(1):
                    sum_copy(1, step).wait_recv()
                total = shards[0].astype(F32)
                for at in range(1, many):
                    total = total + shards[at].astype(F32)
                whole[inner] = (total * scale).astype(BF16)
            for step in far_first(stage):
                sum_copy(stage, step).start()

    def far_first(stage):
        def hops(step):
            return min(step % 4, -step % 4) + min(step // 4, -(step // 4) % 4)

        return sorted(peers(stage), key=hops, reverse=True)

    def sum_end():
        for step in peers(2):
            sum_copy(2, step).wait_recv()
        total = jnp.concatenate([whole[at].astype(F32) for at in range(group)], axis=0)
        for layer in range(LAYERS):
            weight_grad_ref[layer] = total[layer * CH : (layer + 1) * CH, :576]
        column = total[:, 4 * LANES :].T[CH : CH + 1]
        bias_grad_ref[0:1, :] = column[:, :CH]
        bias_grad_ref[1:2, :] = swap(column)[:, :CH]
        for stage in range(3):
            for step in peers(stage):
                sum_copy(stage, step).wait_send()

    for layer in reversed(range(LAYERS)):
        index = 2 * LAYERS - 1 - layer
        bias_rows = slope_step(layer)
        if layer == 0:
            weight_terms(layer, bias_rows)
            sum_start(0, 0)
        edge = 64 // BWD // 4
        tile_grad(layer, (*range(edge), *range(3 * edge, 4 * edge)))
        pack_outer(index)
        if layer == 0:
            sum_start(1, 1)
        tile_grad(layer, range(edge, 3 * edge))
        pack_centre(index)
        if layer == 0:
            sum_start(2, 1)
            sum_start(1, 0)
            sum_start(2, 0)
        else:
            weight_terms(layer, bias_rows)
            sum_start(0, 1)

            @pl.loop(0, 16, unroll=4)
            def _(k):
                from_tiles(out_ref, k, last[2 * k], last[2 * k + 1])

        wait(index, (RIGHT, LEFT))
        unpack_back_sides(index)
        wait(index, (ABOVE, BELOW, CORNER_ABOVE, FAR_ABOVE, FAR_BELOW, CORNER_BELOW))
        unpack_backward(index)

    @pl.loop(0, 16, unroll=4)
    def _(k):
        from_tiles(grad_ref, k, kept * grad[2 * k], kept * grad[2 * k + 1])

    sum_end()
    for index in range(2 * LAYERS):
        finish(index)


def finish_kernel(*refs):
    sources, targets, sems = refs[:4], refs[4:8], refs[8]
    copies = []
    for at, (source, target) in enumerate(zip(sources, targets)):
        parts = 4 if at < 2 else 1
        for part in range(parts):
            if parts > 1:
                lanes = source.shape[1] // parts
                span = pl.ds(part * lanes, lanes)
                pair = source.at[:, span], target.at[:, span]
            else:
                pair = source, target
            copies.append(pltpu.make_async_copy(*pair, sems.at[at, part]))
            copies[-1].start()
    for copy in copies:
        copy.wait()


def per_device(input_map, cotangent, band_width, dilation, conv_weight, conv_bias):
    rows_all = lax.axis_size("pos")
    offsets_all = lax.axis_size("band")
    bins = BLOCK * BLOCK
    vmem = pl.BlockSpec(memory_space=pltpu.VMEM)
    smem = pl.BlockSpec(memory_space=pltpu.SMEM)
    hbm = pl.BlockSpec(memory_space=pltpu.HBM)
    group = 16 if rows_all % 16 == 0 else rows_all
    many = rows_all // group * offsets_all
    shard = (LAYERS * CH // group, 5 * LANES)
    scale = 1.0 / (BLOCK * math.sqrt(input_map.shape[0] * rows_all * offsets_all))
    shapes = (
        jax.ShapeDtypeStruct((CH, bins), BF16),
        jax.ShapeDtypeStruct((CH, bins), F32),
        jax.ShapeDtypeStruct((LAYERS, CH, 576), F32),
        jax.ShapeDtypeStruct((LAYERS, CH), F32),
    )
    results = pl.pallas_call(
        functools.partial(net_kernel, rows_all, offsets_all, scale),
        out_shape=shapes,
        in_specs=[smem, smem, hbm, hbm, hbm, hbm],
        out_specs=(vmem, vmem, vmem, vmem),
        scratch_shapes=[
            pltpu.VMEM((CH, bins), BF16),
            pltpu.VMEM((CH, bins), BF16),
            pltpu.VMEM((LAYERS, CH, 576), BF16),
            pltpu.VMEM((LAYERS, CH), F32),
            pltpu.SemaphoreType.DMA((4,)),
            pltpu.VMEM((64, WIDE, LANES), F32),
            pltpu.VMEM((HALF, BLOCK, LANES), F32),
            pltpu.VMEM((group, *shard), BF16),
            pltpu.VMEM((group, *shard), BF16),
            pltpu.VMEM((many, *shard), BF16),
            pltpu.VMEM((group, *shard), BF16),
            pltpu.VMEM((LAYERS, 64, BLOCK, 3 * LANES), BF16),
            pltpu.VMEM((LAYERS, HALF, BLOCK, 2 * LANES), F32),
            pltpu.VMEM((64, BLOCK, 2 * LANES), BF16),
            pltpu.VMEM((SLOTS, 3, BWD, 128, LANES), F32),
            pltpu.VMEM((HALF, BLOCK, LANES), F32),
            pltpu.VMEM((8, WIDE, LANES), F32),
            pltpu.VMEM((8, WIDE, LANES), F32),
            pltpu.VMEM((2 * LANES, 9 * LANES), F32),
            pltpu.VMEM((LAYERS, 9 * LANES, 2 * LANES), BF16),
            pltpu.VMEM((LAYERS, 6 * LANES, 3 * LANES), BF16),
            pltpu.VMEM((512, LANES), F32),
            pltpu.VMEM((4, 8, BLOCK, LANES), BF16),
            pltpu.VMEM((4, 8, BLOCK, LANES), BF16),
            pltpu.VMEM((4, HALF, DMAX, LANES), BF16),
            pltpu.VMEM((4, HALF, DMAX, LANES), BF16),
            pltpu.VMEM((2, 4, 8, DMAX, LANES), BF16),
            pltpu.VMEM((4, 8, BLOCK, LANES), BF16),
            pltpu.VMEM((4, 8, BLOCK, LANES), BF16),
            pltpu.VMEM((4, HALF, DMAX, LANES), BF16),
            pltpu.VMEM((4, HALF, DMAX, LANES), BF16),
            pltpu.VMEM((4, 4, 8, DMAX, LANES), BF16),
            pltpu.SemaphoreType.DMA((4, 8)),
            pltpu.SemaphoreType.DMA((4, 8)),
            pltpu.SemaphoreType.DMA((3, 16)),
            pltpu.SemaphoreType.DMA((3, 16)),
        ],
        compiler_params=pltpu.CompilerParams(
            collective_id=0, has_side_effects=True, vmem_limit_bytes=46 * 2**20
        ),
        name="net",
    )(
        band_width,
        pltpu.with_memory_space_constraint(dilation, pltpu.HBM),
        pltpu.with_memory_space_constraint(input_map.reshape(CH, bins), pltpu.HBM),
        pltpu.with_memory_space_constraint(cotangent.reshape(CH, bins), pltpu.HBM),
        pltpu.with_memory_space_constraint(conv_weight, pltpu.HBM),
        pltpu.with_memory_space_constraint(conv_bias, pltpu.HBM),
    )
    anywhere = pl.BlockSpec(memory_space=pl.ANY)
    output, input_grad, weight_grad, bias_grad = pl.pallas_call(
        finish_kernel,
        out_shape=shapes,
        in_specs=[vmem] * 4,
        out_specs=(anywhere,) * 4,
        scratch_shapes=[pltpu.SemaphoreType.DMA((4, 4))],
        compiler_params=pltpu.CompilerParams(vmem_limit_bytes=4 * 2**20),
        name="finish",
    )(*results)
    return (
        output.reshape(input_map.shape),
        input_grad.reshape(input_map.shape),
        weight_grad,
        bias_grad,
    )


def solution(mesh):
    split = P(None, "pos", "band", None, None)
    return jax.shard_map(
        per_device,
        mesh=mesh,
        in_specs=(split, split, P("pos"), P(), P(), P()),
        out_specs=(split, split, P(), P()),
        check_vma=False,
    )
```

```python
import functools
import math

import jax
import jax.numpy as jnp
from jax import lax
from jax.experimental import pallas as pl
from jax.experimental.pallas import tpu as pltpu
from jax.sharding import PartitionSpec as P

BLOCK = 64
DMAX = 16
LAYERS = 2
BWD = 8
SLOTS = 2
CH = 64
LANES = 128
HALF = 32
WIDE = BLOCK + 2 * DMAX
F32 = jnp.float32
BF16 = jnp.bfloat16
MESH = pl.DeviceIdType.MESH

STEPS = ((1, -1), (0, -1), (0, 1), (-1, 1), (1, 0), (1, -2), (-1, 2), (-1, 0))
ABOVE, RIGHT, LEFT, BELOW, CORNER_ABOVE, FAR_ABOVE, FAR_BELOW, CORNER_BELOW = range(8)
EDGE_LOW = slice(0, DMAX)
CENTRE = slice(DMAX, DMAX + BLOCK)
EDGE_HIGH = slice(DMAX + BLOCK, WIDE)
FARTHEST_FIRST = (
    RIGHT, LEFT, FAR_ABOVE, FAR_BELOW, ABOVE, BELOW, CORNER_ABOVE, CORNER_BELOW
)
SQRT_2_PI = math.sqrt(2.0 / math.pi)
CUBIC = 0.044715


def is_low(shape):
    return lax.broadcasted_iota(jnp.int32, shape, len(shape) - 1) < CH


def swap(value):
    return pltpu.roll(value, CH, value.ndim - 1)


def pick(low_value, high_value):
    return jnp.where(is_low(low_value.shape), low_value, high_value)


def merge(first, second):
    return jnp.concatenate([pick(first, swap(second)), pick(swap(first), second)], axis=0)


def both_gelu(value):
    square = value * value
    inner = SQRT_2_PI * (value + CUBIC * (square * value))
    bend = jnp.tanh(inner)
    cdf = 0.5 * (1.0 + bend)
    slope = cdf + 0.5 * value * (1.0 - bend * bend) * (SQRT_2_PI * (1.0 + 3.0 * CUBIC * square))
    return value * cdf, slope


def net_kernel(
    rows_all,
    offsets_all,
    scale,
    width_ref,
    dilation_ref,
    input_hbm,
    cot_hbm,
    weight_hbm,
    bias_hbm,
    out_ref,
    grad_ref,
    weight_grad_ref,
    bias_grad_ref,
    input_ref,
    cot_ref,
    weight_ref,
    bias_ref,
    load_sem,
    frame,
    last,
    term_ref,
    slots,
    shards,
    whole,
    cols,
    slopes,
    slope_low,
    padded,
    grad,
    above,
    below,
    pair_grad,
    w_fwd,
    w_bwd,
    turn,
    send_a,
    send_b,
    send_l,
    send_r,
    send_c,
    recv_a,
    recv_b,
    recv_l,
    recv_r,
    recv_c,
    send_sem,
    recv_sem,
    sum_send,
    sum_recv,
):
    row = lax.axis_index("pos")
    off = lax.axis_index("band")
    loads = [
        pltpu.make_async_copy(source, target, load_sem.at[at])
        for at, (source, target) in enumerate(
            (
                (input_hbm, input_ref),
                (weight_hbm, weight_ref),
                (bias_hbm, bias_ref),
                (cot_hbm, cot_ref),
            )
        )
    ]
    for load in loads:
        load.start()

    def exists(di, do):
        return (row + di >= 0) & (row + di < rows_all) & (off + do >= 0) & (off + do < offsets_all)

    group = whole.shape[0]
    many = shards.shape[0]
    rows = term_ref.shape[1]
    inner = lax.rem(row, group)
    high = lax.div(row, group)
    mine = high * offsets_all + off

    def in_plane(step):
        other = lax.rem(inner + step, group)
        return other, {"pos": high * group + other, "band": off}

    def across(step):
        other = lax.rem(mine + step, many)
        return other, {
            "pos": lax.div(other, offsets_all) * group + inner,
            "band": lax.rem(other, offsets_all),
        }

    kept = jnp.where(
        (off <= width_ref[0]) & (row + off < rows_all), jnp.float32(1.0), jnp.float32(0.0)
    )

    first, final = slice(0, DMAX), slice(BLOCK - DMAX, BLOCK)
    strips = {
        ABOVE: (send_a, recv_a),
        RIGHT: (send_r, recv_r),
        LEFT: (send_l, recv_l),
        BELOW: (send_b, recv_b),
    }
    corners = {
        CORNER_ABOVE: (send_a, final),
        FAR_ABOVE: (send_a, first),
        FAR_BELOW: (send_b, final),
        CORNER_BELOW: (send_b, first),
    }

    def arrival(index, piece):
        if piece in corners:
            return recv_c.at[index, piece - 4]
        return strips[piece][1].at[index]

    def departure(index, piece):
        if piece in strips:
            return strips[piece][0].at[index]
        if index < LAYERS:
            source, part = corners[piece]
            return source.at[index, :, part, :]
        return send_c.at[index - LAYERS, piece - 4]

    for piece in range(8):
        di, do = STEPS[piece]
        for sign, indices in ((1, (0, 1)), (-1, (2, 3))):

            @pl.when(jnp.logical_not(exists(-sign * di, -sign * do)))
            def _():
                for index in indices:
                    there = arrival(index, piece)
                    there[...] = jnp.zeros(there.shape, BF16)

    barrier = pltpu.get_barrier_semaphore()
    count = jnp.int32(0)
    for di, do in STEPS:
        count = count + exists(di, do).astype(jnp.int32)

        @pl.when(exists(di, do))
        def _():
            pl.semaphore_signal(
                barrier,
                inc=1,
                device_id={"pos": row + di, "band": off + do},
                device_id_type=MESH,
            )

    for step in range(1, group):
        pl.semaphore_signal(barrier, inc=1, device_id=in_plane(step)[1], device_id_type=MESH)
    for step in range(1, many):
        pl.semaphore_signal(barrier, inc=1, device_id=across(step)[1], device_id_type=MESH)
    count = count + (group + many - 2)

    def piece_copy(index, piece):
        di, do = STEPS[piece]
        sign = 1 if index < LAYERS else -1
        return pltpu.make_async_remote_copy(
            src_ref=departure(index, piece),
            dst_ref=arrival(index, piece),
            send_sem=send_sem.at[index, piece],
            recv_sem=recv_sem.at[index, piece],
            device_id={"pos": row + sign * di, "band": off + sign * do},
            device_id_type=MESH,
        )

    def send(index, pieces):
        sign = 1 if index < LAYERS else -1
        for piece in pieces:
            di, do = STEPS[piece]

            @pl.when(exists(sign * di, sign * do))
            def _():
                piece_copy(index, piece).start()

    def wait(index, pieces):
        sign = 1 if index < LAYERS else -1
        for piece in pieces:
            di, do = STEPS[piece]

            @pl.when(exists(-sign * di, -sign * do))
            def _():
                piece_copy(index, piece).wait_recv()

    def finish(index):
        sign = 1 if index < LAYERS else -1
        for piece in range(8):
            di, do = STEPS[piece]

            @pl.when(exists(sign * di, sign * do))
            def _():
                piece_copy(index, piece).wait_send()

    def to_tiles(source, k):
        first = source[:, pl.ds(pl.multiple_of(k * LANES, LANES), LANES)].astype(F32)
        second = source[:, pl.ds(pl.multiple_of((k + 16) * LANES, LANES), LANES)].astype(F32)
        return jnp.concatenate([first, second], axis=0).T

    def from_tiles(target, k, first, second):
        turned = jnp.concatenate([first, second], axis=0).T.astype(target.dtype)
        target[:, pl.ds(pl.multiple_of(k * LANES, LANES), LANES)] = turned[:CH]
        target[:, pl.ds(pl.multiple_of((k + 16) * LANES, LANES), LANES)] = turned[CH:]

    def rows_to_cols(load, store):
        @pl.loop(0, 8, unroll=8)
        def _(k):
            turn[pl.ds(pl.multiple_of(k * 64, 64), 64), :] = load(k)

        for t in range(HALF):
            store(t, merge(turn[pl.ds(t, 8, stride=64), :], turn[pl.ds(HALF + t, 8, stride=64), :]))

    def cols_to_rows(load, store):
        @pl.loop(0, HALF, unroll=8)
        def _(t):
            turn[pl.ds(pl.multiple_of(t * 16, 16), 16), :] = load(t)

        for k in range(8):
            store(
                k,
                merge(turn[pl.ds(k, HALF, stride=16), :], turn[pl.ds(8 + k, HALF, stride=16), :]),
            )

    def turn_corner(load, store):
        for k in range(8):
            turn[pl.ds(k * 16, 16), :] = load(k)
        for k in range(8):
            store(k, merge(turn[pl.ds(k, 8, stride=16), :], turn[pl.ds(8 + k, 8, stride=16), :]))

    def pack_forward(index):
        @pl.loop(0, 8, unroll=8)
        def _(k):
            send_a[index, k] = pick(
                swap(frame[32 + k, CENTRE, :]), frame[40 + k, CENTRE, :]
            ).astype(BF16)
            send_b[index, k] = pick(
                frame[16 + k, CENTRE, :], swap(frame[24 + k, CENTRE, :])
            ).astype(BF16)

        @pl.loop(0, HALF, unroll=8)
        def _(t):
            send_l[index, t] = frame[16 + t, slice(64, 80), :].astype(BF16)
            send_r[index, t] = frame[16 + t, slice(16, 32), :].astype(BF16)

    def unpack_sides(index):
        @pl.when(off == 0)
        def _():
            def put_below(k, value):
                recv_b[index, k] = value.astype(BF16)

            cols_to_rows(lambda t: recv_r[index, t].astype(F32), put_below)

        @pl.when(off == 1)
        def _():
            turn_corner(
                lambda k: send_a[index, k, first, :].astype(F32),
                functools.partial(put_down_left, index),
            )

        @pl.when(off > 0)
        def _():
            @pl.loop(0, HALF, unroll=8)
            def _(t):
                frame[16 + t, EDGE_LOW, :] = recv_l[index, t].astype(F32)

        @pl.loop(0, HALF, unroll=8)
        def _(t):
            frame[16 + t, EDGE_HIGH, :] = recv_r[index, t].astype(F32)

    def put_down_left(index, k, value):
        recv_c[index, FAR_BELOW - 4, k] = value.astype(BF16)

    def unpack_forward(index):
        @pl.when(off == 0)
        def _():
            def put_left(t, value):
                frame[16 + t, EDGE_LOW, :] = value

            rows_to_cols(lambda k: recv_a[index, k].astype(F32), put_left)
            turn_corner(
                lambda k: recv_c[index, FAR_ABOVE - 4, k].astype(F32),
                functools.partial(put_down_left, index),
            )

        @pl.loop(0, 8, unroll=8)
        def _(k):
            above, below = (
                jnp.concatenate(
                    [recv_c[index, low - 4, k], strip[index, k], recv_c[index, high - 4, k]], axis=0
                ).astype(F32)
                for low, strip, high in (
                    (CORNER_ABOVE, recv_a, FAR_ABOVE),
                    (FAR_BELOW, recv_b, CORNER_BELOW),
                )
            )
            frame[k] = pick(above, swap(frame[32 + k]))
            frame[8 + k] = swap(pick(frame[40 + k], above))
            frame[48 + k] = swap(pick(below, frame[16 + k]))
            frame[56 + k] = pick(swap(frame[24 + k]), below)

    def prepare_weights(layer):
        weight = weight_ref[layer].astype(F32)
        pieces = [weight[:, j * LANES : (j + 1) * LANES] for j in range(4)]
        pieces.append(
            jnp.concatenate([weight[:, 512:576], jnp.zeros((CH, CH), F32)], axis=1)
        )
        turned = [jnp.concatenate([piece, piece], axis=0).T for piece in pieces]
        for a in range(3):
            for b in range(3):
                for pair, tap in enumerate((3 * a + b, 3 * b + a)):
                    plain = turned[tap // 2][(tap % 2) * CH : (tap % 2) * CH + CH]
                    low = is_low(plain.shape)
                    at = (3 * a + b) * LANES
                    lane = pair * LANES
                    w_fwd[layer, at : at + CH, lane : lane + LANES] = jnp.where(
                        low, plain, 0.0
                    ).astype(BF16)
                    w_fwd[layer, at + CH : at + LANES, lane : lane + LANES] = jnp.where(
                        low, 0.0, plain
                    ).astype(BF16)
                    own = pieces[tap // 2]
                    other = swap(own)
                    if tap % 2:
                        own, other = other, own
                    at = a * 2 * LANES + pair * LANES
                    lane = b * LANES
                    w_bwd[layer, at : at + CH, lane : lane + LANES] = jnp.where(
                        low, own, 0.0
                    ).astype(BF16)
                    w_bwd[layer, at + CH : at + LANES, lane : lane + LANES] = jnp.where(
                        low, 0.0, other
                    ).astype(BF16)

    def shift_columns(layer, tiles, which):
        spread = dilation_ref[layer]

        @pl.loop(*tiles, unroll=4)
        def _(t):
            for b in which:
                cols[layer, t, :, b * LANES : (b + 1) * LANES] = frame[
                    t, pl.ds(DMAX + (b - 1) * spread, BLOCK), :
                ].astype(BF16)

    def taps(layer, t, tiles):
        spread = dilation_ref[layer]
        return [
            cols[layer, pl.ds(DMAX + t + (a - 1) * spread, tiles)].reshape(tiles * BLOCK, 3 * LANES)
            for a in range(3)
        ]

    FWD = 8

    def forward(layer):
        bias = bias_ref[layer : layer + 1, :]
        bias = jnp.concatenate([bias, bias, bias, bias], axis=1)

        @pl.loop(0, HALF // FWD, unroll=4)
        def _(step):
            t = step * FWD
            mixed = (
                jnp.dot(
                    jnp.concatenate(taps(layer, t, FWD), axis=1),
                    w_fwd[layer],
                    preferred_element_type=F32,
                )
                + bias
            )
            value, slope = both_gelu(mixed)
            slopes[layer, pl.ds(t, FWD)] = slope.reshape(FWD, BLOCK, 2 * LANES)
            active = 0.5 * (value[:, :LANES] + value[:, LANES:])
            stored = frame[pl.ds(16 + t, FWD), CENTRE, :].reshape(FWD * BLOCK, LANES)
            result = (kept * (stored + active)).astype(BF16).astype(F32)
            result = result.reshape(FWD, BLOCK, LANES)
            if layer == LAYERS - 1:
                last[pl.ds(t, FWD)] = result
            else:
                frame[pl.ds(16 + t, FWD), CENTRE, :] = result

    loads[0].wait()

    @pl.loop(0, 16, unroll=4)
    def _(k):
        tiles = (to_tiles(input_ref, k) * kept).astype(BF16).astype(F32)
        frame[16 + 2 * k, CENTRE, :] = tiles[:BLOCK]
        frame[17 + 2 * k, CENTRE, :] = tiles[BLOCK:]

    pack_forward(0)
    pl.semaphore_wait(barrier, count)
    send(0, FARTHEST_FIRST)
    loads[1].wait()
    loads[2].wait()
    for layer in range(LAYERS):
        prepare_weights(layer)
    loads[3].wait()

    @pl.loop(0, 16, unroll=4)
    def _(k):
        tiles = to_tiles(cot_ref, k)
        grad[2 * k] = tiles[:BLOCK]
        grad[2 * k + 1] = tiles[BLOCK:]

    for layer in range(LAYERS):
        wait(layer, (RIGHT, LEFT))
        unpack_sides(layer)
        shift_columns(layer, (16, 48), (1, 2))
        wait(layer, (ABOVE, BELOW, CORNER_ABOVE, FAR_ABOVE, FAR_BELOW, CORNER_BELOW))
        unpack_forward(layer)
        shift_columns(layer, (16, 48), (0,))
        shift_columns(layer, (0, 16), range(3))
        shift_columns(layer, (48, 64), range(3))
        forward(layer)
        if layer < LAYERS - 1:
            pack_forward(layer + 1)
            send(layer + 1, FARTHEST_FIRST)

    @pl.loop(0, 16, unroll=4)
    def _(t):
        slope_low[t] = jnp.zeros((BLOCK, 2 * LANES), BF16)
        slope_low[48 + t] = jnp.zeros((BLOCK, 2 * LANES), BF16)

    @pl.loop(0, BWD, unroll=4)
    def _(t):
        for b in range(3):
            for slot in range(SLOTS):
                padded[slot, b, t, 0:32, :] = jnp.zeros((32, LANES), F32)
                padded[slot, b, t, 96:128, :] = jnp.zeros((32, LANES), F32)

    def slope_step(layer):
        def step(t, total):
            masked = kept * grad[t]
            grad[t] = masked
            half = 0.5 * masked
            slope = slopes[layer, t] * jnp.concatenate([half, half], axis=1)
            slope_low[16 + t] = slope.astype(BF16)
            return total + jnp.sum(slope.reshape(8, 8, 2 * LANES), axis=0)

        return lax.fori_loop(0, HALF, step, jnp.zeros((8, 2 * LANES), F32), unroll=4)

    def tile_grad(layer, steps):
        spread = dilation_ref[layer]

        def part(step, which, slot):
            first = step * BWD
            held = [
                slope_low[pl.ds(first - (a - 1) * spread, BWD)].reshape(BWD * BLOCK, 2 * LANES)
                for a in which
            ]
            left = held[0] if len(held) == 1 else jnp.concatenate(held, axis=1)
            rows = w_bwd[layer, which[0] * 2 * LANES : (which[-1] + 1) * 2 * LANES, :]
            result = jnp.dot(left, rows, preferred_element_type=F32)
            for b in range(3):
                padded[slot, b, :, 32:96, :] = result[:, b * LANES : (b + 1) * LANES].reshape(
                    BWD, BLOCK, LANES
                )
            for at in range(BWD):
                total = None
                for b in range(3):
                    term = padded[slot, b, at, pl.ds(DMAX - (b - 1) * spread, WIDE), :]
                    total = term if total is None else total + term
                frame[first + at] = total

        for count, step in enumerate(steps):
            at = step * BWD
            which = (0,) if at < 16 else (2,) if at >= 48 else (0, 1, 2)
            part(step, which, count % SLOTS)

    def pack_outer(index):
        @pl.loop(0, 8, unroll=8)
        def _(k):
            above[k] = pick(frame[k], swap(frame[8 + k]))
            below[k] = pick(swap(frame[48 + k]), frame[56 + k])

        @pl.when(off == 0)
        def _():
            def add_far(k, value):
                above[k, EDGE_HIGH, :] = above[k, EDGE_HIGH, :] + value

            turn_corner(lambda k: below[k, EDGE_LOW, :], add_far)

        @pl.loop(0, 8, unroll=8)
        def _(k):
            send_b[index, k] = below[k, CENTRE, :].astype(BF16)
            for piece, strip, part in (
                (CORNER_ABOVE, above, EDGE_LOW),
                (FAR_ABOVE, above, EDGE_HIGH),
                (FAR_BELOW, below, EDGE_LOW),
                (CORNER_BELOW, below, EDGE_HIGH),
            ):
                send_c[index - LAYERS, piece - 4, k] = strip[k, part, :].astype(BF16)

        @pl.when(off > 0)
        def _():
            send_above(index)

        send(index, (FAR_ABOVE, FAR_BELOW, BELOW, CORNER_ABOVE, CORNER_BELOW))

    def send_above(index):
        @pl.loop(0, 8, unroll=8)
        def _(k):
            send_a[index, k] = above[k, CENTRE, :].astype(BF16)

        send(index, (ABOVE,))

    def pack_centre(index):
        @pl.when(off == 0)
        def _():
            @pl.loop(0, 8, unroll=8)
            def _(k):
                share(k, EDGE_LOW)

            def add_above(k, value):
                above[k, CENTRE, :] = above[k, CENTRE, :] + value

            cols_to_rows(lambda t: frame[16 + t, EDGE_LOW, :], add_above)
            send_above(index)

            @pl.loop(0, 8, unroll=8)
            def _(k):
                share(k, slice(DMAX, WIDE))

            def add_right(t, value):
                frame[16 + t, EDGE_HIGH, :] = frame[16 + t, EDGE_HIGH, :] + value

            rows_to_cols(lambda k: below[k, CENTRE, :], add_right)

        @pl.when(off > 0)
        def _():
            @pl.loop(0, 8, unroll=8)
            def _(k):
                share(k, slice(0, WIDE))

        @pl.when(off == 1)
        def _():
            def add_own(k, value):
                low = is_low(value.shape)
                at = slice(16, 32)
                frame[32 + k, at, :] = frame[32 + k, at, :] + jnp.where(low, 0.0, swap(value))
                frame[40 + k, at, :] = frame[40 + k, at, :] + jnp.where(low, 0.0, value)

            turn_corner(lambda k: below[k, EDGE_LOW, :], add_own)

        @pl.loop(0, HALF, unroll=8)
        def _(t):
            send_l[index, t] = frame[16 + t, EDGE_LOW, :].astype(BF16)
            send_r[index, t] = frame[16 + t, EDGE_HIGH, :].astype(BF16)

        send(index, (LEFT, RIGHT))

    def share(k, part):
        def add(to, value, keep_low):
            low = is_low(value.shape)
            moved = swap(value)
            moved = jnp.where(low, moved, 0.0) if keep_low else jnp.where(low, 0.0, moved)
            frame[to, part, :] = frame[to, part, :] + moved

        add(16 + k, frame[48 + k, part, :], False)
        add(24 + k, frame[56 + k, part, :], False)
        add(32 + k, frame[k, part, :], True)
        add(40 + k, frame[8 + k, part, :], True)

    def unpack_back_sides(index):
        @pl.loop(0, HALF, unroll=8)
        def _(t):
            total = grad[t] + frame[16 + t, CENTRE, :]
            right = recv_r[index, t].astype(F32)
            left = recv_l[index, t].astype(F32)
            edge = jnp.concatenate([right, jnp.zeros((32, LANES), F32), left], axis=0)
            grad[t] = total + edge

    def unpack_backward(index):
        @pl.loop(0, 8, unroll=8)
        def _(k):
            def strip(ref, low, high):
                corners = [
                    recv_c[index, high - 4, k].astype(F32),
                    jnp.zeros((32, LANES), F32),
                    recv_c[index, low - 4, k].astype(F32),
                ]
                return ref[index, k].astype(F32) + jnp.concatenate(corners, axis=0)

            top = strip(recv_b, FAR_BELOW, CORNER_BELOW)
            bottom = strip(recv_a, CORNER_ABOVE, FAR_ABOVE)
            low = is_low(top.shape)
            grad[k] = grad[k] + jnp.where(low, top, 0.0)
            grad[8 + k] = grad[8 + k] + jnp.where(low, swap(top), 0.0)
            grad[16 + k] = grad[16 + k] + jnp.where(low, 0.0, swap(bottom))
            grad[24 + k] = grad[24 + k] + jnp.where(low, 0.0, bottom)

    def weight_terms(layer, bias_rows):
        left = slope_low[16:48].reshape(HALF * BLOCK, 2 * LANES)
        for a, part in enumerate(taps(layer, 0, HALF)):
            lane = a * 3 * LANES
            pair_grad[:, lane : lane + 3 * LANES] = lax.dot_general(
                left, part, (((0,), (0,)), ((), ())), preferred_element_type=F32
            )

        def tap_part(tap, half):
            turned = 3 * (tap % 3) + tap // 3
            first = pair_grad[half * CH : half * CH + CH, tap * LANES : (tap + 1) * LANES]
            at = LANES + half * CH
            second = pair_grad[at : at + CH, turned * LANES : (turned + 1) * LANES]
            return first + second

        for j in range(5):
            low_part = tap_part(2 * j, 0) + swap(tap_part(2 * j, 1))
            if j < 4:
                high_part = tap_part(2 * j + 1, 1) + swap(tap_part(2 * j + 1, 0))
            else:
                total = jnp.sum(bias_rows, axis=0, keepdims=True)
                total = total[:, :LANES] + total[:, LANES:]
                total = total + swap(total)
                high_part = jnp.broadcast_to(total, (LANES, LANES)).T[:CH]
            part = pick(low_part, high_part).astype(BF16)
            for at in range(CH // rows):
                term_ref[layer * (CH // rows) + at, :, j * LANES : (j + 1) * LANES] = part[
                    at * rows : (at + 1) * rows
                ]

    def sum_copy(stage, step):
        if stage == 1:
            other, device = across(step)
            source, target = shards.at[mine], shards.at[mine]
        else:
            other, device = in_plane(step)
            if stage == 0:
                source, target = term_ref.at[other], slots.at[step]
            else:
                source, target = whole.at[inner], whole.at[inner]
        return pltpu.make_async_remote_copy(
            src_ref=source,
            dst_ref=target,
            send_sem=sum_send.at[stage, step],
            recv_sem=sum_recv.at[stage, step],
            device_id=device,
            device_id_type=MESH,
        )

    def peers(stage):
        return range(1, many if stage == 1 else group)

    def of_layer(slab, layer):
        return lax.div(slab, group // LAYERS) == layer

    def sum_start(stage, layer):
        if stage == 0:
            for step in far_first(0):

                @pl.when(of_layer(in_plane(step)[0], layer))
                def _():
                    sum_copy(0, step).start()

            return

        @pl.when(of_layer(inner, layer))
        def _():
            if stage == 1:
                total = term_ref[inner].astype(F32)
                for step in peers(0):
                    sum_copy(0, step).wait_recv()
                    total = total + slots[step].astype(F32)
                shards[mine] = total.astype(BF16)
            else:
                for step in peers(1):
                    sum_copy(1, step).wait_recv()
                total = shards[0].astype(F32)
                for at in range(1, many):
                    total = total + shards[at].astype(F32)
                whole[inner] = (total * scale).astype(BF16)
            for step in far_first(stage):
                sum_copy(stage, step).start()

    def far_first(stage):
        def hops(step):
            if stage == 1:
                return min(step, many - step)
            return min(step % 4, -step % 4) + min(step // 4, -(step // 4) % 4)

        return sorted(peers(stage), key=hops, reverse=True)

    def sum_end():
        for step in peers(2):
            sum_copy(2, step).wait_recv()
        total = jnp.concatenate([whole[at].astype(F32) for at in range(group)], axis=0)
        for layer in range(LAYERS):
            weight_grad_ref[layer] = total[layer * CH : (layer + 1) * CH, :576]
        column = total[:, 4 * LANES :].T[CH : CH + 1]
        bias_grad_ref[0:1, :] = column[:, :CH]
        bias_grad_ref[1:2, :] = swap(column)[:, :CH]
        for stage in range(3):
            for step in peers(stage):
                sum_copy(stage, step).wait_send()

    for layer in reversed(range(LAYERS)):
        index = 2 * LAYERS - 1 - layer
        bias_rows = slope_step(layer)
        if layer == 0:
            weight_terms(layer, bias_rows)
            sum_start(0, 0)
        edge = 64 // BWD // 4
        tile_grad(layer, (*range(edge), *range(3 * edge, 4 * edge)))
        pack_outer(index)
        if layer == 0:
            sum_start(1, 1)
        tile_grad(layer, range(edge, 3 * edge))
        pack_centre(index)
        if layer == 0:
            sum_start(2, 1)
            sum_start(1, 0)
            sum_start(2, 0)
        else:
            weight_terms(layer, bias_rows)
            sum_start(0, 1)

            @pl.loop(0, 16, unroll=4)
            def _(k):
                from_tiles(out_ref, k, last[2 * k], last[2 * k + 1])

        wait(index, (RIGHT, LEFT))
        unpack_back_sides(index)
        wait(index, (ABOVE, BELOW, CORNER_ABOVE, FAR_ABOVE, FAR_BELOW, CORNER_BELOW))
        unpack_backward(index)

    @pl.loop(0, 16, unroll=4)
    def _(k):
        from_tiles(grad_ref, k, kept * grad[2 * k], kept * grad[2 * k + 1])

    sum_end()
    for index in range(2 * LAYERS):
        finish(index)


def finish_kernel(*refs):
    sources, targets, sems = refs[:4], refs[4:8], refs[8]
    copies = []
    for at, (source, target) in enumerate(zip(sources, targets)):
        parts = 4 if at < 2 else 1
        for part in range(parts):
            if parts > 1:
                lanes = source.shape[1] // parts
                span = pl.ds(part * lanes, lanes)
                pair = source.at[:, span], target.at[:, span]
            else:
                pair = source, target
            copies.append(pltpu.make_async_copy(*pair, sems.at[at, part]))
            copies[-1].start()
    for copy in copies:
        copy.wait()


def per_device(input_map, cotangent, band_width, dilation, conv_weight, conv_bias):
    rows_all = lax.axis_size("pos")
    offsets_all = lax.axis_size("band")
    bins = BLOCK * BLOCK
    vmem = pl.BlockSpec(memory_space=pltpu.VMEM)
    smem = pl.BlockSpec(memory_space=pltpu.SMEM)
    hbm = pl.BlockSpec(memory_space=pltpu.HBM)
    group = 16 if rows_all % 16 == 0 else rows_all
    many = rows_all // group * offsets_all
    shard = (LAYERS * CH // group, 5 * LANES)
    scale = 1.0 / (BLOCK * math.sqrt(input_map.shape[0] * rows_all * offsets_all))
    shapes = (
        jax.ShapeDtypeStruct((CH, bins), BF16),
        jax.ShapeDtypeStruct((CH, bins), F32),
        jax.ShapeDtypeStruct((LAYERS, CH, 576), F32),
        jax.ShapeDtypeStruct((LAYERS, CH), F32),
    )
    results = pl.pallas_call(
        functools.partial(net_kernel, rows_all, offsets_all, scale),
        out_shape=shapes,
        in_specs=[smem, smem, hbm, hbm, hbm, hbm],
        out_specs=(vmem, vmem, vmem, vmem),
        scratch_shapes=[
            pltpu.VMEM((CH, bins), BF16),
            pltpu.VMEM((CH, bins), BF16),
            pltpu.VMEM((LAYERS, CH, 576), BF16),
            pltpu.VMEM((LAYERS, CH), F32),
            pltpu.SemaphoreType.DMA((4,)),
            pltpu.VMEM((64, WIDE, LANES), F32),
            pltpu.VMEM((HALF, BLOCK, LANES), F32),
            pltpu.VMEM((group, *shard), BF16),
            pltpu.VMEM((group, *shard), BF16),
            pltpu.VMEM((many, *shard), BF16),
            pltpu.VMEM((group, *shard), BF16),
            pltpu.VMEM((LAYERS, 64, BLOCK, 3 * LANES), BF16),
            pltpu.VMEM((LAYERS, HALF, BLOCK, 2 * LANES), F32),
            pltpu.VMEM((64, BLOCK, 2 * LANES), BF16),
            pltpu.VMEM((SLOTS, 3, BWD, 128, LANES), F32),
            pltpu.VMEM((HALF, BLOCK, LANES), F32),
            pltpu.VMEM((8, WIDE, LANES), F32),
            pltpu.VMEM((8, WIDE, LANES), F32),
            pltpu.VMEM((2 * LANES, 9 * LANES), F32),
            pltpu.VMEM((LAYERS, 9 * LANES, 2 * LANES), BF16),
            pltpu.VMEM((LAYERS, 6 * LANES, 3 * LANES), BF16),
            pltpu.VMEM((512, LANES), F32),
            pltpu.VMEM((4, 8, BLOCK, LANES), BF16),
            pltpu.VMEM((4, 8, BLOCK, LANES), BF16),
            pltpu.VMEM((4, HALF, DMAX, LANES), BF16),
            pltpu.VMEM((4, HALF, DMAX, LANES), BF16),
            pltpu.VMEM((2, 4, 8, DMAX, LANES), BF16),
            pltpu.VMEM((4, 8, BLOCK, LANES), BF16),
            pltpu.VMEM((4, 8, BLOCK, LANES), BF16),
            pltpu.VMEM((4, HALF, DMAX, LANES), BF16),
            pltpu.VMEM((4, HALF, DMAX, LANES), BF16),
            pltpu.VMEM((4, 4, 8, DMAX, LANES), BF16),
            pltpu.SemaphoreType.DMA((4, 8)),
            pltpu.SemaphoreType.DMA((4, 8)),
            pltpu.SemaphoreType.DMA((3, 16)),
            pltpu.SemaphoreType.DMA((3, 16)),
        ],
        compiler_params=pltpu.CompilerParams(
            collective_id=0, has_side_effects=True, vmem_limit_bytes=46 * 2**20
        ),
        name="net",
    )(
        band_width,
        pltpu.with_memory_space_constraint(dilation, pltpu.HBM),
        pltpu.with_memory_space_constraint(input_map.reshape(CH, bins), pltpu.HBM),
        pltpu.with_memory_space_constraint(cotangent.reshape(CH, bins), pltpu.HBM),
        pltpu.with_memory_space_constraint(conv_weight, pltpu.HBM),
        pltpu.with_memory_space_constraint(conv_bias, pltpu.HBM),
    )
    anywhere = pl.BlockSpec(memory_space=pl.ANY)
    output, input_grad, weight_grad, bias_grad = pl.pallas_call(
        finish_kernel,
        out_shape=shapes,
        in_specs=[vmem] * 4,
        out_specs=(anywhere,) * 4,
        scratch_shapes=[pltpu.SemaphoreType.DMA((4, 4))],
        compiler_params=pltpu.CompilerParams(vmem_limit_bytes=4 * 2**20),
        name="finish",
    )(*results)
    return (
        output.reshape(input_map.shape),
        input_grad.reshape(input_map.shape),
        weight_grad,
        bias_grad,
    )


def solution(mesh):
    split = P(None, "pos", "band", None, None)
    return jax.shard_map(
        per_device,
        mesh=mesh,
        in_specs=(split, split, P("pos"), P(), P(), P()),
        out_specs=(split, split, P(), P()),
        check_vma=False,
    )
```
